32 devices in a mesh: groups: 2 (over x), row: 16 (over z, y, core).
Axes of the slice: x: 2, y: 2, z: 4, core: 2. Of those that a mesh axis runs over, the one named last changes fastest.
Arguments:
- obj_field: float32 [2, 2, 8192, 1024], P(None, None, ('groups', 'row')), parts along dimension 2, may hold values from -4.2 to 4.2
- probe_wave: float32 [4, 256, 256], P('groups'), parts along dimension 0, may hold values from -4.2 to 4.2
- prop_phase: float32 [256, 256], replicated, may hold values from -3.140625 to 3.140625
- win_offsets: int32 [128, 2], P(('groups', 'row')), parts along dimension 0, may hold values from 0 to 3840, as said below
- live_counts: int32 [32], P(('groups', 'row')), parts along dimension 0, may hold values from 0 to 4, as said below
- intensity: float32 [128, 256, 256], P(('groups', 'row')), parts along dimension 0, may hold values from 0.1 to 3
Outputs:
- gradient: float32 [2, 2, 8192, 1024], P(None, None, ('groups', 'row')), parts along dimension 2
The draws below stay inside these ranges and needn't reach their ends.
There are 2 independent parts, one for each index of `groups`. The reference program is written for one: setup_inputs(seed, part) draws one part's arguments, and reference() takes and returns one part's arrays. A program takes and returns all parts, laid end to end along the dimension named above; an argument that names none is the same for every part. Nothing has to cross between parts.
Inputs may be any that keep to these rules, and one draw needn't show every extreme that they name: `win_offsets`: slot j belongs to index j div 4 of row; its window's top row lies in that index's block of rows, (j div 4) * 256 to (j div 4) * 256 + 255, and never past 4096 - 256; its left column is at most 768. The used slots of an index of row are its first live_counts ones; some index has all 4 in use.
All inputs are finite; a program needn't handle non-finite values.
Results may differ from the reference program's by a relative error of at most 0.0003.
Values sent between devices are 32-bit elements; how exact they have to be, the bound alone decides.
No kernel may reach another device: no remote copies, remote signals or barrier semaphores. Data moves between devices by JAX's collectives and lax.ppermute only.
A program may use at most 128 MiB of HBM per device.

```python
import math
import jax
import jax.numpy as jnp
from jax import lax

WIN = 256
SLICES = 2
OW = 1024
CAP = 4
NR = 4096
N_ROW = 16


def draw_win_offsets(key, part):
    key = jax.random.fold_in(key, 11)
    key_row, key_col = jax.random.split(key)
    slots_all = NR // WIN * CAP
    owner_idx = jnp.arange(slots_all, dtype=jnp.int32) // CAP
    within = jax.random.randint(key_row, (slots_all,), 0, WIN, dtype=jnp.int32)
    top_rows = jnp.minimum(owner_idx * WIN + within, NR - WIN)
    left_cols = jax.random.randint(key_col, (slots_all,), 0, OW - WIN + 1, dtype=jnp.int32)
    return jnp.stack([top_rows, left_cols], axis=1).astype(jnp.int32)


def draw_live_counts(key, part):
    key = jax.random.fold_in(key, 23)
    key_low, key_hot = jax.random.split(key)
    devices = NR // WIN
    low_counts = jax.random.randint(key_low, (devices,), 0, CAP // 2 + 1, dtype=jnp.int32)
    group_total = (devices + 3) // 4
    picked = jax.random.randint(key_hot, (group_total,), 0, 3, dtype=jnp.int32)
    device_ids = jnp.arange(devices, dtype=jnp.int32)
    is_hot = device_ids % 4 == picked[device_ids // 4]
    return jnp.where(is_hot, CAP, low_counts).astype(jnp.int32)


def steps_of(own_key, dims, shards, smallest, top_value):
    level, own = 1.0, jax.random.fold_in(own_key, 6)
    for axis_at, shards_of in shards:
        steps = jnp.exp(jax.random.uniform(jax.random.fold_in(own, axis_at), (shards_of,), jnp.float32, smallest / len(shards), top_value / len(shards)))
        level = level * jnp.repeat(steps, dims[axis_at] // shards_of).reshape([-1 if axis == axis_at else 1 for axis in range(len(dims))])
    return level


def normal_values(own_key, dims, scale, reach, shards=(), held_as=jnp.bfloat16):
    array = jax.random.normal(own_key, dims, jnp.float32) * scale
    if len(shards) > 0:
        array = steps_of(own_key, dims, shards, -0.22, 0.18) * array
    return jnp.clip(array, min=-reach, max=reach).astype(held_as)


def setup_inputs(seed: int = 0, part: int = 0) -> dict:
    key_of = jax.random.split(jax.random.key(seed), 7)
    own_keys = jax.random.split(jax.random.fold_in(key_of[6], part), 7)
    return {
        "obj_field": normal_values(own_keys[0], (SLICES, 2, NR, OW), 0.7, 4.2, ((2, 16),), jnp.float32),
        "probe_wave": normal_values(own_keys[1], (2, WIN, WIN), 0.7, 4.2, (), jnp.float32),
        "prop_phase": jnp.clip(jax.random.uniform(key_of[2], (WIN, WIN), jnp.float32, -3.140625, 3.140625), -3.140625, 3.140625),
        "win_offsets": draw_win_offsets(jax.random.fold_in(jax.random.fold_in(key_of[6], part), 71), part),
        "live_counts": draw_live_counts(jax.random.fold_in(jax.random.fold_in(key_of[6], part), 71), part),
        "intensity": jnp.clip(jnp.exp(math.log(3.0) - 3.4011974 * jax.random.uniform(own_keys[5], (N_ROW * CAP, WIN, WIN), jnp.float32) ** steps_of(own_keys[5], (N_ROW * CAP, WIN, WIN), ((0, 16),), -0.2, 0.2)), 0.1, 3.0),
    }


def reference(obj_field, probe_wave, prop_phase, win_offsets, live_counts, intensity):
    objects = obj_field[:, 0] + 1j * obj_field[:, 1]
    probe_in = probe_wave[0] + 1j * probe_wave[1]
    kernel = jnp.cos(prop_phase) + 1j * jnp.sin(prop_phase)
    slots_all = win_offsets.shape[0]
    slot_ids = jnp.arange(slots_all, dtype=jnp.int32)
    live_flag = ((slot_ids % CAP) < live_counts[slot_ids // CAP]).astype(jnp.float32)

    def visit(running, item):
        corner_at, measured, flag_now = item
        zero_idx = jnp.int32(0)
        corner = (zero_idx, corner_at[0].astype(jnp.int32), corner_at[1].astype(jnp.int32))
        tiles_at = lax.dynamic_slice(objects, corner, (SLICES, WIN, WIN))
        entering = [probe_in]
        exit_wave = probe_in * tiles_at[0]
        for layer_at in range(1, SLICES):
            entered = jnp.fft.ifft2(kernel * jnp.fft.fft2(exit_wave, norm="ortho"), norm="ortho")
            entering.append(entered)
            exit_wave = entered * tiles_at[layer_at]
        far_field = jnp.fft.fft2(exit_wave, norm="ortho")
        power_now = far_field.real * far_field.real + far_field.imag * far_field.imag
        back_wave = jnp.fft.ifft2((power_now - measured) * far_field, norm="ortho")
        layer_grads = [None] * SLICES
        for layer_at in range(SLICES - 1, -1, -1):
            layer_grads[layer_at] = jnp.conj(entering[layer_at]) * back_wave
            if layer_at > 0:
                spectrum = jnp.fft.fft2(jnp.conj(tiles_at[layer_at]) * back_wave, norm="ortho")
                back_wave = jnp.fft.ifft2(jnp.conj(kernel) * spectrum, norm="ortho")
        contrib = jnp.stack(layer_grads) * flag_now
        previous = lax.dynamic_slice(running, corner, (SLICES, WIN, WIN))
        return lax.dynamic_update_slice(running, previous + contrib, corner), None

    start_acc = jnp.zeros((SLICES, NR, OW), objects.dtype)
    final_acc, _ = lax.scan(visit, start_acc, (win_offsets, intensity, live_flag))
    return jnp.stack([final_acc.real, final_acc.imag], axis=1).astype(jnp.float32)
```

```python
import functools

import jax
import jax.numpy as jnp
import numpy as np
from jax import lax
from jax.experimental import pallas as pl
from jax.experimental.pallas import tpu as pltpu
from jax.sharding import PartitionSpec as P

WIN = 256
HALF = WIN // 2
LANES = 128
SUB = 8
CAP = 4
GROUPS = WIN // SUB
INT_GROUPS = GROUPS // 4
CAP_FWD = 48
CAP_BACK_A = 48
CAP_BACK_B = 32
DEAD, AT_A, AT_B = 0, 1, 2
FIELDS = 8
f32 = jnp.float32
bf16 = jnp.bfloat16
VM = pltpu.MemorySpace.VMEM
SM = pltpu.MemorySpace.SMEM


def real_tables():
    k = np.arange(HALF)[:, None]
    n = np.arange(HALF)[None, :]
    out = []
    for odd in (0, 1):
        angle = 2.0 * np.pi * (((2 * k + odd) * n) % WIN) / WIN
        c, s = np.cos(angle) / 16.0, np.sin(angle) / 16.0
        out.append(np.block([[c, s], [-s, c]]))
    return out


def high_low(table):
    high = table.astype(np.float32).astype(bf16)
    low = (table - high.astype(np.float64)).astype(np.float32).astype(bf16)
    return high, low


def left_table(table):
    high, low = high_low(table)
    return np.concatenate([high, low, high], axis=1)


def right_table(table):
    high, low = high_low(table)
    return np.concatenate([high, high, low], axis=0)


def make_tables():
    even, odd = real_tables()
    left = np.stack([left_table(m) for m in (even, odd, even.T, odd.T)])
    right = np.stack([right_table(m) for m in (even.T, odd.T, even, odd)])
    order = np.concatenate([np.arange(0, WIN, 2), np.arange(1, WIN, 2)])
    shuffle = np.zeros((WIN, WIN), np.float32)
    shuffle[order, np.arange(WIN)] = 1.0
    return left, right, np.concatenate([shuffle, shuffle], axis=0).astype(bf16)


def split(x):
    high = x.astype(bf16)
    return high, (x - high.astype(f32)).astype(bf16)


def left_mul(table, x):
    high, low = split(x)
    return jnp.dot(table, jnp.concatenate([high, high, low], axis=0), preferred_element_type=f32)


def right_mul(x, table):
    high, low = split(x)
    return jnp.dot(jnp.concatenate([high, low, high], axis=1), table, preferred_element_type=f32)


def rows_forward(re, im, left, cols):
    def halves(x):
        return x[:HALF], x[HALF:]

    tr, br = halves(re)
    ti, bi = halves(im)
    e = left_mul(left[0], jnp.concatenate([tr + br, ti + bi], axis=0))
    o = left_mul(left[1], jnp.concatenate([tr - br, ti - bi], axis=0))
    return e, o


def rows_inverse(xr, xi, left):
    u = left_mul(left[2], jnp.concatenate([xr[:HALF], xi[:HALF]], axis=0))
    v = left_mul(left[3], jnp.concatenate([xr[HALF:], xi[HALF:]], axis=0))
    return u, v


def lanes_forward(re, im, right):
    lr, rr = re[:, :HALF], re[:, HALF:]
    li, ri = im[:, :HALF], im[:, HALF:]
    e = right_mul(jnp.concatenate([lr + rr, li + ri], axis=1), right[0])
    o = right_mul(jnp.concatenate([lr - rr, li - ri], axis=1), right[1])
    return (
        jnp.concatenate([e[:, :HALF], o[:, :HALF]], axis=1),
        jnp.concatenate([e[:, HALF:], o[:, HALF:]], axis=1),
    )


def lanes_inverse(re, im, right):
    u = right_mul(jnp.concatenate([re[:, :HALF], im[:, :HALF]], axis=1), right[2])
    v = right_mul(jnp.concatenate([re[:, HALF:], im[:, HALF:]], axis=1), right[3])
    return (
        jnp.concatenate([u[:, :HALF] + v[:, :HALF], u[:, :HALF] - v[:, :HALF]], axis=1),
        jnp.concatenate([u[:, HALF:] + v[:, HALF:], u[:, HALF:] - v[:, HALF:]], axis=1),
    )


def cmul(ar, ai, br, bi):
    return ar * br - ai * bi, ar * bi + ai * br


def cmul_conj(ar, ai, br, bi):
    return ar * br + ai * bi, ar * bi - ai * br


def decide_kernel(offsets, live, table):
    count = live[0]
    rows = [jnp.bitwise_and(offsets[j, 0], WIN - 1) for j in range(CAP)]
    used = [(j < count).astype(jnp.int32) for j in range(CAP)]
    on_a = [used[j] * ((rows[j] + SUB - 1) // SUB) for j in range(CAP)]
    on_b = [used[j] * (GROUPS - rows[j] // SUB + INT_GROUPS) for j in range(CAP)]
    best, chosen = jnp.int32(10000), jnp.int32(0)
    for mask in range(1 << CAP):
        total_a = jnp.int32(0)
        total_b = jnp.int32(0)
        for j in range(CAP):
            if mask >> j & 1:
                total_b = total_b + on_b[j]
            else:
                total_a = total_a + on_a[j]
        cost = jnp.maximum(total_a, total_b)
        better = cost < best
        best = jnp.where(better, cost, best)
        chosen = jnp.where(better, mask, chosen)
    at_a = jnp.int32(0)
    at_b = jnp.int32(0)
    back = jnp.int32(0)
    for j in range(CAP):
        to_b = jnp.bitwise_and(chosen >> j, 1) * used[j]
        to_b = jnp.where(rows[j] == 0, 0, to_b)
        to_a = used[j] - to_b
        table[FIELDS * j] = to_a * AT_A + to_b * AT_B
        table[FIELDS * j + 1] = rows[j]
        table[FIELDS * j + 2] = offsets[j, 1]
        table[FIELDS * j + 3] = jnp.where(to_b == 1, at_b, at_a)
        table[FIELDS * j + 4] = jnp.where(to_b == 1, back, at_a)
        at_a = at_a + to_a * on_a[j]
        at_b = at_b + to_b * on_b[j]
        back = back + to_b * (on_b[j] - INT_GROUPS)
        table[FIELDS * j + 5] = 0
        table[FIELDS * j + 6] = 0
        table[FIELDS * j + 7] = 0


def slot_of(table, j):
    base = FIELDS * j
    return table[base], table[base + 1], table[base + 2], table[base + 3], table[base + 4]


def lane_blocks(col):
    first = col // LANES
    starts = [jnp.minimum(first + k, 7) * LANES for k in range(3)]
    return [pl.multiple_of(start, LANES) for start in starts], jnp.bitwise_and(col, LANES - 1)


def lane_iota():
    return lax.broadcasted_iota(jnp.int32, (SUB, LANES), 1)


def load_group(field, plane, group, starts, shift):
    rows = pl.ds(pl.multiple_of(group * SUB, SUB), SUB)
    first = field[plane, rows, pl.ds(starts[0], LANES)]
    second = field[plane, rows, pl.ds(starts[1], LANES)]
    third = field[plane, rows, pl.ds(starts[2], LANES)]
    return jnp.where(lane_iota() >= shift, first, third), second


def add_group(total, plane, group, starts, shift, left, right):
    rows = pl.ds(pl.multiple_of(group * SUB, SUB), SUB)
    inside = lane_iota() >= shift
    total[plane, rows, pl.ds(starts[0], LANES)] += jnp.where(inside, left, 0.0)
    total[plane, rows, pl.ds(starts[1], LANES)] += right
    total[plane, rows, pl.ds(starts[2], LANES)] += jnp.where(inside, 0.0, left)


def pack_to_b_kernel(table, field, intensity, out):
    for j in range(CAP):
        state, row, col, start, _ = slot_of(table, j)

        @pl.when(state == AT_B)
        def _():
            starts, shift = lane_blocks(col)
            first = row // SUB

            def body(group, carry):
                at = start + group - first
                for plane in range(4):
                    left, right = load_group(field, plane, group, starts, shift)
                    out[at, plane, :, :LANES] = left
                    out[at, plane, :, LANES:] = right
                return carry

            lax.fori_loop(first, GROUPS, body, 0)
            after = start + GROUPS - first

            def body_int(group, carry):
                for plane in range(4):
                    rows = pl.ds(pl.multiple_of((group * 4 + plane) * SUB, SUB), SUB)
                    out[after + group, plane] = intensity[j, rows, :]
                return carry

            lax.fori_loop(0, INT_GROUPS, body_int, 0)


def pack_to_a_kernel(table, field, out):
    for j in range(CAP):
        state, row, col, start, _ = slot_of(table, j)

        @pl.when(state == AT_A)
        def _():
            starts, shift = lane_blocks(col)

            def body(group, carry):
                for plane in range(4):
                    left, right = load_group(field, plane, group, starts, shift)
                    out[start + group, plane, :, :LANES] = left
                    out[start + group, plane, :, LANES:] = right
                return carry

            lax.fori_loop(0, (row + SUB - 1) // SUB, body, 0)


def slots_kernel(
    first_kind,
    role,
    table,
    field,
    intensity,
    probe,
    kernel,
    left,
    right,
    shuffle,
    from_b,
    from_a,
    total_in,
    total,
    back_a,
    back_b,
    got,
    tile,
    measured,
    twice,
    beam,
    work,
    entered,
    sem,
):
    is_a = role[0] == 0
    mine = jnp.where(is_a, AT_A, AT_B)

    def fetch(source):
        copy = pltpu.make_async_copy(source, got, sem)
        copy.start()
        copy.wait()

    @pl.when(is_a)
    def _():
        fetch(from_b)

    @pl.when(jnp.logical_not(is_a))
    def _():
        fetch(from_a)

    if first_kind:
        total[...] = jnp.zeros_like(total)
    else:
        copy = pltpu.make_async_copy(total_in, total, sem)
        copy.start()
        copy.wait()
    for plane in range(2):
        for part in range(2):
            cut = probe[plane, :, part * LANES : (part + 1) * LANES]
            twice[2 * plane + part, :WIN] = cut
            twice[2 * plane + part, WIN:] = cut

    def slot_body(j, carry):
        state, row, col, start, back = slot_of(table, j)

        @pl.when(state == mine)
        def _():
            starts, shift = lane_blocks(col)
            low = row // SUB
            base = jnp.where(is_a, start, start - low)
            sublane = lax.broadcasted_iota(jnp.int32, (SUB, LANES), 0)

            def own_rows(group):
                below = (group * SUB + sublane < row).astype(jnp.int32)
                return below == jnp.where(is_a, 0, 1)

            def gather(group, carry):
                own = own_rows(group)
                at = jnp.clip(base + group, 0, CAP_FWD - 1)
                rows = pl.ds(pl.multiple_of(group * SUB, SUB), SUB)
                for plane in range(4):
                    lf, rt = load_group(field, plane, group, starts, shift)
                    tile[plane, rows, :LANES] = jnp.where(own, lf, got[at, plane, :, :LANES])
                    tile[plane, rows, LANES:] = jnp.where(own, rt, got[at, plane, :, LANES:])
                return carry

            lax.fori_loop(0, GROUPS, gather, 0)

            @pl.when(is_a)
            def _():
                measured[0] = intensity[j, :, :LANES]
                measured[1] = intensity[j, :, LANES:]

            @pl.when(jnp.logical_not(is_a))
            def _():
                after = start + GROUPS - low

                def unpack(group, carry):
                    for plane in range(4):
                        rows = pl.ds(pl.multiple_of((group * 4 + plane) * SUB, SUB), SUB)
                        measured[0, rows, :] = got[after + group, plane, :, :LANES]
                        measured[1, rows, :] = got[after + group, plane, :, LANES:]
                    return carry

                lax.fori_loop(0, INT_GROUPS, unpack, 0)

            for plane in range(2):
                parts = [twice[2 * plane + part, pl.ds(WIN - row, WIN), :] for part in range(2)]
                beam[plane] = pltpu.roll(jnp.concatenate(parts, axis=1), shift, 1)

            def store_rows(e, o):
                work[0, :HALF], work[1, :HALF] = e[:HALF], e[HALF:]
                work[0, HALF:], work[1, HALF:] = o[:HALF], o[HALF:]

            def middle(pointwise):
                for half in range(2):
                    rows = pl.ds(half * HALF, HALF)
                    re, im = lanes_forward(work[0, rows, :], work[1, rows, :], right)
                    re, im = pointwise(half, rows, re, im)
                    re, im = lanes_inverse(re, im, right)
                    work[0, rows, :], work[1, rows, :] = re, im

            def unstack(u, v):
                return (
                    jnp.concatenate([u[:HALF] + v[:HALF], u[:HALF] - v[:HALF]], axis=0),
                    jnp.concatenate([u[HALF:] + v[HALF:], u[HALF:] - v[HALF:]], axis=0),
                )

            def propagate(half, rows, re, im):
                return cmul(kernel[0, rows, :], kernel[1, rows, :], re, im)

            def propagate_back(half, rows, re, im):
                return cmul_conj(kernel[0, rows, :], kernel[1, rows, :], re, im)

            def residual(half, rows, re, im):
                every = pl.ds(half, HALF, stride=2)
                rows_of = jnp.concatenate([measured[0, every, :], measured[1, every, :]], axis=1)
                high, low_part = split(rows_of)
                wanted = jnp.dot(
                    jnp.concatenate([high, low_part], axis=1), shuffle[...], preferred_element_type=f32
                )
                scale = re * re + im * im - wanted
                return scale * re, scale * im

            re, im = cmul(beam[0], beam[1], tile[0], tile[1])
            store_rows(*rows_forward(re, im, left, None))
            middle(propagate)
            re, im = unstack(*rows_inverse(work[0], work[1], left))
            entered[0], entered[1] = re, im
            re, im = cmul(re, im, tile[2], tile[3])
            store_rows(*rows_forward(re, im, left, None))
            middle(residual)
            br, bi = unstack(*rows_inverse(work[0], work[1], left))
            re, im = cmul_conj(tile[2], tile[3], br, bi)
            tile[2], tile[3] = cmul_conj(entered[0], entered[1], br, bi)
            store_rows(*rows_forward(re, im, left, None))
            middle(propagate_back)
            br, bi = unstack(*rows_inverse(work[0], work[1], left))
            tile[0], tile[1] = cmul_conj(beam[0], beam[1], br, bi)

            def scatter(group, carry):
                own = own_rows(group)
                rows = pl.ds(pl.multiple_of(group * SUB, SUB), SUB)
                for plane in range(4):
                    lf = jnp.where(own, tile[plane, rows, :LANES], 0.0)
                    rt = jnp.where(own, tile[plane, rows, LANES:], 0.0)
                    add_group(total, plane, group, starts, shift, lf, rt)
                return carry

            lax.fori_loop(jnp.where(is_a, low, 0), jnp.where(is_a, GROUPS, (row + SUB - 1) // SUB), scatter, 0)

            def send(out, offset):
                def body(group, carry):
                    rows = pl.ds(pl.multiple_of(group * SUB, SUB), SUB)
                    for plane in range(4):
                        out[offset + group, plane] = tile[plane, rows, :]
                    return carry

                return body

            @pl.when(is_a)
            def _():
                lax.fori_loop(0, (row + SUB - 1) // SUB, send(back_a, back), 0)

            @pl.when(jnp.logical_not(is_a))
            def _():
                lax.fori_loop(low, GROUPS, send(back_b, back - low), 0)

        return carry

    lax.fori_loop(0, CAP, slot_body, 0)


def finish_kernel(
    role_in, table_in, role_out, table_out, total_in, in_a, in_b, out_a, out_b, total, got_in, got_out, sem
):
    def start_copies(role, from_a, from_b, got, at):
        @pl.when(role[0] == 0)
        def _():
            pltpu.make_async_copy(from_b, got.at[pl.ds(0, CAP_BACK_B)], sem.at[at]).start()
            pltpu.make_async_copy(from_b, got.at[pl.ds(0, CAP_BACK_B)], sem.at[at]).wait()

        @pl.when(role[0] == 1)
        def _():
            pltpu.make_async_copy(from_a, got, sem.at[at]).start()
            pltpu.make_async_copy(from_a, got, sem.at[at]).wait()

    start_copies(role_in, in_a, in_b, got_in, 0)
    start_copies(role_out, out_a, out_b, got_out, 1)
    total[...] = total_in[...]
    for role, table, got in ((role_in, table_in, got_in), (role_out, table_out, got_out)):
        is_a = role[0] == 0
        theirs = jnp.where(is_a, AT_B, AT_A)
        for j in range(CAP):
            state, row, col, _, back = slot_of(table, j)

            @pl.when(state == theirs)
            def _():
                starts, shift = lane_blocks(col)
                low = row // SUB
                base = jnp.where(is_a, back - low, back)
                sublane = lax.broadcasted_iota(jnp.int32, (SUB, LANES), 0)

                def body(group, carry):
                    below = (group * SUB + sublane < row).astype(jnp.int32)
                    own = below == jnp.where(is_a, 0, 1)
                    for plane in range(4):
                        lf = jnp.where(own, got[base + group, plane, :, :LANES], 0.0)
                        rt = jnp.where(own, got[base + group, plane, :, LANES:], 0.0)
                        add_group(total, plane, group, starts, shift, lf, rt)
                    return carry

                lax.fori_loop(
                    jnp.where(is_a, low, 0), jnp.where(is_a, GROUPS, (row + SUB - 1) // SUB), body, 0
                )


def spec(space):
    return pl.BlockSpec(memory_space=space)


PARAMS = pltpu.CompilerParams(vmem_limit_bytes=48 << 20)


def packed(groups):
    return jax.ShapeDtypeStruct((groups, 4, SUB, WIN), f32)


def run_slots(first_kind, role, table, field, intensity, probe, kernel, tables, from_b, from_a, total):
    left, right, shuffle = tables
    specs = [spec(SM)] * 2 + [spec(VM)] * 7 + [spec(pl.ANY)] * 3
    return pl.pallas_call(
        functools.partial(slots_kernel, first_kind),
        out_shape=(
            jax.ShapeDtypeStruct(field.shape, f32),
            packed(CAP_BACK_A),
            packed(CAP_BACK_B),
        ),
        in_specs=specs,
        out_specs=(spec(VM),) * 3,
        scratch_shapes=[
            pltpu.VMEM((CAP_FWD, 4, SUB, WIN), f32),
            pltpu.VMEM((4, WIN, WIN), f32),
            pltpu.VMEM((2, WIN, LANES), f32),
            pltpu.VMEM((4, 2 * WIN, LANES), f32),
            pltpu.VMEM((2, WIN, WIN), f32),
            pltpu.VMEM((2, WIN, WIN), f32),
            pltpu.VMEM((2, WIN, WIN), f32),
            pltpu.SemaphoreType.DMA,
        ],
        compiler_params=PARAMS,
    )(role, table, field, intensity, probe, kernel, left, right, shuffle, from_b, from_a, total)


def shards(obj_field, probe_wave, prop_phase, win_offsets, live_counts, intensity):
    field = obj_field.reshape((4,) + obj_field.shape[2:])
    count = lax.axis_size("row")
    within = [(i, i + 1) for i in range(0, count - 1, 2)]
    across = [(i, i + 1) for i in range(1, count - 1, 2)]
    back = lambda pairs: [(b, a) for a, b in pairs]
    move = lambda x, pairs: lax.ppermute(x, "row", pairs)
    odd = jnp.bitwise_and(lax.axis_index("row"), 1)
    role_in = odd.reshape(1)
    role_out = (1 - odd).reshape(1)

    own = pl.pallas_call(
        decide_kernel,
        out_shape=jax.ShapeDtypeStruct((CAP * FIELDS,), jnp.int32),
        in_specs=[spec(SM)] * 2,
        out_specs=spec(SM),
    )(win_offsets, live_counts)
    before = move(own, within + across)
    to_b = pl.pallas_call(
        pack_to_b_kernel,
        out_shape=packed(CAP_FWD),
        in_specs=[spec(SM), spec(VM), spec(VM)],
        out_specs=spec(VM),
        compiler_params=PARAMS,
    )(own, field, intensity)
    in_from_a = move(to_b, within)
    out_from_a = move(to_b, across)
    to_a = pl.pallas_call(
        pack_to_a_kernel,
        out_shape=packed(CAP_FWD),
        in_specs=[spec(SM), spec(VM)],
        out_specs=spec(VM),
        compiler_params=PARAMS,
    )(before, field)
    in_from_b = move(to_a, back(within))
    out_from_b = move(to_a, back(across))
    table_in = jnp.where(odd == 0, own, before)
    table_out = jnp.where(odd == 0, before, own)

    phase = prop_phase.reshape(HALF, 2, HALF, 2).transpose(1, 0, 3, 2).reshape(WIN, WIN)
    kernel = jnp.stack([jnp.cos(phase), jnp.sin(phase)])
    tables = tuple(jnp.asarray(t) for t in make_tables())

    args = (field, intensity, probe_wave, kernel, tables)
    total, in_back_a, in_back_b = run_slots(True, role_in, table_in, *args, in_from_b, in_from_a, field)
    in_a = move(in_back_a, within)
    in_b = move(in_back_b, back(within))
    total, out_back_a, out_back_b = run_slots(False, role_out, table_out, *args, out_from_b, out_from_a, total)
    out_a = move(out_back_a, across)
    out_b = move(out_back_b, back(across))
    grad = pl.pallas_call(
        finish_kernel,
        out_shape=jax.ShapeDtypeStruct(field.shape, f32),
        in_specs=[spec(SM)] * 4 + [spec(VM)] + [spec(pl.ANY)] * 4,
        out_specs=spec(VM),
        scratch_shapes=[
            pltpu.VMEM((CAP_BACK_A, 4, SUB, WIN), f32),
            pltpu.VMEM((CAP_BACK_A, 4, SUB, WIN), f32),
            pltpu.SemaphoreType.DMA((2,)),
        ],
        input_output_aliases={4: 0},
        compiler_params=PARAMS,
    )(role_in, table_in, role_out, table_out, total, in_a, in_b, out_a, out_b)
    return grad.reshape(obj_field.shape)


def solution(mesh):
    in_specs = (
        P(None, None, ("groups", "row"), None),
        P("groups", None, None),
        P(),
        P(("groups", "row"), None),
        P(("groups", "row")),
        P(("groups", "row"), None, None),
    )
    out_specs = P(None, None, ("groups", "row"), None)
    return jax.shard_map(shards, mesh=mesh, in_specs=in_specs, out_specs=out_specs, check_vma=False)
```

```python
import functools

import jax
import jax.numpy as jnp
import numpy as np
from jax import lax
from jax.experimental import pallas as pl
from jax.experimental.pallas import tpu as pltpu
from jax.sharding import PartitionSpec as P

WIN = 256
HALF = WIN // 2
LANES = 128
SUB = 8
CAP = 4
GROUPS = WIN // SUB
INT_GROUPS = GROUPS // 4
CAP_FWD = 48
CAP_BACK_A = 48
CAP_BACK_B = 32
DEAD, AT_A, AT_B = 0, 1, 2
FIELDS = 8
f32 = jnp.float32
bf16 = jnp.bfloat16
VM = pltpu.MemorySpace.VMEM
SM = pltpu.MemorySpace.SMEM


def real_tables():
    k = np.arange(HALF)[:, None]
    n = np.arange(HALF)[None, :]
    out = []
    for odd in (0, 1):
        angle = 2.0 * np.pi * (((2 * k + odd) * n) % WIN) / WIN
        c, s = np.cos(angle) / 16.0, np.sin(angle) / 16.0
        out.append(np.block([[c, s], [-s, c]]))
    return out


def high_low(table):
    high = table.astype(np.float32).astype(bf16)
    low = (table - high.astype(np.float64)).astype(np.float32).astype(bf16)
    return high, low


def make_tables():
    even, odd = real_tables()
    forms = np.stack([np.stack(high_low(m)) for m in (even, odd, even.T, odd.T)])
    order = np.concatenate([np.arange(0, WIN, 2), np.arange(1, WIN, 2)])
    shuffle = np.zeros((WIN, WIN), np.float32)
    shuffle[order, np.arange(WIN)] = 1.0
    return forms, shuffle.astype(bf16)


EVEN, ODD, EVEN_T, ODD_T = range(4)


def split(x):
    high = x.astype(bf16)
    return high, (x - high.astype(f32)).astype(bf16)


def left_mul(forms, which, x):
    high, low = split(x)
    t_high, t_low = forms[which, 0], forms[which, 1]
    wide = jnp.concatenate([t_high, t_low, t_high], axis=1)
    return jnp.dot(wide, jnp.concatenate([high, high, low], axis=0), preferred_element_type=f32)


def right_mul(x, forms, which):
    high, low = split(x)
    t_high, t_low = forms[which, 0], forms[which, 1]
    tall = jnp.concatenate([t_high, t_high, t_low], axis=0)
    return jnp.dot(jnp.concatenate([high, low, high], axis=1), tall, preferred_element_type=f32)


def rows_forward(re, im, forms):
    tr, br, ti, bi = re[:HALF], re[HALF:], im[:HALF], im[HALF:]
    e = left_mul(forms, EVEN, jnp.concatenate([tr + br, ti + bi], axis=0))
    o = left_mul(forms, ODD, jnp.concatenate([tr - br, ti - bi], axis=0))
    return e, o


def rows_inverse(re, im, forms):
    u = left_mul(forms, EVEN_T, jnp.concatenate([re[:HALF], im[:HALF]], axis=0))
    v = left_mul(forms, ODD_T, jnp.concatenate([re[HALF:], im[HALF:]], axis=0))
    return u, v


def lanes_forward(re, im, forms):
    lr, rr, li, ri = re[:, :HALF], re[:, HALF:], im[:, :HALF], im[:, HALF:]
    e = right_mul(jnp.concatenate([lr + rr, li + ri], axis=1), forms, EVEN_T)
    o = right_mul(jnp.concatenate([lr - rr, li - ri], axis=1), forms, ODD_T)
    return (
        jnp.concatenate([e[:, :HALF], o[:, :HALF]], axis=1),
        jnp.concatenate([e[:, HALF:], o[:, HALF:]], axis=1),
    )


def lanes_inverse(re, im, forms):
    u = right_mul(jnp.concatenate([re[:, :HALF], im[:, :HALF]], axis=1), forms, EVEN)
    v = right_mul(jnp.concatenate([re[:, HALF:], im[:, HALF:]], axis=1), forms, ODD)
    return (
        jnp.concatenate([u[:, :HALF] + v[:, :HALF], u[:, :HALF] - v[:, :HALF]], axis=1),
        jnp.concatenate([u[:, HALF:] + v[:, HALF:], u[:, HALF:] - v[:, HALF:]], axis=1),
    )


def cmul(ar, ai, br, bi):
    return ar * br - ai * bi, ar * bi + ai * br


def cmul_conj(ar, ai, br, bi):
    return ar * br + ai * bi, ar * bi - ai * br


INFO = 16


def decide(info, table):
    count = info[2 * CAP]
    rows = [jnp.bitwise_and(info[2 * j], WIN - 1) for j in range(CAP)]
    used = [(j < count).astype(jnp.int32) for j in range(CAP)]
    on_a = [used[j] * ((rows[j] + SUB - 1) // SUB) for j in range(CAP)]
    on_b = [used[j] * (GROUPS - rows[j] // SUB + INT_GROUPS) for j in range(CAP)]
    best, chosen = jnp.int32(10000), jnp.int32(0)
    for mask in range(1 << CAP):
        total_a = jnp.int32(0)
        total_b = jnp.int32(0)
        for j in range(CAP):
            if mask >> j & 1:
                total_b = total_b + on_b[j]
            else:
                total_a = total_a + on_a[j]
        cost = jnp.maximum(total_a, total_b)
        better = cost < best
        best = jnp.where(better, cost, best)
        chosen = jnp.where(better, mask, chosen)
    at_a = jnp.int32(0)
    at_b = jnp.int32(0)
    back = jnp.int32(0)
    for j in range(CAP):
        to_b = jnp.bitwise_and(chosen >> j, 1) * used[j]
        to_b = jnp.where(rows[j] == 0, 0, to_b)
        to_a = used[j] - to_b
        table[FIELDS * j] = to_a * AT_A + to_b * AT_B
        table[FIELDS * j + 1] = rows[j]
        table[FIELDS * j + 2] = info[2 * j + 1]
        table[FIELDS * j + 3] = jnp.where(to_b == 1, at_b, at_a)
        table[FIELDS * j + 4] = jnp.where(to_b == 1, back, at_a)
        at_a = at_a + to_a * on_a[j]
        at_b = at_b + to_b * on_b[j]
        back = back + to_b * (on_b[j] - INT_GROUPS)


def slot_of(table, j):
    base = FIELDS * j
    return table[base], table[base + 1], table[base + 2], table[base + 3], table[base + 4]


def lane_blocks(col):
    first = col // LANES
    starts = [jnp.minimum(first + k, 7) * LANES for k in range(3)]
    return [pl.multiple_of(start, LANES) for start in starts], jnp.bitwise_and(col, LANES - 1)


def lane_iota():
    return lax.broadcasted_iota(jnp.int32, (SUB, LANES), 1)


def load_group(field, plane, group, starts, shift):
    rows = pl.ds(pl.multiple_of(group * SUB, SUB), SUB)
    first = field[plane, rows, pl.ds(starts[0], LANES)]
    second = field[plane, rows, pl.ds(starts[1], LANES)]
    third = field[plane, rows, pl.ds(starts[2], LANES)]
    return jnp.where(lane_iota() >= shift, first, third), second


def add_group(total, plane, group, starts, shift, left, right):
    rows = pl.ds(pl.multiple_of(group * SUB, SUB), SUB)
    inside = lane_iota() >= shift
    total[plane, rows, pl.ds(starts[0], LANES)] += jnp.where(inside, left, 0.0)
    total[plane, rows, pl.ds(starts[1], LANES)] += right
    total[plane, rows, pl.ds(starts[2], LANES)] += jnp.where(inside, 0.0, left)


def pack_to_b(table, field, intensity, out):
    for j in range(CAP):
        state, row, col, start, _ = slot_of(table, j)

        @pl.when(state == AT_B)
        def _():
            starts, shift = lane_blocks(col)
            first = row // SUB

            def body(group, carry):
                at = start + group - first
                for plane in range(4):
                    left, right = load_group(field, plane, group, starts, shift)
                    out[at, plane, :, :LANES] = left
                    out[at, plane, :, LANES:] = right
                return carry

            lax.fori_loop(first, GROUPS, body, 0)
            after = start + GROUPS - first

            def body_int(group, carry):
                for plane in range(4):
                    rows = pl.ds(pl.multiple_of((group * 4 + plane) * SUB, SUB), SUB)
                    out[after + group, plane] = intensity[j, rows, :]
                return carry

            lax.fori_loop(0, INT_GROUPS, body_int, 0)


def pack_to_a(table, field, out):
    for j in range(CAP):
        state, row, col, start, _ = slot_of(table, j)

        @pl.when(state == AT_A)
        def _():
            starts, shift = lane_blocks(col)

            def body(group, carry):
                for plane in range(4):
                    left, right = load_group(field, plane, group, starts, shift)
                    out[start + group, plane, :, :LANES] = left
                    out[start + group, plane, :, LANES:] = right
                return carry

            lax.fori_loop(0, (row + SUB - 1) // SUB, body, 0)


def pack_early_kernel(odd, own, field, intensity, out, table):
    @pl.when(odd[0] == 1)
    def _():
        decide(own, table)
        pack_to_b(table, field, intensity, out)


def pack_late_kernel(odd, own, before, field, intensity, out, inner, table_in, table_out):
    @pl.when(odd[0] == 0)
    def _():
        decide(own, table_in)
        decide(before, table_out)
        pack_to_a(table_out, field, out)
        pack_to_b(table_in, field, intensity, inner)

    @pl.when(odd[0] == 1)
    def _():
        decide(before, table_in)
        decide(own, table_out)
        pack_to_a(table_in, field, inner)


def prepare_kernel(phases, shuffle, out, halves):
    for plane in range(2):
        halves[0] = phases[plane, :, :LANES]
        halves[1] = phases[plane, :, LANES:]
        for part in range(2):
            every = pl.ds(part, HALF, stride=2)
            x = jnp.concatenate([halves[0, every, :], halves[1, every, :]], axis=1)
            high = x.astype(bf16)
            rest = x - high.astype(f32)
            middle, low = split(rest)
            total = jnp.dot(high, shuffle[...], preferred_element_type=f32)
            total += jnp.dot(middle, shuffle[...], preferred_element_type=f32)
            total += jnp.dot(low, shuffle[...], preferred_element_type=f32)
            out[plane, part * HALF : (part + 1) * HALF, :] = total


def slots_kernel(
    first_kind,
    role,
    table,
    field,
    intensity,
    probe,
    kernel,
    forms,
    shuffle,
    from_b,
    from_a,
    total_in,
    total,
    back_a,
    back_b,
    got,
    tile,
    measured,
    twice,
    beam,
    work,
    entered,
    sem,
):
    is_a = role[0] == 0
    mine = jnp.where(is_a, AT_A, AT_B)

    def fetch(source):
        copy = pltpu.make_async_copy(source, got, sem)
        copy.start()
        copy.wait()

    @pl.when(is_a)
    def _():
        fetch(from_b)

    @pl.when(jnp.logical_not(is_a))
    def _():
        fetch(from_a)

    if first_kind:
        total[...] = jnp.zeros_like(total)
    else:
        copy = pltpu.make_async_copy(total_in, total, sem)
        copy.start()
        copy.wait()
    for plane in range(2):
        for part in range(2):
            cut = probe[plane, :, part * LANES : (part + 1) * LANES]
            twice[2 * plane + part, :WIN] = cut
            twice[2 * plane + part, WIN:] = cut

    def slot_body(j, carry):
        state, row, col, start, back = slot_of(table, j)

        @pl.when(state == mine)
        def _():
            starts, shift = lane_blocks(col)
            low = row // SUB
            base = jnp.where(is_a, start, start - low)
            sublane = lax.broadcasted_iota(jnp.int32, (SUB, LANES), 0)

            def own_rows(group):
                below = (group * SUB + sublane < row).astype(jnp.int32)
                return below == jnp.where(is_a, 0, 1)

            def gather(group, carry):
                own = own_rows(group)
                at = jnp.clip(base + group, 0, CAP_FWD - 1)
                rows = pl.ds(pl.multiple_of(group * SUB, SUB), SUB)
                for plane in range(4):
                    lf, rt = load_group(field, plane, group, starts, shift)
                    tile[plane, rows, :LANES] = jnp.where(own, lf, got[at, plane, :, :LANES])
                    tile[plane, rows, LANES:] = jnp.where(own, rt, got[at, plane, :, LANES:])
                return carry

            lax.fori_loop(0, GROUPS, gather, 0)

            @pl.when(is_a)
            def _():
                measured[0] = intensity[j, :, :LANES]
                measured[1] = intensity[j, :, LANES:]

            @pl.when(jnp.logical_not(is_a))
            def _():
                after = start + GROUPS - low

                def unpack(group, carry):
                    for plane in range(4):
                        rows = pl.ds(pl.multiple_of((group * 4 + plane) * SUB, SUB), SUB)
                        measured[0, rows, :] = got[after + group, plane, :, :LANES]
                        measured[1, rows, :] = got[after + group, plane, :, LANES:]
                    return carry

                lax.fori_loop(0, INT_GROUPS, unpack, 0)

            for plane in range(2):
                parts = [twice[2 * plane + part, pl.ds(WIN - row, WIN), :] for part in range(2)]
                beam[plane] = pltpu.roll(jnp.concatenate(parts, axis=1), shift, 1)

            def store_rows(e, o):
                work[0, :HALF], work[1, :HALF] = e[:HALF], e[HALF:]
                work[0, HALF:], work[1, HALF:] = o[:HALF], o[HALF:]

            def middle(pointwise):
                for half in range(2):
                    rows = pl.ds(half * HALF, HALF)
                    re, im = lanes_forward(work[0, rows, :], work[1, rows, :], forms)
                    re, im = pointwise(half, rows, re, im)
                    re, im = lanes_inverse(re, im, forms)
                    work[0, rows, :], work[1, rows, :] = re, im

            def unstack(u, v):
                return (
                    jnp.concatenate([u[:HALF] + v[:HALF], u[:HALF] - v[:HALF]], axis=0),
                    jnp.concatenate([u[HALF:] + v[HALF:], u[HALF:] - v[HALF:]], axis=0),
                )

            def propagate(half, rows, re, im):
                return cmul(kernel[0, rows, :], kernel[1, rows, :], re, im)

            def propagate_back(half, rows, re, im):
                return cmul_conj(kernel[0, rows, :], kernel[1, rows, :], re, im)

            def residual(half, rows, re, im):
                every = pl.ds(half, HALF, stride=2)
                rows_of = jnp.concatenate([measured[0, every, :], measured[1, every, :]], axis=1)
                high, low_part = split(rows_of)
                wanted = jnp.dot(high, shuffle[...], preferred_element_type=f32)
                wanted += jnp.dot(low_part, shuffle[...], preferred_element_type=f32)
                scale = re * re + im * im - wanted
                return scale * re, scale * im

            re, im = cmul(beam[0], beam[1], tile[0], tile[1])
            store_rows(*rows_forward(re, im, forms))
            middle(propagate)
            re, im = unstack(*rows_inverse(work[0], work[1], forms))
            entered[0], entered[1] = re, im
            re, im = cmul(re, im, tile[2], tile[3])
            store_rows(*rows_forward(re, im, forms))
            middle(residual)
            br, bi = unstack(*rows_inverse(work[0], work[1], forms))
            re, im = cmul_conj(tile[2], tile[3], br, bi)
            tile[2], tile[3] = cmul_conj(entered[0], entered[1], br, bi)
            store_rows(*rows_forward(re, im, forms))
            middle(propagate_back)
            br, bi = unstack(*rows_inverse(work[0], work[1], forms))
            tile[0], tile[1] = cmul_conj(beam[0], beam[1], br, bi)

            def scatter(group, carry):
                own = own_rows(group)
                rows = pl.ds(pl.multiple_of(group * SUB, SUB), SUB)
                for plane in range(4):
                    lf = jnp.where(own, tile[plane, rows, :LANES], 0.0)
                    rt = jnp.where(own, tile[plane, rows, LANES:], 0.0)
                    add_group(total, plane, group, starts, shift, lf, rt)
                return carry

            lax.fori_loop(jnp.where(is_a, low, 0), jnp.where(is_a, GROUPS, (row + SUB - 1) // SUB), scatter, 0)

            def send(out, offset):
                def body(group, carry):
                    rows = pl.ds(pl.multiple_of(group * SUB, SUB), SUB)
                    for plane in range(4):
                        out[offset + group, plane] = tile[plane, rows, :]
                    return carry

                return body

            @pl.when(is_a)
            def _():
                lax.fori_loop(0, (row + SUB - 1) // SUB, send(back_a, back), 0)

            @pl.when(jnp.logical_not(is_a))
            def _():
                lax.fori_loop(low, GROUPS, send(back_b, back - low), 0)

        return carry

    lax.fori_loop(0, CAP, slot_body, 0)


def finish_kernel(
    role_in, table_in, role_out, table_out, total_in, in_a, in_b, out_a, out_b, total, got_in, got_out, sem
):
    def start_copies(role, from_a, from_b, got, at):
        @pl.when(role[0] == 0)
        def _():
            pltpu.make_async_copy(from_b, got.at[pl.ds(0, CAP_BACK_B)], sem.at[at]).start()
            pltpu.make_async_copy(from_b, got.at[pl.ds(0, CAP_BACK_B)], sem.at[at]).wait()

        @pl.when(role[0] == 1)
        def _():
            pltpu.make_async_copy(from_a, got, sem.at[at]).start()
            pltpu.make_async_copy(from_a, got, sem.at[at]).wait()

    start_copies(role_in, in_a, in_b, got_in, 0)
    start_copies(role_out, out_a, out_b, got_out, 1)
    total[...] = total_in[...]
    for role, table, got in ((role_in, table_in, got_in), (role_out, table_out, got_out)):
        is_a = role[0] == 0
        theirs = jnp.where(is_a, AT_B, AT_A)
        for j in range(CAP):
            state, row, col, _, back = slot_of(table, j)

            @pl.when(state == theirs)
            def _():
                starts, shift = lane_blocks(col)
                low = row // SUB
                base = jnp.where(is_a, back - low, back)
                sublane = lax.broadcasted_iota(jnp.int32, (SUB, LANES), 0)

                def body(group, carry):
                    below = (group * SUB + sublane < row).astype(jnp.int32)
                    own = below == jnp.where(is_a, 0, 1)
                    for plane in range(4):
                        lf = jnp.where(own, got[base + group, plane, :, :LANES], 0.0)
                        rt = jnp.where(own, got[base + group, plane, :, LANES:], 0.0)
                        add_group(total, plane, group, starts, shift, lf, rt)
                    return carry

                lax.fori_loop(
                    jnp.where(is_a, low, 0), jnp.where(is_a, GROUPS, (row + SUB - 1) // SUB), body, 0
                )


def spec(space):
    return pl.BlockSpec(memory_space=space)


PARAMS = pltpu.CompilerParams(vmem_limit_bytes=48 << 20)


def packed(groups):
    return jax.ShapeDtypeStruct((groups, 4, SUB, WIN), f32)


def run_slots(first_kind, role, table, field, intensity, probe, kernel, tables, from_b, from_a, total):
    specs = [spec(SM)] * 2 + [spec(VM)] * 6 + [spec(pl.ANY)] * 3
    return pl.pallas_call(
        functools.partial(slots_kernel, first_kind),
        out_shape=(
            jax.ShapeDtypeStruct(field.shape, f32),
            packed(CAP_BACK_A),
            packed(CAP_BACK_B),
        ),
        in_specs=specs,
        out_specs=(spec(VM),) * 3,
        scratch_shapes=[
            pltpu.VMEM((CAP_FWD, 4, SUB, WIN), f32),
            pltpu.VMEM((4, WIN, WIN), f32),
            pltpu.VMEM((2, WIN, LANES), f32),
            pltpu.VMEM((4, 2 * WIN, LANES), f32),
            pltpu.VMEM((2, WIN, WIN), f32),
            pltpu.VMEM((2, WIN, WIN), f32),
            pltpu.VMEM((2, WIN, WIN), f32),
            pltpu.SemaphoreType.DMA,
        ],
        compiler_params=PARAMS,
    )(role, table, field, intensity, probe, kernel, *tables, from_b, from_a, total)


def shards(obj_field, probe_wave, prop_phase, win_offsets, live_counts, intensity):
    field = obj_field.reshape((4,) + obj_field.shape[2:])
    count = lax.axis_size("row")
    within = [(i, i + 1) for i in range(0, count - 1, 2)]
    across = [(i, i + 1) for i in range(1, count - 1, 2)]
    back = lambda pairs: [(b, a) for a, b in pairs]
    move = lambda x, pairs: lax.ppermute(x, "row", pairs)
    odd = jnp.bitwise_and(lax.axis_index("row"), 1)
    role_in = odd.reshape(1)
    role_out = (1 - odd).reshape(1)

    flag = odd.reshape(1)
    own = jnp.concatenate([win_offsets.reshape(-1), live_counts, jnp.zeros((INFO - 2 * CAP - 1,), jnp.int32)])
    before = move(own, within + across)
    to_b = pl.pallas_call(
        pack_early_kernel,
        out_shape=packed(CAP_FWD),
        in_specs=[spec(SM)] * 2 + [spec(VM)] * 2,
        out_specs=spec(VM),
        scratch_shapes=[pltpu.SMEM((CAP * FIELDS,), jnp.int32)],
        compiler_params=PARAMS,
    )(flag, own, field, intensity)
    out_from_a = move(to_b, across)
    table = jax.ShapeDtypeStruct((CAP * FIELDS,), jnp.int32)
    to_a, inner, table_in, table_out = pl.pallas_call(
        pack_late_kernel,
        out_shape=(packed(CAP_FWD), packed(CAP_FWD), table, table),
        in_specs=[spec(SM)] * 3 + [spec(VM)] * 2,
        out_specs=(spec(VM), spec(VM), spec(SM), spec(SM)),
        compiler_params=PARAMS,
    )(flag, own, before, field, intensity)
    out_from_b = move(to_a, back(across))
    in_from = move(inner, within + back(within))

    forms, shuffle = (jnp.asarray(t) for t in make_tables())
    kernel = pl.pallas_call(
        prepare_kernel,
        out_shape=jax.ShapeDtypeStruct((2, WIN, WIN), f32),
        in_specs=[spec(VM)] * 2,
        out_specs=spec(VM),
        scratch_shapes=[pltpu.VMEM((2, WIN, LANES), f32)],
        compiler_params=PARAMS,
    )(jnp.stack([jnp.cos(prop_phase), jnp.sin(prop_phase)]), shuffle)

    args = (field, intensity, probe_wave, kernel, (forms, shuffle))
    total, in_back_a, in_back_b = run_slots(True, role_in, table_in, *args, in_from, in_from, field)
    in_a = move(in_back_a, within)
    in_b = move(in_back_b, back(within))
    total, out_back_a, out_back_b = run_slots(False, role_out, table_out, *args, out_from_b, out_from_a, total)
    out_a = move(out_back_a, across)
    out_b = move(out_back_b, back(across))
    grad = pl.pallas_call(
        finish_kernel,
        out_shape=jax.ShapeDtypeStruct(field.shape, f32),
        in_specs=[spec(SM)] * 4 + [spec(VM)] + [spec(pl.ANY)] * 4,
        out_specs=spec(VM),
        scratch_shapes=[
            pltpu.VMEM((CAP_BACK_A, 4, SUB, WIN), f32),
            pltpu.VMEM((CAP_BACK_A, 4, SUB, WIN), f32),
            pltpu.SemaphoreType.DMA((2,)),
        ],
        input_output_aliases={4: 0},
        compiler_params=PARAMS,
    )(role_in, table_in, role_out, table_out, total, in_a, in_b, out_a, out_b)
    return grad.reshape(obj_field.shape)


def solution(mesh):
    in_specs = (
        P(None, None, ("groups", "row"), None),
        P("groups", None, None),
        P(),
        P(("groups", "row"), None),
        P(("groups", "row")),
        P(("groups", "row"), None, None),
    )
    out_specs = P(None, None, ("groups", "row"), None)
    return jax.shard_map(shards, mesh=mesh, in_specs=in_specs, out_specs=out_specs, check_vma=False)
```

```python
import functools

import jax
import jax.numpy as jnp
import numpy as np
from jax import lax
from jax.experimental import pallas as pl
from jax.experimental.pallas import tpu as pltpu
from jax.sharding import PartitionSpec as P

WIN = 256
HALF = WIN // 2
LANES = 128
SUB = 8
CAP = 4
GROUPS = WIN // SUB
INT_GROUPS = GROUPS // 4
CAP_FWD = 48
CAP_BACK_A = 48
CAP_BACK_B = 32
UNEVEN = 24
DEAD, AT_A, AT_B = 0, 1, 2
FIELDS = 8
f32 = jnp.float32
bf16 = jnp.bfloat16
VM = pltpu.MemorySpace.VMEM
SM = pltpu.MemorySpace.SMEM


def real_tables():
    k = np.arange(HALF)[:, None]
    n = np.arange(HALF)[None, :]
    out = []
    for odd in (0, 1):
        angle = 2.0 * np.pi * (((2 * k + odd) * n) % WIN) / WIN
        c, s = np.cos(angle) / 16.0, np.sin(angle) / 16.0
        out.append(np.block([[c, s], [-s, c]]))
    return out


def high_low(table):
    high = table.astype(np.float32).astype(bf16)
    low = (table - high.astype(np.float64)).astype(np.float32).astype(bf16)
    return high, low


def make_tables():
    even, odd = real_tables()
    forms = np.stack([np.stack(high_low(m)) for m in (even, odd, even.T, odd.T)])
    order = np.concatenate([np.arange(0, WIN, 2), np.arange(1, WIN, 2)])
    shuffle = np.zeros((WIN, WIN), np.float32)
    shuffle[order, np.arange(WIN)] = 1.0
    return forms, shuffle.astype(bf16)


EVEN, ODD, EVEN_T, ODD_T = range(4)


def split(x):
    high = x.astype(bf16)
    return high, (x - high.astype(f32)).astype(bf16)


def left_mul(forms, which, x):
    high, low = split(x)
    t_high, t_low = forms[which, 0], forms[which, 1]
    wide = jnp.concatenate([t_high, t_low, t_high], axis=1)
    return jnp.dot(wide, jnp.concatenate([high, high, low], axis=0), preferred_element_type=f32)


def right_mul(x, forms, which):
    high, low = split(x)
    t_high, t_low = forms[which, 0], forms[which, 1]
    tall = jnp.concatenate([t_high, t_high, t_low], axis=0)
    return jnp.dot(jnp.concatenate([high, low, high], axis=1), tall, preferred_element_type=f32)


def rows_forward(re, im, forms):
    tr, br, ti, bi = re[:HALF], re[HALF:], im[:HALF], im[HALF:]
    e = left_mul(forms, EVEN, jnp.concatenate([tr + br, ti + bi], axis=0))
    o = left_mul(forms, ODD, jnp.concatenate([tr - br, ti - bi], axis=0))
    return e, o


def rows_inverse(re, im, forms):
    u = left_mul(forms, EVEN_T, jnp.concatenate([re[:HALF], im[:HALF]], axis=0))
    v = left_mul(forms, ODD_T, jnp.concatenate([re[HALF:], im[HALF:]], axis=0))
    return u, v


def lanes_forward(re, im, forms):
    lr, rr, li, ri = re[:, :HALF], re[:, HALF:], im[:, :HALF], im[:, HALF:]
    e = right_mul(jnp.concatenate([lr + rr, li + ri], axis=1), forms, EVEN_T)
    o = right_mul(jnp.concatenate([lr - rr, li - ri], axis=1), forms, ODD_T)
    return (
        jnp.concatenate([e[:, :HALF], o[:, :HALF]], axis=1),
        jnp.concatenate([e[:, HALF:], o[:, HALF:]], axis=1),
    )


def lanes_inverse(re, im, forms):
    u = right_mul(jnp.concatenate([re[:, :HALF], im[:, :HALF]], axis=1), forms, EVEN)
    v = right_mul(jnp.concatenate([re[:, HALF:], im[:, HALF:]], axis=1), forms, ODD)
    return (
        jnp.concatenate([u[:, :HALF] + v[:, :HALF], u[:, :HALF] - v[:, :HALF]], axis=1),
        jnp.concatenate([u[:, HALF:] + v[:, HALF:], u[:, HALF:] - v[:, HALF:]], axis=1),
    )


def cmul(ar, ai, br, bi):
    return ar * br - ai * bi, ar * bi + ai * br


def cmul_conj(ar, ai, br, bi):
    return ar * br + ai * bi, ar * bi - ai * br


INFO = 16


def decide(info, table):
    count = info[2 * CAP]
    rows = [jnp.bitwise_and(info[2 * j], WIN - 1) for j in range(CAP)]
    used = [(j < count).astype(jnp.int32) for j in range(CAP)]
    on_a = [used[j] * ((rows[j] + SUB - 1) // SUB) for j in range(CAP)]
    on_b = [used[j] * (GROUPS - rows[j] // SUB + INT_GROUPS) for j in range(CAP)]
    best, chosen = jnp.int32(10000), jnp.int32(0)
    for mask in range(1 << CAP):
        total_a = jnp.int32(0)
        total_b = jnp.int32(0)
        slots_a = jnp.int32(0)
        slots_b = jnp.int32(0)
        for j in range(CAP):
            if mask >> j & 1:
                total_b = total_b + on_b[j]
                slots_b = slots_b + used[j]
            else:
                total_a = total_a + on_a[j]
                slots_a = slots_a + used[j]
        cost = jnp.maximum(total_a, total_b)
        cost = cost + jnp.where(cost > CAP_FWD, 1000, 0)
        cost = cost + jnp.where(jnp.maximum(slots_a, slots_b) > 2, UNEVEN, 0)
        better = cost < best
        best = jnp.where(better, cost, best)
        chosen = jnp.where(better, mask, chosen)
    at_a = jnp.int32(0)
    at_b = jnp.int32(0)
    back = jnp.int32(0)
    for j in range(CAP):
        to_b = jnp.bitwise_and(chosen >> j, 1) * used[j]
        to_b = jnp.where(rows[j] == 0, 0, to_b)
        to_a = used[j] - to_b
        table[FIELDS * j] = to_a * AT_A + to_b * AT_B
        table[FIELDS * j + 1] = rows[j]
        table[FIELDS * j + 2] = info[2 * j + 1]
        table[FIELDS * j + 3] = jnp.where(to_b == 1, at_b, at_a)
        table[FIELDS * j + 4] = jnp.where(to_b == 1, back, at_a)
        at_a = at_a + to_a * on_a[j]
        at_b = at_b + to_b * on_b[j]
        back = back + to_b * (on_b[j] - INT_GROUPS)


def slot_of(table, j):
    base = FIELDS * j
    return table[base], table[base + 1], table[base + 2], table[base + 3], table[base + 4]


def lane_blocks(col):
    first = col // LANES
    starts = [jnp.minimum(first + k, 7) * LANES for k in range(3)]
    return [pl.multiple_of(start, LANES) for start in starts], jnp.bitwise_and(col, LANES - 1)


def lane_iota():
    return lax.broadcasted_iota(jnp.int32, (SUB, LANES), 1)


def load_group(field, plane, group, starts, shift):
    rows = pl.ds(pl.multiple_of(group * SUB, SUB), SUB)
    first = field[plane, rows, pl.ds(starts[0], LANES)]
    second = field[plane, rows, pl.ds(starts[1], LANES)]
    third = field[plane, rows, pl.ds(starts[2], LANES)]
    return jnp.where(lane_iota() >= shift, first, third), second


def add_group(total, plane, group, starts, shift, left, right):
    rows = pl.ds(pl.multiple_of(group * SUB, SUB), SUB)
    inside = lane_iota() >= shift
    total[plane, rows, pl.ds(starts[0], LANES)] += jnp.where(inside, left, 0.0)
    total[plane, rows, pl.ds(starts[1], LANES)] += right
    total[plane, rows, pl.ds(starts[2], LANES)] += jnp.where(inside, 0.0, left)


def pack_to_b(table, field, intensity, out):
    for j in range(CAP):
        state, row, col, start, _ = slot_of(table, j)

        @pl.when(state == AT_B)
        def _():
            starts, shift = lane_blocks(col)
            first = row // SUB

            def body(group, carry):
                at = start + group - first
                for plane in range(4):
                    left, right = load_group(field, plane, group, starts, shift)
                    out[at, plane, :, :LANES] = left
                    out[at, plane, :, LANES:] = right
                return carry

            lax.fori_loop(first, GROUPS, body, 0)
            after = start + GROUPS - first

            def body_int(group, carry):
                for plane in range(4):
                    rows = pl.ds(pl.multiple_of((group * 4 + plane) * SUB, SUB), SUB)
                    out[after + group, plane] = intensity[j, rows, :]
                return carry

            lax.fori_loop(0, INT_GROUPS, body_int, 0)


def pack_to_a(table, field, out):
    for j in range(CAP):
        state, row, col, start, _ = slot_of(table, j)

        @pl.when(state == AT_A)
        def _():
            starts, shift = lane_blocks(col)

            def body(group, carry):
                for plane in range(4):
                    left, right = load_group(field, plane, group, starts, shift)
                    out[start + group, plane, :, :LANES] = left
                    out[start + group, plane, :, LANES:] = right
                return carry

            lax.fori_loop(0, (row + SUB - 1) // SUB, body, 0)


def pack_early_kernel(odd, own, field, intensity, out, table):
    @pl.when(odd[0] == 1)
    def _():
        decide(own, table)
        pack_to_b(table, field, intensity, out)


def pack_late_kernel(odd, own, before, field, intensity, out, inner, table_in, table_out):
    @pl.when(odd[0] == 0)
    def _():
        decide(own, table_in)
        decide(before, table_out)
        pack_to_a(table_out, field, out)
        pack_to_b(table_in, field, intensity, inner)

    @pl.when(odd[0] == 1)
    def _():
        decide(before, table_in)
        decide(own, table_out)
        pack_to_a(table_in, field, inner)


def prepare_kernel(phases, shuffle, out, halves):
    for plane in range(2):
        halves[0] = phases[plane, :, :LANES]
        halves[1] = phases[plane, :, LANES:]
        for part in range(2):
            every = pl.ds(part, HALF, stride=2)
            x = jnp.concatenate([halves[0, every, :], halves[1, every, :]], axis=1)
            high = x.astype(bf16)
            rest = x - high.astype(f32)
            middle, low = split(rest)
            total = jnp.dot(high, shuffle[...], preferred_element_type=f32)
            total += jnp.dot(middle, shuffle[...], preferred_element_type=f32)
            total += jnp.dot(low, shuffle[...], preferred_element_type=f32)
            out[plane, part * HALF : (part + 1) * HALF, :] = total


def slots_kernel(joint, role, table, field, intensity, probe, kernel, forms, shuffle, from_b, from_a, *rest):
    back_a, back_b = rest[0], rest[0 if joint else 1]
    tiles, got, tile, measured, twice, beam, work, entered, chosen, got_sem, tile_sem = rest[1 if joint else 2 :]
    is_a = role[0] == 0
    mine = jnp.where(is_a, AT_A, AT_B)

    @pl.when(is_a)
    def _():
        pltpu.make_async_copy(from_b, got, got_sem).start()

    @pl.when(jnp.logical_not(is_a))
    def _():
        pltpu.make_async_copy(from_a, got, got_sem).start()

    for plane in range(2):
        for part in range(2):
            cut = probe[plane, :, part * LANES : (part + 1) * LANES]
            twice[2 * plane + part, :WIN] = cut
            twice[2 * plane + part, WIN:] = cut
    found = jnp.int32(0)
    for j in range(CAP):
        chosen[j] = 0
    for j in range(CAP):
        state = table[FIELDS * j]

        @pl.when(state == mine)
        def _():
            chosen[found] = j

        found = found + (state == mine).astype(jnp.int32)
    pltpu.make_async_copy(from_b, got, got_sem).wait()
    sublane = lax.broadcasted_iota(jnp.int32, (SUB, LANES), 0)

    def load(m, j):
        _, row, col, start, _ = slot_of(table, j)
        starts, shift = lane_blocks(col)
        low = row // SUB
        base = jnp.where(is_a, start, start - low)

        def gather(group, carry):
            below = (group * SUB + sublane < row).astype(jnp.int32)
            own = below == jnp.where(is_a, 0, 1)
            at = jnp.clip(base + group, 0, CAP_FWD - 1)
            rows = pl.ds(pl.multiple_of(group * SUB, SUB), SUB)
            for plane in range(4):
                lf, rt = load_group(field, plane, group, starts, shift)
                tile[m, plane, rows, :LANES] = jnp.where(own, lf, got[at, plane, :, :LANES])
                tile[m, plane, rows, LANES:] = jnp.where(own, rt, got[at, plane, :, LANES:])
            return carry

        lax.fori_loop(0, GROUPS, gather, 0)

        @pl.when(is_a)
        def _():
            measured[m, 0] = intensity[j, :, :LANES]
            measured[m, 1] = intensity[j, :, LANES:]

        @pl.when(jnp.logical_not(is_a))
        def _():
            after = start + GROUPS - low

            def unpack(group, carry):
                for plane in range(4):
                    rows = pl.ds(pl.multiple_of((group * 4 + plane) * SUB, SUB), SUB)
                    measured[m, 0, rows, :] = got[after + group, plane, :, :LANES]
                    measured[m, 1, rows, :] = got[after + group, plane, :, LANES:]
                return carry

            lax.fori_loop(0, INT_GROUPS, unpack, 0)

        for plane in range(2):
            parts = [twice[2 * plane + part, pl.ds(WIN - row, WIN), :] for part in range(2)]
            beam[m, plane] = pltpu.roll(jnp.concatenate(parts, axis=1), shift, 1)

    def store_rows(m, e, o):
        work[m, 0, :HALF], work[m, 1, :HALF] = e[:HALF], e[HALF:]
        work[m, 0, HALF:], work[m, 1, HALF:] = o[:HALF], o[HALF:]

    def middle(pointwise):
        for half in range(2):
            rows = pl.ds(half * HALF, HALF)
            for m in range(2):
                re, im = lanes_forward(work[m, 0, rows, :], work[m, 1, rows, :], forms)
                re, im = pointwise(m, half, rows, re, im)
                re, im = lanes_inverse(re, im, forms)
                work[m, 0, rows, :], work[m, 1, rows, :] = re, im

    def rows_back(m):
        u, v = rows_inverse(work[m, 0], work[m, 1], forms)
        return (
            jnp.concatenate([u[:HALF] + v[:HALF], u[:HALF] - v[:HALF]], axis=0),
            jnp.concatenate([u[HALF:] + v[HALF:], u[HALF:] - v[HALF:]], axis=0),
        )

    def propagate(m, half, rows, re, im):
        return cmul(kernel[0, rows, :], kernel[1, rows, :], re, im)

    def propagate_back(m, half, rows, re, im):
        return cmul_conj(kernel[0, rows, :], kernel[1, rows, :], re, im)

    def residual(m, half, rows, re, im):
        every = pl.ds(half, HALF, stride=2)
        rows_of = jnp.concatenate([measured[m, 0, every, :], measured[m, 1, every, :]], axis=1)
        high, low = split(rows_of)
        wanted = jnp.dot(high, shuffle[...], preferred_element_type=f32)
        wanted += jnp.dot(low, shuffle[...], preferred_element_type=f32)
        scale = re * re + im * im - wanted
        return scale * re, scale * im

    def write(m, j):
        _, row, _, _, back = slot_of(table, j)
        low = row // SUB

        def send(out, offset):
            def body(group, carry):
                rows = pl.ds(pl.multiple_of(group * SUB, SUB), SUB)
                for plane in range(4):
                    out[offset + group, plane] = tile[m, plane, rows, :]
                return carry

            return body

        pltpu.make_async_copy(tile.at[m], tiles.at[j], tile_sem.at[m]).start()

        @pl.when(is_a)
        def _():
            lax.fori_loop(0, (row + SUB - 1) // SUB, send(back_a, back), 0)

        @pl.when(jnp.logical_not(is_a))
        def _():
            lax.fori_loop(low, GROUPS, send(back_b, back - low), 0)

        pltpu.make_async_copy(tile.at[m], tiles.at[j], tile_sem.at[m]).wait()

    def pair(p, carry):
        two = 2 * p + 1 < found
        first = chosen[2 * p]
        second = jnp.where(two, chosen[jnp.minimum(2 * p + 1, CAP - 1)], first)
        load(0, first)
        load(1, second)
        for m in range(2):
            re, im = cmul(beam[m, 0], beam[m, 1], tile[m, 0], tile[m, 1])
            store_rows(m, *rows_forward(re, im, forms))
        middle(propagate)
        for m in range(2):
            re, im = rows_back(m)
            entered[m, 0], entered[m, 1] = re, im
            re, im = cmul(re, im, tile[m, 2], tile[m, 3])
            store_rows(m, *rows_forward(re, im, forms))
        middle(residual)
        for m in range(2):
            br, bi = rows_back(m)
            re, im = cmul_conj(tile[m, 2], tile[m, 3], br, bi)
            tile[m, 2], tile[m, 3] = cmul_conj(entered[m, 0], entered[m, 1], br, bi)
            store_rows(m, *rows_forward(re, im, forms))
        middle(propagate_back)
        for m in range(2):
            br, bi = rows_back(m)
            tile[m, 0], tile[m, 1] = cmul_conj(beam[m, 0], beam[m, 1], br, bi)
        write(0, first)

        @pl.when(two)
        def _():
            write(1, second)

        return carry

    lax.fori_loop(0, (found + 1) // 2, pair, 0)


def add_back(role, table, got, total, planes):
    is_a = role[0] == 0
    theirs = jnp.where(is_a, AT_B, AT_A)
    for j in range(CAP):
        state, row, col, _, back = slot_of(table, j)

        @pl.when(state == theirs)
        def _():
            starts, shift = lane_blocks(col)
            low = row // SUB
            base = jnp.where(is_a, back - low, back)
            sublane = lax.broadcasted_iota(jnp.int32, (SUB, LANES), 0)

            def body(group, carry):
                below = (group * SUB + sublane < row).astype(jnp.int32)
                own = below == jnp.where(is_a, 0, 1)
                for plane in planes:
                    lf = jnp.where(own, got[base + group, plane, :, :LANES], 0.0)
                    rt = jnp.where(own, got[base + group, plane, :, LANES:], 0.0)
                    add_group(total, plane, group, starts, shift, lf, rt)
                return carry

            lax.fori_loop(jnp.where(is_a, low, 0), jnp.where(is_a, GROUPS, (row + SUB - 1) // SUB), body, 0)


def sum_kernel(
    role_in, table_in, role_out, table_out, in_back, tiles_in, tiles_out, total, got, tile, got_sem, tile_sem
):
    pltpu.make_async_copy(in_back, got, got_sem).start()
    sublane = lax.broadcasted_iota(jnp.int32, (SUB, LANES), 0)
    kinds = ((role_in, table_in, tiles_in), (role_out, table_out, tiles_out))
    for k, (role, table, tiles) in enumerate(kinds):
        mine = jnp.where(role[0] == 0, AT_A, AT_B)
        for j in range(CAP):

            @pl.when(table[FIELDS * j] == mine)
            def _():
                pltpu.make_async_copy(tiles.at[j], tile.at[k * CAP + j], tile_sem.at[k * CAP + j]).start()

    total[...] = jnp.zeros_like(total)
    pltpu.make_async_copy(in_back, got, got_sem).wait()
    add_back(role_in, table_in, got, total, range(4))
    for k, (role, table, tiles) in enumerate(kinds):
        is_a = role[0] == 0
        mine = jnp.where(is_a, AT_A, AT_B)
        for j in range(CAP):
            state, row, col, _, _ = slot_of(table, j)

            @pl.when(state == mine)
            def _():
                at = k * CAP + j
                pltpu.make_async_copy(tiles.at[j], tile.at[at], tile_sem.at[at]).wait()
                starts, shift = lane_blocks(col)
                low = row // SUB

                def body(group, carry):
                    below = (group * SUB + sublane < row).astype(jnp.int32)
                    own = below == jnp.where(is_a, 0, 1)
                    rows = pl.ds(pl.multiple_of(group * SUB, SUB), SUB)
                    for plane in range(4):
                        lf = jnp.where(own, tile[at, plane, rows, :LANES], 0.0)
                        rt = jnp.where(own, tile[at, plane, rows, LANES:], 0.0)
                        add_group(total, plane, group, starts, shift, lf, rt)
                    return carry

                lax.fori_loop(
                    jnp.where(is_a, low, 0), jnp.where(is_a, GROUPS, (row + SUB - 1) // SUB), body, 0
                )


def finish_kernel(role, table, total_in, out_a, out_b, grad, total, got, got_sem, out_sem):
    is_a = role[0] == 0

    @pl.when(is_a)
    def _():
        copy = pltpu.make_async_copy(out_b, got.at[pl.ds(0, CAP_BACK_B)], got_sem)
        copy.start()
        copy.wait()

    @pl.when(jnp.logical_not(is_a))
    def _():
        copy = pltpu.make_async_copy(out_a, got, got_sem)
        copy.start()
        copy.wait()

    for plane in range(4):
        total[plane] = total_in[plane]
        add_back(role, table, got, total, (plane,))
        pltpu.make_async_copy(total.at[plane], grad.at[plane], out_sem.at[plane]).start()
    for plane in range(4):
        pltpu.make_async_copy(total.at[plane], grad.at[plane], out_sem.at[plane]).wait()


def spec(space):
    return pl.BlockSpec(memory_space=space)


PARAMS = pltpu.CompilerParams(vmem_limit_bytes=48 << 20)


def packed(groups):
    return jax.ShapeDtypeStruct((groups, 4, SUB, WIN), f32)


def run_slots(joint, role, table, field, intensity, probe, kernel, tables, from_b, from_a):
    backs = (CAP_BACK_A,) if joint else (CAP_BACK_A, CAP_BACK_B)
    return pl.pallas_call(
        functools.partial(slots_kernel, joint),
        out_shape=tuple(packed(n) for n in backs) + (jax.ShapeDtypeStruct((CAP, 4, WIN, WIN), f32),),
        in_specs=[spec(SM)] * 2 + [spec(VM)] * 6 + [spec(pl.ANY)] * 2,
        out_specs=(spec(VM),) * len(backs) + (spec(pl.ANY),),
        scratch_shapes=[
            pltpu.VMEM((CAP_FWD, 4, SUB, WIN), f32),
            pltpu.VMEM((2, 4, WIN, WIN), f32),
            pltpu.VMEM((2, 2, WIN, LANES), f32),
            pltpu.VMEM((4, 2 * WIN, LANES), f32),
            pltpu.VMEM((2, 2, WIN, WIN), f32),
            pltpu.VMEM((2, 2, WIN, WIN), f32),
            pltpu.VMEM((2, 2, WIN, WIN), f32),
            pltpu.SMEM((CAP,), jnp.int32),
            pltpu.SemaphoreType.DMA,
            pltpu.SemaphoreType.DMA((2,)),
        ],
        compiler_params=PARAMS,
    )(role, table, field, intensity, probe, kernel, *tables, from_b, from_a)


def shards(obj_field, probe_wave, prop_phase, win_offsets, live_counts, intensity):
    field = obj_field.reshape((4,) + obj_field.shape[2:])
    count = lax.axis_size("row")
    within = [(i, i + 1) for i in range(0, count - 1, 2)]
    across = [(i, i + 1) for i in range(1, count - 1, 2)]
    back = lambda pairs: [(b, a) for a, b in pairs]
    move = lambda x, pairs: lax.ppermute(x, "row", pairs)
    odd = jnp.bitwise_and(lax.axis_index("row"), 1)
    role_in = odd.reshape(1)
    role_out = (1 - odd).reshape(1)

    flag = odd.reshape(1)
    own = jnp.concatenate([win_offsets.reshape(-1), live_counts, jnp.zeros((INFO - 2 * CAP - 1,), jnp.int32)])
    before = move(own, within + across)
    to_b = pl.pallas_call(
        pack_early_kernel,
        out_shape=packed(CAP_FWD),
        in_specs=[spec(SM)] * 2 + [spec(VM)] * 2,
        out_specs=spec(VM),
        scratch_shapes=[pltpu.SMEM((CAP * FIELDS,), jnp.int32)],
        compiler_params=PARAMS,
    )(flag, own, field, intensity)
    out_from_a = move(to_b, across)
    table = jax.ShapeDtypeStruct((CAP * FIELDS,), jnp.int32)
    to_a, inner, table_in, table_out = pl.pallas_call(
        pack_late_kernel,
        out_shape=(packed(CAP_FWD), packed(CAP_FWD), table, table),
        in_specs=[spec(SM)] * 3 + [spec(VM)] * 2,
        out_specs=(spec(VM), spec(VM), spec(SM), spec(SM)),
        compiler_params=PARAMS,
    )(flag, own, before, field, intensity)
    out_from_b = move(to_a, back(across))
    in_from = move(inner, within + back(within))

    forms, shuffle = (jnp.asarray(t) for t in make_tables())
    kernel = pl.pallas_call(
        prepare_kernel,
        out_shape=jax.ShapeDtypeStruct((2, WIN, WIN), f32),
        in_specs=[spec(VM)] * 2,
        out_specs=spec(VM),
        scratch_shapes=[pltpu.VMEM((2, WIN, LANES), f32)],
        compiler_params=PARAMS,
    )(jnp.stack([jnp.cos(prop_phase), jnp.sin(prop_phase)]), shuffle)

    args = (field, intensity, probe_wave, kernel, (forms, shuffle))
    in_back, tiles_in = run_slots(True, role_in, table_in, *args, in_from, in_from)
    in_back = move(in_back, within + back(within))
    out_back_a, out_back_b, tiles_out = run_slots(False, role_out, table_out, *args, out_from_b, out_from_a)
    out_a = move(out_back_a, across)
    out_b = move(out_back_b, back(across))
    total = pl.pallas_call(
        sum_kernel,
        out_shape=jax.ShapeDtypeStruct(field.shape, f32),
        in_specs=[spec(SM)] * 4 + [spec(pl.ANY)] * 3,
        out_specs=spec(VM),
        scratch_shapes=[
            pltpu.VMEM((CAP_BACK_A, 4, SUB, WIN), f32),
            pltpu.VMEM((2 * CAP, 4, WIN, WIN), f32),
            pltpu.SemaphoreType.DMA,
            pltpu.SemaphoreType.DMA((2 * CAP,)),
        ],
        compiler_params=PARAMS,
    )(role_in, table_in, role_out, table_out, in_back, tiles_in, tiles_out)
    grad = pl.pallas_call(
        finish_kernel,
        out_shape=jax.ShapeDtypeStruct(field.shape, f32),
        in_specs=[spec(SM)] * 2 + [spec(VM)] + [spec(pl.ANY)] * 2,
        out_specs=spec(pl.ANY),
        scratch_shapes=[
            pltpu.VMEM(field.shape, f32),
            pltpu.VMEM((CAP_BACK_A, 4, SUB, WIN), f32),
            pltpu.SemaphoreType.DMA,
            pltpu.SemaphoreType.DMA((4,)),
        ],
        compiler_params=PARAMS,
    )(role_out, table_out, total, out_a, out_b)
    return grad.reshape(obj_field.shape)


def solution(mesh):
    in_specs = (
        P(None, None, ("groups", "row"), None),
        P("groups", None, None),
        P(),
        P(("groups", "row"), None),
        P(("groups", "row")),
        P(("groups", "row"), None, None),
    )
    out_specs = P(None, None, ("groups", "row"), None)
    return jax.shard_map(shards, mesh=mesh, in_specs=in_specs, out_specs=out_specs, check_vma=False)
```

```python
import functools

import jax
import jax.numpy as jnp
import numpy as np
from jax import lax
from jax.experimental import pallas as pl
from jax.experimental.pallas import tpu as pltpu
from jax.sharding import PartitionSpec as P

WIN = 256
HALF = WIN // 2
LANES = 128
SUB = 8
CAP = 4
GROUPS = WIN // SUB
INT_GROUPS = GROUPS // 4
CAP_FWD = 48
CAP_BACK_A = 48
CAP_BACK_B = 32
UNEVEN = 24
DEAD, AT_A, AT_B = 0, 1, 2
FIELDS = 8
f32 = jnp.float32
bf16 = jnp.bfloat16
VM = pltpu.MemorySpace.VMEM
SM = pltpu.MemorySpace.SMEM


def real_tables():
    k = np.arange(HALF)[:, None]
    n = np.arange(HALF)[None, :]
    out = []
    for odd in (0, 1):
        angle = 2.0 * np.pi * (((2 * k + odd) * n) % WIN) / WIN
        c, s = np.cos(angle) / 16.0, np.sin(angle) / 16.0
        out.append(np.block([[c, s], [-s, c]]))
    return out


def high_low(table):
    high = table.astype(np.float32).astype(bf16)
    low = (table - high.astype(np.float64)).astype(np.float32).astype(bf16)
    return high, low


def make_tables():
    even, odd = real_tables()
    forms = np.stack([np.stack(high_low(m)) for m in (even, odd, even.T, odd.T)])
    order = np.concatenate([np.arange(0, WIN, 2), np.arange(1, WIN, 2)])
    shuffle = np.zeros((WIN, WIN), np.float32)
    shuffle[order, np.arange(WIN)] = 1.0
    return forms, shuffle.astype(bf16)


EVEN, ODD, EVEN_T, ODD_T = range(4)


def split(x):
    high = x.astype(bf16)
    return high, (x - high.astype(f32)).astype(bf16)


def left_mul(forms, which, x):
    high, low = split(x)
    t_high, t_low = forms[which, 0], forms[which, 1]
    wide = jnp.concatenate([t_high, t_low, t_high], axis=1)
    return jnp.dot(wide, jnp.concatenate([high, high, low], axis=0), preferred_element_type=f32)


def right_mul(x, forms, which):
    high, low = split(x)
    t_high, t_low = forms[which, 0], forms[which, 1]
    tall = jnp.concatenate([t_high, t_high, t_low], axis=0)
    return jnp.dot(jnp.concatenate([high, low, high], axis=1), tall, preferred_element_type=f32)


def rows_forward(re, im, forms):
    tr, br, ti, bi = re[:HALF], re[HALF:], im[:HALF], im[HALF:]
    e = left_mul(forms, EVEN, jnp.concatenate([tr + br, ti + bi], axis=0))
    o = left_mul(forms, ODD, jnp.concatenate([tr - br, ti - bi], axis=0))
    return e, o


def rows_inverse(re, im, forms):
    u = left_mul(forms, EVEN_T, jnp.concatenate([re[:HALF], im[:HALF]], axis=0))
    v = left_mul(forms, ODD_T, jnp.concatenate([re[HALF:], im[HALF:]], axis=0))
    return u, v


def lanes_forward(re, im, forms):
    lr, rr, li, ri = re[:, :HALF], re[:, HALF:], im[:, :HALF], im[:, HALF:]
    e = right_mul(jnp.concatenate([lr + rr, li + ri], axis=1), forms, EVEN_T)
    o = right_mul(jnp.concatenate([lr - rr, li - ri], axis=1), forms, ODD_T)
    return (
        jnp.concatenate([e[:, :HALF], o[:, :HALF]], axis=1),
        jnp.concatenate([e[:, HALF:], o[:, HALF:]], axis=1),
    )


def lanes_inverse(re, im, forms):
    u = right_mul(jnp.concatenate([re[:, :HALF], im[:, :HALF]], axis=1), forms, EVEN)
    v = right_mul(jnp.concatenate([re[:, HALF:], im[:, HALF:]], axis=1), forms, ODD)
    return (
        jnp.concatenate([u[:, :HALF] + v[:, :HALF], u[:, :HALF] - v[:, :HALF]], axis=1),
        jnp.concatenate([u[:, HALF:] + v[:, HALF:], u[:, HALF:] - v[:, HALF:]], axis=1),
    )


def cmul(ar, ai, br, bi):
    return ar * br - ai * bi, ar * bi + ai * br


def cmul_conj(ar, ai, br, bi):
    return ar * br + ai * bi, ar * bi - ai * br


INFO = 16


def decide(info, table):
    count = info[2 * CAP]
    rows = [jnp.bitwise_and(info[2 * j], WIN - 1) for j in range(CAP)]
    used = [(j < count).astype(jnp.int32) for j in range(CAP)]
    on_a = [used[j] * ((rows[j] + SUB - 1) // SUB) for j in range(CAP)]
    on_b = [used[j] * (GROUPS - rows[j] // SUB + INT_GROUPS) for j in range(CAP)]
    best, chosen = jnp.int32(10000), jnp.int32(0)
    for mask in range(1 << CAP):
        total_a = jnp.int32(0)
        total_b = jnp.int32(0)
        slots_a = jnp.int32(0)
        slots_b = jnp.int32(0)
        for j in range(CAP):
            if mask >> j & 1:
                total_b = total_b + on_b[j]
                slots_b = slots_b + used[j]
            else:
                total_a = total_a + on_a[j]
                slots_a = slots_a + used[j]
        cost = jnp.maximum(total_a, total_b)
        cost = cost + jnp.where(cost > CAP_FWD, 1000, 0)
        cost = cost + jnp.where(jnp.maximum(slots_a, slots_b) > 2, UNEVEN, 0)
        better = cost < best
        best = jnp.where(better, cost, best)
        chosen = jnp.where(better, mask, chosen)
    at_a = jnp.int32(0)
    at_b = jnp.int32(0)
    back = jnp.int32(0)
    for j in range(CAP):
        to_b = jnp.bitwise_and(chosen >> j, 1) * used[j]
        to_b = jnp.where(rows[j] == 0, 0, to_b)
        to_a = used[j] - to_b
        table[FIELDS * j] = to_a * AT_A + to_b * AT_B
        table[FIELDS * j + 1] = rows[j]
        table[FIELDS * j + 2] = info[2 * j + 1]
        table[FIELDS * j + 3] = jnp.where(to_b == 1, at_b, at_a)
        table[FIELDS * j + 4] = jnp.where(to_b == 1, back, at_a)
        at_a = at_a + to_a * on_a[j]
        at_b = at_b + to_b * on_b[j]
        back = back + to_b * (on_b[j] - INT_GROUPS)


def slot_of(table, j):
    base = FIELDS * j
    return table[base], table[base + 1], table[base + 2], table[base + 3], table[base + 4]


def lane_blocks(col):
    first = col // LANES
    starts = [jnp.minimum(first + k, 7) * LANES for k in range(3)]
    return [pl.multiple_of(start, LANES) for start in starts], jnp.bitwise_and(col, LANES - 1)


WIDE = 3 * LANES


def near_columns(col):
    first = jnp.minimum(col // LANES, 5)
    skip = col // LANES - first
    starts = [pl.multiple_of(jnp.minimum(skip + k, 2) * LANES, LANES) for k in range(3)]
    return pl.ds(pl.multiple_of(first * LANES, LANES), WIDE), starts, jnp.bitwise_and(col, LANES - 1)


def lane_iota():
    return lax.broadcasted_iota(jnp.int32, (SUB, LANES), 1)


def load_group(field, plane, group, starts, shift):
    rows = pl.ds(pl.multiple_of(group * SUB, SUB), SUB)
    first = field[plane, rows, pl.ds(starts[0], LANES)]
    second = field[plane, rows, pl.ds(starts[1], LANES)]
    third = field[plane, rows, pl.ds(starts[2], LANES)]
    return jnp.where(lane_iota() >= shift, first, third), second


def add_group(total, plane, group, starts, shift, left, right):
    rows = pl.ds(pl.multiple_of(group * SUB, SUB), SUB)
    inside = lane_iota() >= shift
    total[plane, rows, pl.ds(starts[0], LANES)] += jnp.where(inside, left, 0.0)
    total[plane, rows, pl.ds(starts[1], LANES)] += right
    total[plane, rows, pl.ds(starts[2], LANES)] += jnp.where(inside, 0.0, left)


def fetch_columns(table, wanted, field, held, sem, base):
    for j in range(CAP):

        @pl.when(table[FIELDS * j] == wanted)
        def _():
            columns, _, _ = near_columns(table[FIELDS * j + 2])
            pltpu.make_async_copy(field.at[:, :, columns], held.at[base + j], sem.at[base + j]).start()


def copy_groups(held, out, at, offset, low, high, starts, shift):
    def body(group, carry):
        for plane in range(4):
            left, right = load_group(held.at[at], plane, group, starts, shift)
            out[offset + group, plane, :, :LANES] = left
            out[offset + group, plane, :, LANES:] = right
        return carry

    lax.fori_loop(low, high, body, 0)


def pack_to_b(table, field, intensity, out, held, sem, int_sem, base):
    def intensity_copy(j):
        _, row, _, start, _ = slot_of(table, j)
        after = start + GROUPS - row // SUB
        return pltpu.make_async_copy(intensity.at[j], out.at[pl.ds(after, INT_GROUPS)], int_sem.at[j])

    for j in range(CAP):

        @pl.when(table[FIELDS * j] == AT_B)
        def _():
            intensity_copy(j).start()

    for j in range(CAP):
        state, row, col, start, _ = slot_of(table, j)

        @pl.when(state == AT_B)
        def _():
            columns, starts, shift = near_columns(col)
            at = base + j
            pltpu.make_async_copy(field.at[:, :, columns], held.at[at], sem.at[at]).wait()
            copy_groups(held, out, at, start - row // SUB, row // SUB, GROUPS, starts, shift)
            intensity_copy(j).wait()


def pack_to_a(table, field, out, held, sem, base):
    for j in range(CAP):
        state, row, col, start, _ = slot_of(table, j)

        @pl.when(state == AT_A)
        def _():
            columns, starts, shift = near_columns(col)
            at = base + j
            pltpu.make_async_copy(field.at[:, :, columns], held.at[at], sem.at[at]).wait()
            copy_groups(held, out, at, start, 0, (row + SUB - 1) // SUB, starts, shift)


def pack_early_kernel(odd, own, field, intensity, out, info, table, held, sem, int_sem):
    for j in range(INFO):
        info[j] = own[j]

    @pl.when(odd[0] == 1)
    def _():
        decide(own, table)
        fetch_columns(table, AT_B, field, held, sem, 0)
        pack_to_b(table, field, intensity, out, held, sem, int_sem, 0)


def pack_late_kernel(odd, own, before, field, intensity, out, inner, table_in, table_out, held, sem, int_sem):
    @pl.when(odd[0] == 0)
    def _():
        decide(before, table_out)
        fetch_columns(table_out, AT_A, field, held, sem, 0)
        decide(own, table_in)
        fetch_columns(table_in, AT_B, field, held, sem, CAP)
        pack_to_a(table_out, field, out, held, sem, 0)
        pack_to_b(table_in, field, intensity, inner, held, sem, int_sem, CAP)

    @pl.when(odd[0] == 1)
    def _():
        decide(before, table_in)
        fetch_columns(table_in, AT_A, field, held, sem, 0)
        decide(own, table_out)
        pack_to_a(table_in, field, inner, held, sem, 0)


def prepare_kernel(phases, shuffle, out, halves):
    for plane in range(2):
        halves[0] = phases[plane, :, :LANES]
        halves[1] = phases[plane, :, LANES:]
        for part in range(2):
            every = pl.ds(part, HALF, stride=2)
            x = jnp.concatenate([halves[0, every, :], halves[1, every, :]], axis=1)
            high = x.astype(bf16)
            rest = x - high.astype(f32)
            middle, low = split(rest)
            total = jnp.dot(high, shuffle[...], preferred_element_type=f32)
            total += jnp.dot(middle, shuffle[...], preferred_element_type=f32)
            total += jnp.dot(low, shuffle[...], preferred_element_type=f32)
            out[plane, part * HALF : (part + 1) * HALF, :] = total


def slots_kernel(joint, role, table, field, intensity, probe, kernel, forms, shuffle, from_b, from_a, *rest):
    back_a, back_b = rest[0], rest[0 if joint else 1]
    tiles, held, got, tile, measured, twice, beam, work, entered, chosen = rest[1 if joint else 2 : -4]
    held_sem, int_sem, got_sem, tile_sem = rest[-4:]
    is_a = role[0] == 0
    mine = jnp.where(is_a, AT_A, AT_B)

    @pl.when(is_a)
    def _():
        pltpu.make_async_copy(from_b, got, got_sem).start()

    @pl.when(jnp.logical_not(is_a))
    def _():
        pltpu.make_async_copy(from_a, got, got_sem).start()

    fetch_columns(table, mine, field, held, held_sem, 0)

    def intensity_copies(j):
        return [
            pltpu.make_async_copy(
                intensity.at[j, :, pl.ds(part * LANES, LANES)], measured.at[j, part], int_sem.at[j, part]
            )
            for part in range(2)
        ]

    for j in range(CAP):

        @pl.when(jnp.logical_and(is_a, table[FIELDS * j] == AT_A))
        def _():
            for copy in intensity_copies(j):
                copy.start()

    for plane in range(2):
        for part in range(2):
            cut = probe[plane, :, part * LANES : (part + 1) * LANES]
            twice[2 * plane + part, :WIN] = cut
            twice[2 * plane + part, WIN:] = cut
    found = jnp.int32(0)
    for j in range(CAP):
        chosen[j] = 0
    for j in range(CAP):
        state = table[FIELDS * j]

        @pl.when(state == mine)
        def _():
            chosen[found] = j

        found = found + (state == mine).astype(jnp.int32)
    pltpu.make_async_copy(from_b, got, got_sem).wait()
    sublane = lax.broadcasted_iota(jnp.int32, (SUB, LANES), 0)

    def load(m, j):
        _, row, col, start, _ = slot_of(table, j)
        columns, starts, shift = near_columns(col)
        low = row // SUB
        high = (row + SUB - 1) // SUB
        base = jnp.where(is_a, start, start - low)

        def own_groups(group, carry):
            rows = pl.ds(pl.multiple_of(group * SUB, SUB), SUB)
            for plane in range(4):
                lf, rt = load_group(held.at[j], plane, group, starts, shift)
                tile[m, plane, rows, :LANES] = lf
                tile[m, plane, rows, LANES:] = rt
            return carry

        def their_groups(group, carry):
            rows = pl.ds(pl.multiple_of(group * SUB, SUB), SUB)
            for plane in range(4):
                tile[m, plane, rows, :] = got[base + group, plane]
            return carry

        lax.fori_loop(jnp.where(is_a, 0, low), jnp.where(is_a, high, GROUPS), their_groups, 0)
        lax.fori_loop(jnp.where(is_a, high, 0), jnp.where(is_a, GROUPS, low), own_groups, 0)

        @pl.when(low < high)
        def _():
            own = (low * SUB + sublane < row).astype(jnp.int32) == jnp.where(is_a, 0, 1)
            rows = pl.ds(pl.multiple_of(low * SUB, SUB), SUB)
            for plane in range(4):
                lf, rt = load_group(held.at[j], plane, low, starts, shift)
                tile[m, plane, rows, :LANES] = jnp.where(own, lf, tile[m, plane, rows, :LANES])
                tile[m, plane, rows, LANES:] = jnp.where(own, rt, tile[m, plane, rows, LANES:])

        @pl.when(jnp.logical_not(is_a))
        def _():
            after = start + GROUPS - low

            def unpack(group, carry):
                for plane in range(4):
                    rows = pl.ds(pl.multiple_of((group * 4 + plane) * SUB, SUB), SUB)
                    measured[j, 0, rows, :] = got[after + group, plane, :, :LANES]
                    measured[j, 1, rows, :] = got[after + group, plane, :, LANES:]
                return carry

            lax.fori_loop(0, INT_GROUPS, unpack, 0)

        for plane in range(2):
            parts = [twice[2 * plane + part, pl.ds(WIN - row, WIN), :] for part in range(2)]
            beam[m, plane] = pltpu.roll(jnp.concatenate(parts, axis=1), shift, 1)

    def arrive(j):
        columns, _, _ = near_columns(table[FIELDS * j + 2])
        pltpu.make_async_copy(field.at[:, :, columns], held.at[j], held_sem.at[j]).wait()

        @pl.when(is_a)
        def _():
            for copy in intensity_copies(j):
                copy.wait()

    def store_rows(m, e, o):
        work[m, 0, :HALF], work[m, 1, :HALF] = e[:HALF], e[HALF:]
        work[m, 0, HALF:], work[m, 1, HALF:] = o[:HALF], o[HALF:]

    def middle(pointwise, slots=None):
        for half in range(2):
            rows = pl.ds(half * HALF, HALF)
            for m in range(2):
                re, im = lanes_forward(work[m, 0, rows, :], work[m, 1, rows, :], forms)
                re, im = pointwise(m, half, rows, re, im, slots)
                re, im = lanes_inverse(re, im, forms)
                work[m, 0, rows, :], work[m, 1, rows, :] = re, im

    def rows_back(m):
        u, v = rows_inverse(work[m, 0], work[m, 1], forms)
        return (
            jnp.concatenate([u[:HALF] + v[:HALF], u[:HALF] - v[:HALF]], axis=0),
            jnp.concatenate([u[HALF:] + v[HALF:], u[HALF:] - v[HALF:]], axis=0),
        )

    def propagate(m, half, rows, re, im, slots):
        return cmul(kernel[0, rows, :], kernel[1, rows, :], re, im)

    def propagate_back(m, half, rows, re, im, slots):
        return cmul_conj(kernel[0, rows, :], kernel[1, rows, :], re, im)

    def residual(m, half, rows, re, im, slots):
        every = pl.ds(half, HALF, stride=2)
        at = slots[m]
        rows_of = jnp.concatenate([measured[at, 0, every, :], measured[at, 1, every, :]], axis=1)
        high, low = split(rows_of)
        wanted = jnp.dot(high, shuffle[...], preferred_element_type=f32)
        wanted += jnp.dot(low, shuffle[...], preferred_element_type=f32)
        scale = re * re + im * im - wanted
        return scale * re, scale * im

    def tile_copy(m, j):
        return pltpu.make_async_copy(tile.at[m], tiles.at[j], tile_sem.at[m])

    def write(m, j):
        _, row, _, _, back = slot_of(table, j)
        low = row // SUB

        def send(out, offset):
            def body(group, carry):
                rows = pl.ds(pl.multiple_of(group * SUB, SUB), SUB)
                for plane in range(4):
                    out[offset + group, plane] = tile[m, plane, rows, :]
                return carry

            return body

        tile_copy(m, j).start()

        @pl.when(is_a)
        def _():
            lax.fori_loop(0, (row + SUB - 1) // SUB, send(back_a, back), 0)

        @pl.when(jnp.logical_not(is_a))
        def _():
            lax.fori_loop(low, GROUPS, send(back_b, back - low), 0)

    def pair(p, carry):
        two = 2 * p + 1 < found
        first = chosen[2 * p]
        second = jnp.where(two, chosen[jnp.minimum(2 * p + 1, CAP - 1)], first)

        @pl.when(p > 0)
        def _():
            tile_copy(0, chosen[2 * p - 2]).wait()
            tile_copy(1, chosen[2 * p - 1]).wait()

        arrive(first)

        @pl.when(two)
        def _():
            arrive(second)

        load(0, first)
        load(1, second)
        for m in range(2):
            re, im = cmul(beam[m, 0], beam[m, 1], tile[m, 0], tile[m, 1])
            store_rows(m, *rows_forward(re, im, forms))
        middle(propagate)
        for m in range(2):
            re, im = rows_back(m)
            entered[m, 0], entered[m, 1] = re, im
            re, im = cmul(re, im, tile[m, 2], tile[m, 3])
            store_rows(m, *rows_forward(re, im, forms))
        middle(residual, (first, second))
        for m in range(2):
            br, bi = rows_back(m)
            re, im = cmul_conj(tile[m, 2], tile[m, 3], br, bi)
            tile[m, 2], tile[m, 3] = cmul_conj(entered[m, 0], entered[m, 1], br, bi)
            store_rows(m, *rows_forward(re, im, forms))
        middle(propagate_back)
        for m in range(2):
            br, bi = rows_back(m)
            tile[m, 0], tile[m, 1] = cmul_conj(beam[m, 0], beam[m, 1], br, bi)
        write(0, first)

        @pl.when(two)
        def _():
            write(1, second)

        return carry

    lax.fori_loop(0, (found + 1) // 2, pair, 0)

    @pl.when(found > 0)
    def _():
        tile_copy(0, 0).wait()

    @pl.when(jnp.logical_and(found > 0, jnp.bitwise_and(found, 1) == 0))
    def _():
        tile_copy(1, 0).wait()


def add_back(role, table, got, total, planes):
    is_a = role[0] == 0
    theirs = jnp.where(is_a, AT_B, AT_A)
    for j in range(CAP):
        state, row, col, _, back = slot_of(table, j)

        @pl.when(state == theirs)
        def _():
            starts, shift = lane_blocks(col)
            low = row // SUB
            base = jnp.where(is_a, back - low, back)
            sublane = lax.broadcasted_iota(jnp.int32, (SUB, LANES), 0)

            def body(group, carry):
                below = (group * SUB + sublane < row).astype(jnp.int32)
                own = below == jnp.where(is_a, 0, 1)
                for plane in planes:
                    lf = jnp.where(own, got[base + group, plane, :, :LANES], 0.0)
                    rt = jnp.where(own, got[base + group, plane, :, LANES:], 0.0)
                    add_group(total, plane, group, starts, shift, lf, rt)
                return carry

            lax.fori_loop(jnp.where(is_a, low, 0), jnp.where(is_a, GROUPS, (row + SUB - 1) // SUB), body, 0)


def sum_kernel(
    role_in, table_in, role_out, table_out, in_back, tiles_in, tiles_out, total, got, tile, got_sem, tile_sem
):
    pltpu.make_async_copy(in_back, got, got_sem).start()
    sublane = lax.broadcasted_iota(jnp.int32, (SUB, LANES), 0)
    kinds = ((role_in, table_in, tiles_in), (role_out, table_out, tiles_out))
    for k, (role, table, tiles) in enumerate(kinds):
        mine = jnp.where(role[0] == 0, AT_A, AT_B)
        for j in range(CAP):

            @pl.when(table[FIELDS * j] == mine)
            def _():
                pltpu.make_async_copy(tiles.at[j], tile.at[k * CAP + j], tile_sem.at[k * CAP + j]).start()

    total[...] = jnp.zeros_like(total)
    pltpu.make_async_copy(in_back, got, got_sem).wait()
    add_back(role_in, table_in, got, total, range(4))
    for k, (role, table, tiles) in enumerate(kinds):
        is_a = role[0] == 0
        mine = jnp.where(is_a, AT_A, AT_B)
        for j in range(CAP):
            state, row, col, _, _ = slot_of(table, j)

            @pl.when(state == mine)
            def _():
                at = k * CAP + j
                pltpu.make_async_copy(tiles.at[j], tile.at[at], tile_sem.at[at]).wait()
                starts, shift = lane_blocks(col)
                low = row // SUB

                def body(group, carry):
                    below = (group * SUB + sublane < row).astype(jnp.int32)
                    own = below == jnp.where(is_a, 0, 1)
                    rows = pl.ds(pl.multiple_of(group * SUB, SUB), SUB)
                    for plane in range(4):
                        lf = jnp.where(own, tile[at, plane, rows, :LANES], 0.0)
                        rt = jnp.where(own, tile[at, plane, rows, LANES:], 0.0)
                        add_group(total, plane, group, starts, shift, lf, rt)
                    return carry

                lax.fori_loop(
                    jnp.where(is_a, low, 0), jnp.where(is_a, GROUPS, (row + SUB - 1) // SUB), body, 0
                )


def finish_kernel(role, table, total_in, out_a, out_b, grad, total, got, got_sem, out_sem):
    is_a = role[0] == 0

    @pl.when(is_a)
    def _():
        copy = pltpu.make_async_copy(out_b, got.at[pl.ds(0, CAP_BACK_B)], got_sem)
        copy.start()
        copy.wait()

    @pl.when(jnp.logical_not(is_a))
    def _():
        copy = pltpu.make_async_copy(out_a, got, got_sem)
        copy.start()
        copy.wait()

    for plane in range(4):
        total[plane] = total_in[plane]
        add_back(role, table, got, total, (plane,))
        pltpu.make_async_copy(total.at[plane], grad.at[plane], out_sem.at[plane]).start()
    for plane in range(4):
        pltpu.make_async_copy(total.at[plane], grad.at[plane], out_sem.at[plane]).wait()


def spec(space):
    return pl.BlockSpec(memory_space=space)


def vmem(mib):
    return pltpu.CompilerParams(vmem_limit_bytes=mib << 20)


def packed(groups):
    return jax.ShapeDtypeStruct((groups, 4, SUB, WIN), f32)


def run_slots(joint, role, table, field, intensity, probe, kernel, tables, from_b, from_a):
    backs = (CAP_BACK_A,) if joint else (CAP_BACK_A, CAP_BACK_B)
    return pl.pallas_call(
        functools.partial(slots_kernel, joint),
        out_shape=tuple(packed(n) for n in backs) + (jax.ShapeDtypeStruct((CAP, 4, WIN, WIN), f32),),
        in_specs=[spec(SM)] * 2 + [spec(pl.ANY)] * 2 + [spec(VM)] * 4 + [spec(pl.ANY)] * 2,
        out_specs=(spec(VM),) * len(backs) + (spec(pl.ANY),),
        scratch_shapes=[
            pltpu.VMEM((CAP, 4, WIN, WIDE), f32),
            pltpu.VMEM((CAP_FWD, 4, SUB, WIN), f32),
            pltpu.VMEM((2, 4, WIN, WIN), f32),
            pltpu.VMEM((CAP, 2, WIN, LANES), f32),
            pltpu.VMEM((4, 2 * WIN, LANES), f32),
            pltpu.VMEM((2, 2, WIN, WIN), f32),
            pltpu.VMEM((2, 2, WIN, WIN), f32),
            pltpu.VMEM((2, 2, WIN, WIN), f32),
            pltpu.SMEM((CAP,), jnp.int32),
            pltpu.SemaphoreType.DMA((CAP,)),
            pltpu.SemaphoreType.DMA((CAP, 2)),
            pltpu.SemaphoreType.DMA,
            pltpu.SemaphoreType.DMA((2,)),
        ],
        compiler_params=vmem(32),
    )(role, table, field, intensity, probe, kernel, *tables, from_b, from_a)


def shards(obj_field, probe_wave, prop_phase, win_offsets, live_counts, intensity):
    field = obj_field.reshape((4,) + obj_field.shape[2:])
    count = lax.axis_size("row")
    within = [(i, i + 1) for i in range(0, count - 1, 2)]
    across = [(i, i + 1) for i in range(1, count - 1, 2)]
    back = lambda pairs: [(b, a) for a, b in pairs]
    move = lambda x, pairs: lax.ppermute(x, "row", pairs)
    odd = jnp.bitwise_and(lax.axis_index("row"), 1)
    role_in = odd.reshape(1)
    role_out = (1 - odd).reshape(1)

    flag = odd.reshape(1)
    own = jnp.concatenate([win_offsets.reshape(-1), live_counts, jnp.zeros((INFO - 2 * CAP - 1,), jnp.int32)])
    maps = intensity.reshape(CAP, INT_GROUPS, 4, SUB, WIN)
    to_b, info = pl.pallas_call(
        pack_early_kernel,
        out_shape=(packed(CAP_FWD), jax.ShapeDtypeStruct((INFO,), jnp.int32)),
        in_specs=[spec(SM)] * 2 + [spec(pl.ANY)] * 2,
        out_specs=(spec(VM), spec(SM)),
        scratch_shapes=[
            pltpu.SMEM((CAP * FIELDS,), jnp.int32),
            pltpu.VMEM((CAP, 4, WIN, WIDE), f32),
            pltpu.SemaphoreType.DMA((CAP,)),
            pltpu.SemaphoreType.DMA((CAP,)),
        ],
        compiler_params=vmem(16),
    )(flag, own, field, maps)
    out_from_a = move(to_b, across)
    before = move(info, within + across)
    table = jax.ShapeDtypeStruct((CAP * FIELDS,), jnp.int32)
    to_a, inner, table_in, table_out = pl.pallas_call(
        pack_late_kernel,
        out_shape=(packed(CAP_FWD), packed(CAP_FWD), table, table),
        in_specs=[spec(SM)] * 3 + [spec(pl.ANY)] * 2,
        out_specs=(spec(VM), spec(VM), spec(SM), spec(SM)),
        scratch_shapes=[
            pltpu.VMEM((2 * CAP, 4, WIN, WIDE), f32),
            pltpu.SemaphoreType.DMA((2 * CAP,)),
            pltpu.SemaphoreType.DMA((CAP,)),
        ],
        compiler_params=vmem(24),
    )(flag, own, before, field, maps)
    out_from_b = move(to_a, back(across))
    in_from = move(inner, within + back(within))

    forms, shuffle = (jnp.asarray(t) for t in make_tables())
    kernel = pl.pallas_call(
        prepare_kernel,
        out_shape=jax.ShapeDtypeStruct((2, WIN, WIN), f32),
        in_specs=[spec(VM)] * 2,
        out_specs=spec(VM),
        scratch_shapes=[pltpu.VMEM((2, WIN, LANES), f32)],
        compiler_params=vmem(8),
    )(jnp.stack([jnp.cos(prop_phase), jnp.sin(prop_phase)]), shuffle)

    args = (field, intensity, probe_wave, kernel, (forms, shuffle))
    in_back, tiles_in = run_slots(True, role_in, table_in, *args, in_from, in_from)
    in_back = move(in_back, within + back(within))
    out_back_a, out_back_b, tiles_out = run_slots(False, role_out, table_out, *args, out_from_b, out_from_a)
    out_a = move(out_back_a, across)
    out_b = move(out_back_b, back(across))
    total = pl.pallas_call(
        sum_kernel,
        out_shape=jax.ShapeDtypeStruct(field.shape, f32),
        in_specs=[spec(SM)] * 4 + [spec(pl.ANY)] * 3,
        out_specs=spec(VM),
        scratch_shapes=[
            pltpu.VMEM((CAP_BACK_A, 4, SUB, WIN), f32),
            pltpu.VMEM((2 * CAP, 4, WIN, WIN), f32),
            pltpu.SemaphoreType.DMA,
            pltpu.SemaphoreType.DMA((2 * CAP,)),
        ],
        compiler_params=vmem(20),
    )(role_in, table_in, role_out, table_out, in_back, tiles_in, tiles_out)
    grad = pl.pallas_call(
        finish_kernel,
        out_shape=jax.ShapeDtypeStruct(field.shape, f32),
        in_specs=[spec(SM)] * 2 + [spec(VM)] + [spec(pl.ANY)] * 2,
        out_specs=spec(pl.ANY),
        scratch_shapes=[
            pltpu.VMEM(field.shape, f32),
            pltpu.VMEM((CAP_BACK_A, 4, SUB, WIN), f32),
            pltpu.SemaphoreType.DMA,
            pltpu.SemaphoreType.DMA((4,)),
        ],
        compiler_params=vmem(16),
    )(role_out, table_out, total, out_a, out_b)
    return grad.reshape(obj_field.shape)


def solution(mesh):
    in_specs = (
        P(None, None, ("groups", "row"), None),
        P("groups", None, None),
        P(),
        P(("groups", "row"), None),
        P(("groups", "row")),
        P(("groups", "row"), None, None),
    )
    out_specs = P(None, None, ("groups", "row"), None)
    return jax.shard_map(shards, mesh=mesh, in_specs=in_specs, out_specs=out_specs, check_vma=False)
```

```python
import functools

import jax
import jax.numpy as jnp
import numpy as np
from jax import lax
from jax.experimental import pallas as pl
from jax.experimental.pallas import tpu as pltpu
from jax.sharding import PartitionSpec as P

WIN = 256
HALF = WIN // 2
LANES = 128
SUB = 8
CAP = 4
GROUPS = WIN // SUB
INT_GROUPS = GROUPS // 4
CAP_FWD = 48
CAP_BACK_A = 48
CAP_BACK_B = 32
UNEVEN = 24
DEAD, AT_A, AT_B = 0, 1, 2
FIELDS = 8
f32 = jnp.float32
bf16 = jnp.bfloat16
VM = pltpu.MemorySpace.VMEM
SM = pltpu.MemorySpace.SMEM
HB = pltpu.MemorySpace.HBM
CHEAP = pl.CostEstimate(flops=1, transcendentals=0, bytes_accessed=1)


def real_tables():
    k = np.arange(HALF)[:, None]
    n = np.arange(HALF)[None, :]
    out = []
    for odd in (0, 1):
        angle = 2.0 * np.pi * (((2 * k + odd) * n) % WIN) / WIN
        c, s = np.cos(angle) / 16.0, np.sin(angle) / 16.0
        out.append(np.block([[c, s], [-s, c]]))
    return out


def high_low(table):
    high = table.astype(np.float32).astype(bf16)
    low = (table - high.astype(np.float64)).astype(np.float32).astype(bf16)
    return high, low


def make_tables():
    even, odd = real_tables()
    forms = np.stack([np.stack(high_low(m)) for m in (even, odd, even.T, odd.T)])
    order = np.concatenate([np.arange(0, WIN, 2), np.arange(1, WIN, 2)])
    shuffle = np.zeros((WIN, WIN), np.float32)
    shuffle[order, np.arange(WIN)] = 1.0
    return forms, shuffle.astype(bf16)


EVEN, ODD, EVEN_T, ODD_T = range(4)


def split(x):
    high = x.astype(bf16)
    return high, (x - high.astype(f32)).astype(bf16)


def left_mul(forms, which, x):
    high, low = split(x)
    t_high, t_low = forms[which, 0], forms[which, 1]
    wide = jnp.concatenate([t_high, t_low, t_high], axis=1)
    return jnp.dot(wide, jnp.concatenate([high, high, low], axis=0), preferred_element_type=f32)


def right_mul(x, forms, which):
    high, low = split(x)
    t_high, t_low = forms[which, 0], forms[which, 1]
    tall = jnp.concatenate([t_high, t_high, t_low], axis=0)
    return jnp.dot(jnp.concatenate([high, low, high], axis=1), tall, preferred_element_type=f32)


def rows_forward(re, im, forms):
    tr, br, ti, bi = re[:HALF], re[HALF:], im[:HALF], im[HALF:]
    e = left_mul(forms, EVEN, jnp.concatenate([tr + br, ti + bi], axis=0))
    o = left_mul(forms, ODD, jnp.concatenate([tr - br, ti - bi], axis=0))
    return e, o


def rows_inverse(re, im, forms):
    u = left_mul(forms, EVEN_T, jnp.concatenate([re[:HALF], im[:HALF]], axis=0))
    v = left_mul(forms, ODD_T, jnp.concatenate([re[HALF:], im[HALF:]], axis=0))
    return u, v


def lanes_forward(re, im, forms):
    lr, rr, li, ri = re[:, :HALF], re[:, HALF:], im[:, :HALF], im[:, HALF:]
    e = right_mul(jnp.concatenate([lr + rr, li + ri], axis=1), forms, EVEN_T)
    o = right_mul(jnp.concatenate([lr - rr, li - ri], axis=1), forms, ODD_T)
    return (
        jnp.concatenate([e[:, :HALF], o[:, :HALF]], axis=1),
        jnp.concatenate([e[:, HALF:], o[:, HALF:]], axis=1),
    )


def lanes_inverse(re, im, forms):
    u = right_mul(jnp.concatenate([re[:, :HALF], im[:, :HALF]], axis=1), forms, EVEN)
    v = right_mul(jnp.concatenate([re[:, HALF:], im[:, HALF:]], axis=1), forms, ODD)
    return (
        jnp.concatenate([u[:, :HALF] + v[:, :HALF], u[:, :HALF] - v[:, :HALF]], axis=1),
        jnp.concatenate([u[:, HALF:] + v[:, HALF:], u[:, HALF:] - v[:, HALF:]], axis=1),
    )


def cmul(ar, ai, br, bi):
    return ar * br - ai * bi, ar * bi + ai * br


def cmul_conj(ar, ai, br, bi):
    return ar * br + ai * bi, ar * bi - ai * br


INFO = 16


def decide(info, table):
    count = info[2 * CAP]
    rows = [jnp.bitwise_and(info[2 * j], WIN - 1) for j in range(CAP)]
    used = [(j < count).astype(jnp.int32) for j in range(CAP)]
    on_a = [used[j] * ((rows[j] + SUB - 1) // SUB) for j in range(CAP)]
    on_b = [used[j] * (GROUPS - rows[j] // SUB + INT_GROUPS) for j in range(CAP)]
    best, chosen = jnp.int32(10000), jnp.int32(0)
    for mask in range(1 << CAP):
        total_a = jnp.int32(0)
        total_b = jnp.int32(0)
        slots_a = jnp.int32(0)
        slots_b = jnp.int32(0)
        for j in range(CAP):
            if mask >> j & 1:
                total_b = total_b + on_b[j]
                slots_b = slots_b + used[j]
            else:
                total_a = total_a + on_a[j]
                slots_a = slots_a + used[j]
        cost = jnp.maximum(total_a, total_b)
        cost = cost + jnp.where(cost > CAP_FWD, 1000, 0)
        cost = cost + jnp.where(jnp.maximum(slots_a, slots_b) > 2, UNEVEN, 0)
        better = cost < best
        best = jnp.where(better, cost, best)
        chosen = jnp.where(better, mask, chosen)
    at_a = jnp.int32(0)
    at_b = jnp.int32(0)
    back = jnp.int32(0)
    for j in range(CAP):
        to_b = jnp.bitwise_and(chosen >> j, 1) * used[j]
        to_b = jnp.where(rows[j] == 0, 0, to_b)
        to_a = used[j] - to_b
        table[FIELDS * j] = to_a * AT_A + to_b * AT_B
        table[FIELDS * j + 1] = rows[j]
        table[FIELDS * j + 2] = info[2 * j + 1]
        table[FIELDS * j + 3] = jnp.where(to_b == 1, at_b, at_a)
        table[FIELDS * j + 4] = jnp.where(to_b == 1, back, at_a)
        at_a = at_a + to_a * on_a[j]
        at_b = at_b + to_b * on_b[j]
        back = back + to_b * (on_b[j] - INT_GROUPS)


def slot_of(table, j):
    base = FIELDS * j
    return table[base], table[base + 1], table[base + 2], table[base + 3], table[base + 4]


def lane_blocks(col):
    first = col // LANES
    starts = [jnp.minimum(first + k, 7) * LANES for k in range(3)]
    return [pl.multiple_of(start, LANES) for start in starts], jnp.bitwise_and(col, LANES - 1)


WIDE = 3 * LANES


def near_columns(col):
    first = jnp.minimum(col // LANES, 5)
    skip = col // LANES - first
    starts = [pl.multiple_of(jnp.minimum(skip + k, 2) * LANES, LANES) for k in range(3)]
    return pl.ds(pl.multiple_of(first * LANES, LANES), WIDE), starts, jnp.bitwise_and(col, LANES - 1)


def lane_iota():
    return lax.broadcasted_iota(jnp.int32, (SUB, LANES), 1)


def load_group(field, plane, group, starts, shift):
    rows = pl.ds(pl.multiple_of(group * SUB, SUB), SUB)
    first = field[plane, rows, pl.ds(starts[0], LANES)]
    second = field[plane, rows, pl.ds(starts[1], LANES)]
    third = field[plane, rows, pl.ds(starts[2], LANES)]
    return jnp.where(lane_iota() >= shift, first, third), second


def add_group(total, plane, group, starts, shift, left, right):
    rows = pl.ds(pl.multiple_of(group * SUB, SUB), SUB)
    inside = lane_iota() >= shift
    total[plane, rows, pl.ds(starts[0], LANES)] += jnp.where(inside, left, 0.0)
    total[plane, rows, pl.ds(starts[1], LANES)] += right
    total[plane, rows, pl.ds(starts[2], LANES)] += jnp.where(inside, 0.0, left)


def fetch_columns(table, wanted, field, held, sem, base):
    for j in range(CAP):

        @pl.when(table[FIELDS * j] == wanted)
        def _():
            columns, _, _ = near_columns(table[FIELDS * j + 2])
            pltpu.make_async_copy(field.at[:, :, columns], held.at[base + j], sem.at[base + j]).start()


def copy_groups(held, out, at, offset, low, high, starts, shift):
    def body(group, carry):
        for plane in range(4):
            left, right = load_group(held.at[at], plane, group, starts, shift)
            out[offset + group, plane, :, :LANES] = left
            out[offset + group, plane, :, LANES:] = right
        return carry

    lax.fori_loop(low, high, body, 0)


def pack_to_b(table, field, intensity, out, held, sem, int_sem, base):
    def intensity_copy(j):
        _, row, _, start, _ = slot_of(table, j)
        after = start + GROUPS - row // SUB
        return pltpu.make_async_copy(intensity.at[j], out.at[pl.ds(after, INT_GROUPS)], int_sem.at[j])

    for j in range(CAP):

        @pl.when(table[FIELDS * j] == AT_B)
        def _():
            intensity_copy(j).start()

    for j in range(CAP):
        state, row, col, start, _ = slot_of(table, j)

        @pl.when(state == AT_B)
        def _():
            columns, starts, shift = near_columns(col)
            at = base + j
            pltpu.make_async_copy(field.at[:, :, columns], held.at[at], sem.at[at]).wait()
            copy_groups(held, out, at, start - row // SUB, row // SUB, GROUPS, starts, shift)
            intensity_copy(j).wait()


def pack_to_a(table, field, out, held, sem, base):
    for j in range(CAP):
        state, row, col, start, _ = slot_of(table, j)

        @pl.when(state == AT_A)
        def _():
            columns, starts, shift = near_columns(col)
            at = base + j
            pltpu.make_async_copy(field.at[:, :, columns], held.at[at], sem.at[at]).wait()
            copy_groups(held, out, at, start, 0, (row + SUB - 1) // SUB, starts, shift)


def pack_early_kernel(odd, own, field, intensity, out, info, table, held, sem, int_sem):
    for j in range(INFO):
        info[j] = own[j]

    @pl.when(odd[0] == 1)
    def _():
        decide(own, table)
        fetch_columns(table, AT_B, field, held, sem, 0)
        pack_to_b(table, field, intensity, out, held, sem, int_sem, 0)


def pack_late_kernel(odd, own, before, field, intensity, out, inner, table_in, table_out, held, sem, int_sem):
    @pl.when(odd[0] == 0)
    def _():
        decide(before, table_out)
        fetch_columns(table_out, AT_A, field, held, sem, 0)
        decide(own, table_in)
        fetch_columns(table_in, AT_B, field, held, sem, CAP)
        pack_to_a(table_out, field, out, held, sem, 0)
        pack_to_b(table_in, field, intensity, inner, held, sem, int_sem, CAP)

    @pl.when(odd[0] == 1)
    def _():
        decide(before, table_in)
        fetch_columns(table_in, AT_A, field, held, sem, 0)
        decide(own, table_out)
        pack_to_a(table_in, field, inner, held, sem, 0)


def prepare_kernel(phases, shuffle, out, halves):
    for plane in range(2):
        halves[0] = phases[plane, :, :LANES]
        halves[1] = phases[plane, :, LANES:]
        for part in range(2):
            every = pl.ds(part, HALF, stride=2)
            x = jnp.concatenate([halves[0, every, :], halves[1, every, :]], axis=1)
            high = x.astype(bf16)
            rest = x - high.astype(f32)
            middle, low = split(rest)
            total = jnp.dot(high, shuffle[...], preferred_element_type=f32)
            total += jnp.dot(middle, shuffle[...], preferred_element_type=f32)
            total += jnp.dot(low, shuffle[...], preferred_element_type=f32)
            out[plane, part * HALF : (part + 1) * HALF, :] = total


def slots_kernel(joint, role, table, field, intensity, probe, kernel, forms, shuffle, from_b, from_a, after, *rest):
    del after
    back_a, back_b = rest[0], rest[0 if joint else 1]
    tiles, held, got, tile, measured, twice, beam, work, entered, chosen = rest[1 if joint else 2 : -4]
    held_sem, int_sem, got_sem, tile_sem = rest[-4:]
    is_a = role[0] == 0
    mine = jnp.where(is_a, AT_A, AT_B)

    @pl.when(is_a)
    def _():
        pltpu.make_async_copy(from_b, got, got_sem).start()

    @pl.when(jnp.logical_not(is_a))
    def _():
        pltpu.make_async_copy(from_a, got, got_sem).start()

    fetch_columns(table, mine, field, held, held_sem, 0)

    def intensity_copies(j):
        return [
            pltpu.make_async_copy(
                intensity.at[j, :, pl.ds(part * LANES, LANES)], measured.at[j, part], int_sem.at[j, part]
            )
            for part in range(2)
        ]

    for j in range(CAP):

        @pl.when(jnp.logical_and(is_a, table[FIELDS * j] == AT_A))
        def _():
            for copy in intensity_copies(j):
                copy.start()

    for plane in range(2):
        for part in range(2):
            cut = probe[plane, :, part * LANES : (part + 1) * LANES]
            twice[2 * plane + part, :WIN] = cut
            twice[2 * plane + part, WIN:] = cut
    found = jnp.int32(0)
    for j in range(CAP):
        chosen[j] = 0
    for j in range(CAP):
        state = table[FIELDS * j]

        @pl.when(state == mine)
        def _():
            chosen[found] = j

        found = found + (state == mine).astype(jnp.int32)
    pltpu.make_async_copy(from_b, got, got_sem).wait()
    sublane = lax.broadcasted_iota(jnp.int32, (SUB, LANES), 0)

    def load(m, j):
        _, row, col, start, _ = slot_of(table, j)
        columns, starts, shift = near_columns(col)
        low = row // SUB
        high = (row + SUB - 1) // SUB
        base = jnp.where(is_a, start, start - low)

        def own_groups(group, carry):
            rows = pl.ds(pl.multiple_of(group * SUB, SUB), SUB)
            for plane in range(4):
                lf, rt = load_group(held.at[j], plane, group, starts, shift)
                tile[m, plane, rows, :LANES] = lf
                tile[m, plane, rows, LANES:] = rt
            return carry

        def their_groups(group, carry):
            rows = pl.ds(pl.multiple_of(group * SUB, SUB), SUB)
            for plane in range(4):
                tile[m, plane, rows, :] = got[base + group, plane]
            return carry

        lax.fori_loop(jnp.where(is_a, 0, low), jnp.where(is_a, high, GROUPS), their_groups, 0)
        lax.fori_loop(jnp.where(is_a, high, 0), jnp.where(is_a, GROUPS, low), own_groups, 0)

        @pl.when(low < high)
        def _():
            own = (low * SUB + sublane < row).astype(jnp.int32) == jnp.where(is_a, 0, 1)
            rows = pl.ds(pl.multiple_of(low * SUB, SUB), SUB)
            for plane in range(4):
                lf, rt = load_group(held.at[j], plane, low, starts, shift)
                tile[m, plane, rows, :LANES] = jnp.where(own, lf, tile[m, plane, rows, :LANES])
                tile[m, plane, rows, LANES:] = jnp.where(own, rt, tile[m, plane, rows, LANES:])

        @pl.when(jnp.logical_not(is_a))
        def _():
            after = start + GROUPS - low

            def unpack(group, carry):
                for plane in range(4):
                    rows = pl.ds(pl.multiple_of((group * 4 + plane) * SUB, SUB), SUB)
                    measured[j, 0, rows, :] = got[after + group, plane, :, :LANES]
                    measured[j, 1, rows, :] = got[after + group, plane, :, LANES:]
                return carry

            lax.fori_loop(0, INT_GROUPS, unpack, 0)

        for plane in range(2):
            parts = [twice[2 * plane + part, pl.ds(WIN - row, WIN), :] for part in range(2)]
            beam[m, plane] = pltpu.roll(jnp.concatenate(parts, axis=1), shift, 1)

    def arrive(j):
        columns, _, _ = near_columns(table[FIELDS * j + 2])
        pltpu.make_async_copy(field.at[:, :, columns], held.at[j], held_sem.at[j]).wait()

        @pl.when(is_a)
        def _():
            for copy in intensity_copies(j):
                copy.wait()

    def store_rows(m, e, o):
        work[m, 0, :HALF], work[m, 1, :HALF] = e[:HALF], e[HALF:]
        work[m, 0, HALF:], work[m, 1, HALF:] = o[:HALF], o[HALF:]

    def middle(pointwise, slots=None):
        for half in range(2):
            rows = pl.ds(half * HALF, HALF)
            for m in range(2):
                re, im = lanes_forward(work[m, 0, rows, :], work[m, 1, rows, :], forms)
                re, im = pointwise(m, half, rows, re, im, slots)
                re, im = lanes_inverse(re, im, forms)
                work[m, 0, rows, :], work[m, 1, rows, :] = re, im

    def rows_back(m):
        u, v = rows_inverse(work[m, 0], work[m, 1], forms)
        return (
            jnp.concatenate([u[:HALF] + v[:HALF], u[:HALF] - v[:HALF]], axis=0),
            jnp.concatenate([u[HALF:] + v[HALF:], u[HALF:] - v[HALF:]], axis=0),
        )

    def propagate(m, half, rows, re, im, slots):
        return cmul(kernel[0, rows, :], kernel[1, rows, :], re, im)

    def propagate_back(m, half, rows, re, im, slots):
        return cmul_conj(kernel[0, rows, :], kernel[1, rows, :], re, im)

    def residual(m, half, rows, re, im, slots):
        every = pl.ds(half, HALF, stride=2)
        at = slots[m]
        rows_of = jnp.concatenate([measured[at, 0, every, :], measured[at, 1, every, :]], axis=1)
        high, low = split(rows_of)
        wanted = jnp.dot(high, shuffle[...], preferred_element_type=f32)
        wanted += jnp.dot(low, shuffle[...], preferred_element_type=f32)
        scale = re * re + im * im - wanted
        return scale * re, scale * im

    def tile_copy(m, j):
        return pltpu.make_async_copy(tile.at[m], tiles.at[j], tile_sem.at[m])

    def write(m, j):
        _, row, _, _, back = slot_of(table, j)
        low = row // SUB

        def send(out, offset):
            def body(group, carry):
                rows = pl.ds(pl.multiple_of(group * SUB, SUB), SUB)
                for plane in range(4):
                    out[offset + group, plane] = tile[m, plane, rows, :]
                return carry

            return body

        tile_copy(m, j).start()

        @pl.when(is_a)
        def _():
            lax.fori_loop(0, (row + SUB - 1) // SUB, send(back_a, back), 0)

        @pl.when(jnp.logical_not(is_a))
        def _():
            lax.fori_loop(low, GROUPS, send(back_b, back - low), 0)

    def pair(p, carry):
        two = 2 * p + 1 < found
        first = chosen[2 * p]
        second = jnp.where(two, chosen[jnp.minimum(2 * p + 1, CAP - 1)], first)

        @pl.when(p > 0)
        def _():
            tile_copy(0, chosen[2 * p - 2]).wait()
            tile_copy(1, chosen[2 * p - 1]).wait()

        arrive(first)

        @pl.when(two)
        def _():
            arrive(second)

        load(0, first)
        load(1, second)
        for m in range(2):
            re, im = cmul(beam[m, 0], beam[m, 1], tile[m, 0], tile[m, 1])
            store_rows(m, *rows_forward(re, im, forms))
        middle(propagate)
        for m in range(2):
            re, im = rows_back(m)
            entered[m, 0], entered[m, 1] = re, im
            re, im = cmul(re, im, tile[m, 2], tile[m, 3])
            store_rows(m, *rows_forward(re, im, forms))
        middle(residual, (first, second))
        for m in range(2):
            br, bi = rows_back(m)
            re, im = cmul_conj(tile[m, 2], tile[m, 3], br, bi)
            tile[m, 2], tile[m, 3] = cmul_conj(entered[m, 0], entered[m, 1], br, bi)
            store_rows(m, *rows_forward(re, im, forms))
        middle(propagate_back)
        for m in range(2):
            br, bi = rows_back(m)
            tile[m, 0], tile[m, 1] = cmul_conj(beam[m, 0], beam[m, 1], br, bi)
        write(0, first)

        @pl.when(two)
        def _():
            write(1, second)

        return carry

    lax.fori_loop(0, (found + 1) // 2, pair, 0)

    @pl.when(found > 0)
    def _():
        tile_copy(0, 0).wait()

    @pl.when(jnp.logical_and(found > 0, jnp.bitwise_and(found, 1) == 0))
    def _():
        tile_copy(1, 0).wait()


def add_back(role, table, got, total, planes):
    is_a = role[0] == 0
    theirs = jnp.where(is_a, AT_B, AT_A)
    for j in range(CAP):
        state, row, col, _, back = slot_of(table, j)

        @pl.when(state == theirs)
        def _():
            starts, shift = lane_blocks(col)
            low = row // SUB
            base = jnp.where(is_a, back - low, back)
            sublane = lax.broadcasted_iota(jnp.int32, (SUB, LANES), 0)

            def body(group, carry):
                below = (group * SUB + sublane < row).astype(jnp.int32)
                own = below == jnp.where(is_a, 0, 1)
                for plane in planes:
                    lf = jnp.where(own, got[base + group, plane, :, :LANES], 0.0)
                    rt = jnp.where(own, got[base + group, plane, :, LANES:], 0.0)
                    add_group(total, plane, group, starts, shift, lf, rt)
                return carry

            lax.fori_loop(jnp.where(is_a, low, 0), jnp.where(is_a, GROUPS, (row + SUB - 1) // SUB), body, 0)


def sum_kernel(
    role_in, table_in, role_out, table_out, in_back, tiles_in, tiles_out, total, got, tile, got_sem, tile_sem
):
    pltpu.make_async_copy(in_back, got, got_sem).start()
    sublane = lax.broadcasted_iota(jnp.int32, (SUB, LANES), 0)
    kinds = ((role_in, table_in, tiles_in), (role_out, table_out, tiles_out))
    for k, (role, table, tiles) in enumerate(kinds):
        mine = jnp.where(role[0] == 0, AT_A, AT_B)
        for j in range(CAP):

            @pl.when(table[FIELDS * j] == mine)
            def _():
                pltpu.make_async_copy(tiles.at[j], tile.at[k * CAP + j], tile_sem.at[k * CAP + j]).start()

    total[...] = jnp.zeros_like(total)
    pltpu.make_async_copy(in_back, got, got_sem).wait()
    add_back(role_in, table_in, got, total, range(4))
    for k, (role, table, tiles) in enumerate(kinds):
        is_a = role[0] == 0
        mine = jnp.where(is_a, AT_A, AT_B)
        for j in range(CAP):
            state, row, col, _, _ = slot_of(table, j)

            @pl.when(state == mine)
            def _():
                at = k * CAP + j
                pltpu.make_async_copy(tiles.at[j], tile.at[at], tile_sem.at[at]).wait()
                starts, shift = lane_blocks(col)
                low = row // SUB

                def body(group, carry):
                    below = (group * SUB + sublane < row).astype(jnp.int32)
                    own = below == jnp.where(is_a, 0, 1)
                    rows = pl.ds(pl.multiple_of(group * SUB, SUB), SUB)
                    for plane in range(4):
                        lf = jnp.where(own, tile[at, plane, rows, :LANES], 0.0)
                        rt = jnp.where(own, tile[at, plane, rows, LANES:], 0.0)
                        add_group(total, plane, group, starts, shift, lf, rt)
                    return carry

                lax.fori_loop(
                    jnp.where(is_a, low, 0), jnp.where(is_a, GROUPS, (row + SUB - 1) // SUB), body, 0
                )


def finish_kernel(role, table, total_in, out_a, out_b, grad, total, got, got_sem, out_sem):
    is_a = role[0] == 0

    @pl.when(is_a)
    def _():
        copy = pltpu.make_async_copy(out_b, got.at[pl.ds(0, CAP_BACK_B)], got_sem)
        copy.start()
        copy.wait()

    @pl.when(jnp.logical_not(is_a))
    def _():
        copy = pltpu.make_async_copy(out_a, got, got_sem)
        copy.start()
        copy.wait()

    for plane in range(4):
        total[plane] = total_in[plane]
        add_back(role, table, got, total, (plane,))
        pltpu.make_async_copy(total.at[plane], grad.at[plane], out_sem.at[plane]).start()
    for plane in range(4):
        pltpu.make_async_copy(total.at[plane], grad.at[plane], out_sem.at[plane]).wait()


def spec(space):
    return pl.BlockSpec(memory_space=space)


def vmem(mib):
    return pltpu.CompilerParams(vmem_limit_bytes=mib << 20)


def packed(groups):
    return jax.ShapeDtypeStruct((groups, 4, SUB, WIN), f32)


def run_slots(joint, role, table, field, intensity, probe, kernel, tables, from_b, from_a, after):
    backs = (CAP_BACK_A,) if joint else (CAP_BACK_A, CAP_BACK_B)
    return pl.pallas_call(
        functools.partial(slots_kernel, joint),
        out_shape=tuple(packed(n) for n in backs) + (jax.ShapeDtypeStruct((CAP, 4, WIN, WIN), f32),),
        in_specs=[spec(SM)] * 2 + [spec(HB)] * 2 + [spec(VM)] * 4 + [spec(pl.ANY)] * 3,
        out_specs=(spec(VM),) * len(backs) + (spec(HB),),
        scratch_shapes=[
            pltpu.VMEM((CAP, 4, WIN, WIDE), f32),
            pltpu.VMEM((CAP_FWD, 4, SUB, WIN), f32),
            pltpu.VMEM((2, 4, WIN, WIN), f32),
            pltpu.VMEM((CAP, 2, WIN, LANES), f32),
            pltpu.VMEM((4, 2 * WIN, LANES), f32),
            pltpu.VMEM((2, 2, WIN, WIN), f32),
            pltpu.VMEM((2, 2, WIN, WIN), f32),
            pltpu.VMEM((2, 2, WIN, WIN), f32),
            pltpu.SMEM((CAP,), jnp.int32),
            pltpu.SemaphoreType.DMA((CAP,)),
            pltpu.SemaphoreType.DMA((CAP, 2)),
            pltpu.SemaphoreType.DMA,
            pltpu.SemaphoreType.DMA((2,)),
        ],
        cost_estimate=CHEAP,
        compiler_params=vmem(56),
    )(role, table, field, intensity, probe, kernel, *tables, from_b, from_a, after)


def shards(obj_field, probe_wave, prop_phase, win_offsets, live_counts, intensity):
    field = obj_field.reshape((4,) + obj_field.shape[2:])
    count = lax.axis_size("row")
    within = [(i, i + 1) for i in range(0, count - 1, 2)]
    across = [(i, i + 1) for i in range(1, count - 1, 2)]
    back = lambda pairs: [(b, a) for a, b in pairs]
    move = lambda x, pairs: lax.ppermute(x, "row", pairs)
    odd = jnp.bitwise_and(lax.axis_index("row"), 1)
    role_in = odd.reshape(1)
    role_out = (1 - odd).reshape(1)

    flag = odd.reshape(1)
    own = jnp.concatenate([win_offsets.reshape(-1), live_counts, jnp.zeros((INFO - 2 * CAP - 1,), jnp.int32)])
    maps = intensity.reshape(CAP, INT_GROUPS, 4, SUB, WIN)
    to_b, info = pl.pallas_call(
        pack_early_kernel,
        out_shape=(packed(CAP_FWD), jax.ShapeDtypeStruct((INFO,), jnp.int32)),
        in_specs=[spec(SM)] * 2 + [spec(HB)] * 2,
        out_specs=(spec(VM), spec(SM)),
        scratch_shapes=[
            pltpu.SMEM((CAP * FIELDS,), jnp.int32),
            pltpu.VMEM((CAP, 4, WIN, WIDE), f32),
            pltpu.SemaphoreType.DMA((CAP,)),
            pltpu.SemaphoreType.DMA((CAP,)),
        ],
        cost_estimate=CHEAP,
        compiler_params=vmem(58),
    )(flag, own, field, maps)
    out_from_a = move(to_b, across)
    before = move(info, within + across)
    table = jax.ShapeDtypeStruct((CAP * FIELDS,), jnp.int32)
    to_a, inner, table_in, table_out = pl.pallas_call(
        pack_late_kernel,
        out_shape=(packed(CAP_FWD), packed(CAP_FWD), table, table),
        in_specs=[spec(SM)] * 3 + [spec(HB)] * 2,
        out_specs=(spec(VM), spec(VM), spec(SM), spec(SM)),
        scratch_shapes=[
            pltpu.VMEM((2 * CAP, 4, WIN, WIDE), f32),
            pltpu.SemaphoreType.DMA((2 * CAP,)),
            pltpu.SemaphoreType.DMA((CAP,)),
        ],
        cost_estimate=CHEAP,
        compiler_params=vmem(58),
    )(flag, own, before, field, maps)
    out_from_b = move(to_a, back(across))
    in_from = move(inner, within + back(within))

    forms, shuffle = (jnp.asarray(t) for t in make_tables())
    kernel = pl.pallas_call(
        prepare_kernel,
        out_shape=jax.ShapeDtypeStruct((2, WIN, WIN), f32),
        in_specs=[spec(VM)] * 2,
        out_specs=spec(VM),
        scratch_shapes=[pltpu.VMEM((2, WIN, LANES), f32)],
        cost_estimate=CHEAP,
        compiler_params=vmem(8),
    )(jnp.stack([jnp.cos(prop_phase), jnp.sin(prop_phase)]), shuffle)

    args = (field, intensity, probe_wave, kernel, (forms, shuffle))
    in_back, tiles_in = run_slots(True, role_in, table_in, *args, in_from, in_from, out_from_a)
    in_back = move(in_back, within + back(within))
    out_back_a, out_back_b, tiles_out = run_slots(False, role_out, table_out, *args, out_from_b, out_from_a, out_from_a)
    out_a = move(out_back_a, across)
    out_b = move(out_back_b, back(across))
    total = pl.pallas_call(
        sum_kernel,
        out_shape=jax.ShapeDtypeStruct(field.shape, f32),
        in_specs=[spec(SM)] * 4 + [spec(pl.ANY)] * 3,
        out_specs=spec(VM),
        scratch_shapes=[
            pltpu.VMEM((CAP_BACK_A, 4, SUB, WIN), f32),
            pltpu.VMEM((2 * CAP, 4, WIN, WIN), f32),
            pltpu.SemaphoreType.DMA,
            pltpu.SemaphoreType.DMA((2 * CAP,)),
        ],
        cost_estimate=CHEAP,
        compiler_params=vmem(20),
    )(role_in, table_in, role_out, table_out, in_back, tiles_in, tiles_out)
    grad = pl.pallas_call(
        finish_kernel,
        out_shape=jax.ShapeDtypeStruct(field.shape, f32),
        in_specs=[spec(SM)] * 2 + [spec(VM)] + [spec(pl.ANY)] * 2,
        out_specs=spec(HB),
        scratch_shapes=[
            pltpu.VMEM(field.shape, f32),
            pltpu.VMEM((CAP_BACK_A, 4, SUB, WIN), f32),
            pltpu.SemaphoreType.DMA,
            pltpu.SemaphoreType.DMA((4,)),
        ],
        cost_estimate=CHEAP,
        compiler_params=vmem(16),
    )(role_out, table_out, total, out_a, out_b)
    return grad.reshape(obj_field.shape)


def solution(mesh):
    in_specs = (
        P(None, None, ("groups", "row"), None),
        P("groups", None, None),
        P(),
        P(("groups", "row"), None),
        P(("groups", "row")),
        P(("groups", "row"), None, None),
    )
    out_specs = P(None, None, ("groups", "row"), None)
    return jax.shard_map(shards, mesh=mesh, in_specs=in_specs, out_specs=out_specs, check_vma=False)
```

```python
import functools

import jax
import jax.numpy as jnp
import numpy as np
from jax import lax
from jax.experimental import pallas as pl
from jax.experimental.pallas import tpu as pltpu
from jax.sharding import PartitionSpec as P

WIN = 256
HALF = WIN // 2
LANES = 128
SUB = 8
CAP = 4
GROUPS = WIN // SUB
INT_GROUPS = GROUPS // 4
CAP_FWD = 48
CAP_BACK_A = 48
CAP_BACK_B = 32
UNEVEN = 24
DEAD, AT_A, AT_B = 0, 1, 2
FIELDS = 8
f32 = jnp.float32
bf16 = jnp.bfloat16
VM = pltpu.MemorySpace.VMEM
SM = pltpu.MemorySpace.SMEM
HB = pltpu.MemorySpace.HBM
CHEAP = pl.CostEstimate(flops=1, transcendentals=0, bytes_accessed=1)


def real_tables():
    k = np.arange(HALF)[:, None]
    n = np.arange(HALF)[None, :]
    out = []
    for odd in (0, 1):
        angle = 2.0 * np.pi * (((2 * k + odd) * n) % WIN) / WIN
        c, s = np.cos(angle) / 16.0, np.sin(angle) / 16.0
        out.append(np.block([[c, s], [-s, c]]))
    return out


def high_low(table):
    high = table.astype(np.float32).astype(bf16)
    low = (table - high.astype(np.float64)).astype(np.float32).astype(bf16)
    return high, low


def make_tables():
    even, odd = real_tables()
    forms = np.stack([np.stack(high_low(m)) for m in (even, odd, even.T, odd.T)])
    order = np.concatenate([np.arange(0, WIN, 2), np.arange(1, WIN, 2)])
    shuffle = np.zeros((WIN, WIN), np.float32)
    shuffle[order, np.arange(WIN)] = 1.0
    return forms, shuffle.astype(bf16)


EVEN, ODD, EVEN_T, ODD_T = range(4)


def split(x):
    high = x.astype(bf16)
    return high, (x - high.astype(f32)).astype(bf16)


def left_mul(forms, which, x):
    high, low = split(x)
    t_high, t_low = forms[which, 0], forms[which, 1]
    wide = jnp.concatenate([t_high, t_low, t_high], axis=1)
    return jnp.dot(wide, jnp.concatenate([high, high, low], axis=0), preferred_element_type=f32)


def right_mul(x, forms, which):
    high, low = split(x)
    t_high, t_low = forms[which, 0], forms[which, 1]
    tall = jnp.concatenate([t_high, t_high, t_low], axis=0)
    return jnp.dot(jnp.concatenate([high, low, high], axis=1), tall, preferred_element_type=f32)


def rows_forward(re, im, forms):
    tr, br, ti, bi = re[:HALF], re[HALF:], im[:HALF], im[HALF:]
    e = left_mul(forms, EVEN, jnp.concatenate([tr + br, ti + bi], axis=0))
    o = left_mul(forms, ODD, jnp.concatenate([tr - br, ti - bi], axis=0))
    return e, o


def rows_inverse(re, im, forms):
    u = left_mul(forms, EVEN_T, jnp.concatenate([re[:HALF], im[:HALF]], axis=0))
    v = left_mul(forms, ODD_T, jnp.concatenate([re[HALF:], im[HALF:]], axis=0))
    return u, v


def lanes_forward(re, im, forms):
    lr, rr, li, ri = re[:, :HALF], re[:, HALF:], im[:, :HALF], im[:, HALF:]
    e = right_mul(jnp.concatenate([lr + rr, li + ri], axis=1), forms, EVEN_T)
    o = right_mul(jnp.concatenate([lr - rr, li - ri], axis=1), forms, ODD_T)
    return (
        jnp.concatenate([e[:, :HALF], o[:, :HALF]], axis=1),
        jnp.concatenate([e[:, HALF:], o[:, HALF:]], axis=1),
    )


def lanes_inverse(re, im, forms):
    u = right_mul(jnp.concatenate([re[:, :HALF], im[:, :HALF]], axis=1), forms, EVEN)
    v = right_mul(jnp.concatenate([re[:, HALF:], im[:, HALF:]], axis=1), forms, ODD)
    return (
        jnp.concatenate([u[:, :HALF] + v[:, :HALF], u[:, :HALF] - v[:, :HALF]], axis=1),
        jnp.concatenate([u[:, HALF:] + v[:, HALF:], u[:, HALF:] - v[:, HALF:]], axis=1),
    )


def cmul(ar, ai, br, bi):
    return ar * br - ai * bi, ar * bi + ai * br


def cmul_conj(ar, ai, br, bi):
    return ar * br + ai * bi, ar * bi - ai * br


INFO = 16


def decide(info, table):
    count = info[2 * CAP]
    rows = [jnp.bitwise_and(info[2 * j], WIN - 1) for j in range(CAP)]
    used = [(j < count).astype(jnp.int32) for j in range(CAP)]
    on_a = [used[j] * ((rows[j] + SUB - 1) // SUB) for j in range(CAP)]
    on_b = [used[j] * (GROUPS - rows[j] // SUB + INT_GROUPS) for j in range(CAP)]
    best, chosen = jnp.int32(10000), jnp.int32(0)
    for mask in range(1 << CAP):
        total_a = jnp.int32(0)
        total_b = jnp.int32(0)
        slots_a = jnp.int32(0)
        slots_b = jnp.int32(0)
        for j in range(CAP):
            if mask >> j & 1:
                total_b = total_b + on_b[j]
                slots_b = slots_b + used[j]
            else:
                total_a = total_a + on_a[j]
                slots_a = slots_a + used[j]
        cost = jnp.maximum(total_a, total_b)
        cost = cost + jnp.where(cost > CAP_FWD, 1000, 0)
        cost = cost + jnp.where(jnp.maximum(slots_a, slots_b) > 2, UNEVEN, 0)
        better = cost < best
        best = jnp.where(better, cost, best)
        chosen = jnp.where(better, mask, chosen)
    at_a = jnp.int32(0)
    at_b = jnp.int32(0)
    back = jnp.int32(0)
    for j in range(CAP):
        to_b = jnp.bitwise_and(chosen >> j, 1) * used[j]
        to_b = jnp.where(rows[j] == 0, 0, to_b)
        to_a = used[j] - to_b
        table[FIELDS * j] = to_a * AT_A + to_b * AT_B
        table[FIELDS * j + 1] = rows[j]
        table[FIELDS * j + 2] = info[2 * j + 1]
        table[FIELDS * j + 3] = jnp.where(to_b == 1, at_b, at_a)
        table[FIELDS * j + 4] = jnp.where(to_b == 1, back, at_a)
        at_a = at_a + to_a * on_a[j]
        at_b = at_b + to_b * on_b[j]
        back = back + to_b * (on_b[j] - INT_GROUPS)


def slot_of(table, j):
    base = FIELDS * j
    return table[base], table[base + 1], table[base + 2], table[base + 3], table[base + 4]


def lane_blocks(col):
    first = col // LANES
    starts = [jnp.minimum(first + k, 7) * LANES for k in range(3)]
    return [pl.multiple_of(start, LANES) for start in starts], jnp.bitwise_and(col, LANES - 1)


WIDE = 3 * LANES


def near_columns(col):
    first = jnp.minimum(col // LANES, 5)
    skip = col // LANES - first
    starts = [pl.multiple_of(jnp.minimum(skip + k, 2) * LANES, LANES) for k in range(3)]
    return pl.ds(pl.multiple_of(first * LANES, LANES), WIDE), starts, jnp.bitwise_and(col, LANES - 1)


def lane_iota():
    return lax.broadcasted_iota(jnp.int32, (SUB, LANES), 1)


def load_group(field, plane, group, starts, shift):
    rows = pl.ds(pl.multiple_of(group * SUB, SUB), SUB)
    first = field[plane, rows, pl.ds(starts[0], LANES)]
    second = field[plane, rows, pl.ds(starts[1], LANES)]
    third = field[plane, rows, pl.ds(starts[2], LANES)]
    return jnp.where(lane_iota() >= shift, first, third), second


def add_group(total, plane, group, starts, shift, left, right):
    rows = pl.ds(pl.multiple_of(group * SUB, SUB), SUB)
    inside = lane_iota() >= shift
    total[plane, rows, pl.ds(starts[0], LANES)] += jnp.where(inside, left, 0.0)
    total[plane, rows, pl.ds(starts[1], LANES)] += right
    total[plane, rows, pl.ds(starts[2], LANES)] += jnp.where(inside, 0.0, left)


def fetch_columns(table, wanted, field, held, sem, base):
    for j in range(CAP):

        @pl.when(table[FIELDS * j] == wanted)
        def _():
            columns, _, _ = near_columns(table[FIELDS * j + 2])
            pltpu.make_async_copy(field.at[:, :, columns], held.at[base + j], sem.at[base + j]).start()


def copy_groups(held, out, at, offset, low, high, starts, shift):
    def body(group, carry):
        for plane in range(4):
            left, right = load_group(held.at[at], plane, group, starts, shift)
            out[offset + group, plane, :, :LANES] = left
            out[offset + group, plane, :, LANES:] = right
        return carry

    lax.fori_loop(low, high, body, 0)


def pack_to_b(table, field, intensity, out, held, sem, int_sem, base):
    def intensity_copy(j):
        _, row, _, start, _ = slot_of(table, j)
        after = start + GROUPS - row // SUB
        return pltpu.make_async_copy(intensity.at[j], out.at[pl.ds(after, INT_GROUPS)], int_sem.at[j])

    for j in range(CAP):

        @pl.when(table[FIELDS * j] == AT_B)
        def _():
            intensity_copy(j).start()

    for j in range(CAP):
        state, row, col, start, _ = slot_of(table, j)

        @pl.when(state == AT_B)
        def _():
            columns, starts, shift = near_columns(col)
            at = base + j
            pltpu.make_async_copy(field.at[:, :, columns], held.at[at], sem.at[at]).wait()
            copy_groups(held, out, at, start - row // SUB, row // SUB, GROUPS, starts, shift)
            intensity_copy(j).wait()


def pack_to_a(table, field, out, held, sem, base):
    for j in range(CAP):
        state, row, col, start, _ = slot_of(table, j)

        @pl.when(state == AT_A)
        def _():
            columns, starts, shift = near_columns(col)
            at = base + j
            pltpu.make_async_copy(field.at[:, :, columns], held.at[at], sem.at[at]).wait()
            copy_groups(held, out, at, start, 0, (row + SUB - 1) // SUB, starts, shift)


def pack_kernel(odd, own, before, field, intensity, inner, outer, table_in, table_out, held, sem, int_sem):
    @pl.when(odd[0] == 0)
    def _():
        decide(before, table_out)
        fetch_columns(table_out, AT_A, field, held, sem, 0)
        decide(own, table_in)
        fetch_columns(table_in, AT_B, field, held, sem, CAP)
        pack_to_a(table_out, field, outer, held, sem, 0)
        pack_to_b(table_in, field, intensity, inner, held, sem, int_sem, CAP)

    @pl.when(odd[0] == 1)
    def _():
        decide(own, table_out)
        fetch_columns(table_out, AT_B, field, held, sem, 0)
        decide(before, table_in)
        fetch_columns(table_in, AT_A, field, held, sem, CAP)
        pack_to_b(table_out, field, intensity, outer, held, sem, int_sem, 0)
        pack_to_a(table_in, field, inner, held, sem, CAP)


def prepare_kernel(phases, shuffle, out, halves):
    for plane in range(2):
        halves[0] = phases[plane, :, :LANES]
        halves[1] = phases[plane, :, LANES:]
        for part in range(2):
            every = pl.ds(part, HALF, stride=2)
            x = jnp.concatenate([halves[0, every, :], halves[1, every, :]], axis=1)
            high = x.astype(bf16)
            rest = x - high.astype(f32)
            middle, low = split(rest)
            total = jnp.dot(high, shuffle[...], preferred_element_type=f32)
            total += jnp.dot(middle, shuffle[...], preferred_element_type=f32)
            total += jnp.dot(low, shuffle[...], preferred_element_type=f32)
            out[plane, part * HALF : (part + 1) * HALF, :] = total


def slots_kernel(joint, role, table, field, intensity, probe, kernel, forms, shuffle, from_b, from_a, *rest):
    back_a, back_b = rest[0], rest[0 if joint else 1]
    tiles, held, got, tile, measured, twice, beam, work, entered, chosen = rest[1 if joint else 2 : -4]
    held_sem, int_sem, got_sem, tile_sem = rest[-4:]
    is_a = role[0] == 0
    mine = jnp.where(is_a, AT_A, AT_B)

    @pl.when(is_a)
    def _():
        pltpu.make_async_copy(from_b, got, got_sem).start()

    @pl.when(jnp.logical_not(is_a))
    def _():
        pltpu.make_async_copy(from_a, got, got_sem).start()

    fetch_columns(table, mine, field, held, held_sem, 0)

    def intensity_copies(j):
        return [
            pltpu.make_async_copy(
                intensity.at[j, :, pl.ds(part * LANES, LANES)], measured.at[j, part], int_sem.at[j, part]
            )
            for part in range(2)
        ]

    for j in range(CAP):

        @pl.when(jnp.logical_and(is_a, table[FIELDS * j] == AT_A))
        def _():
            for copy in intensity_copies(j):
                copy.start()

    for plane in range(2):
        for part in range(2):
            cut = probe[plane, :, part * LANES : (part + 1) * LANES]
            twice[2 * plane + part, :WIN] = cut
            twice[2 * plane + part, WIN:] = cut
    found = jnp.int32(0)
    for j in range(CAP):
        chosen[j] = 0
    for j in range(CAP):
        state = table[FIELDS * j]

        @pl.when(state == mine)
        def _():
            chosen[found] = j

        found = found + (state == mine).astype(jnp.int32)
    pltpu.make_async_copy(from_b, got, got_sem).wait()
    sublane = lax.broadcasted_iota(jnp.int32, (SUB, LANES), 0)

    def load(m, j):
        _, row, col, start, _ = slot_of(table, j)
        columns, starts, shift = near_columns(col)
        low = row // SUB
        high = (row + SUB - 1) // SUB
        base = jnp.where(is_a, start, start - low)

        def own_groups(group, carry):
            rows = pl.ds(pl.multiple_of(group * SUB, SUB), SUB)
            for plane in range(4):
                lf, rt = load_group(held.at[j], plane, group, starts, shift)
                tile[m, plane, rows, :LANES] = lf
                tile[m, plane, rows, LANES:] = rt
            return carry

        def their_groups(group, carry):
            rows = pl.ds(pl.multiple_of(group * SUB, SUB), SUB)
            for plane in range(4):
                tile[m, plane, rows, :] = got[base + group, plane]
            return carry

        lax.fori_loop(jnp.where(is_a, 0, low), jnp.where(is_a, high, GROUPS), their_groups, 0)
        lax.fori_loop(jnp.where(is_a, high, 0), jnp.where(is_a, GROUPS, low), own_groups, 0)

        @pl.when(low < high)
        def _():
            own = (low * SUB + sublane < row).astype(jnp.int32) == jnp.where(is_a, 0, 1)
            rows = pl.ds(pl.multiple_of(low * SUB, SUB), SUB)
            for plane in range(4):
                lf, rt = load_group(held.at[j], plane, low, starts, shift)
                tile[m, plane, rows, :LANES] = jnp.where(own, lf, tile[m, plane, rows, :LANES])
                tile[m, plane, rows, LANES:] = jnp.where(own, rt, tile[m, plane, rows, LANES:])

        @pl.when(jnp.logical_not(is_a))
        def _():
            after = start + GROUPS - low

            def unpack(group, carry):
                for plane in range(4):
                    rows = pl.ds(pl.multiple_of((group * 4 + plane) * SUB, SUB), SUB)
                    measured[j, 0, rows, :] = got[after + group, plane, :, :LANES]
                    measured[j, 1, rows, :] = got[after + group, plane, :, LANES:]
                return carry

            lax.fori_loop(0, INT_GROUPS, unpack, 0)

        for plane in range(2):
            parts = [twice[2 * plane + part, pl.ds(WIN - row, WIN), :] for part in range(2)]
            beam[m, plane] = pltpu.roll(jnp.concatenate(parts, axis=1), shift, 1)

    def arrive(j):
        columns, _, _ = near_columns(table[FIELDS * j + 2])
        pltpu.make_async_copy(field.at[:, :, columns], held.at[j], held_sem.at[j]).wait()

        @pl.when(is_a)
        def _():
            for copy in intensity_copies(j):
                copy.wait()

    def store_rows(m, e, o):
        work[m, 0, :HALF], work[m, 1, :HALF] = e[:HALF], e[HALF:]
        work[m, 0, HALF:], work[m, 1, HALF:] = o[:HALF], o[HALF:]

    def middle(pointwise, slots=None):
        for half in range(2):
            rows = pl.ds(half * HALF, HALF)
            for m in range(2):
                re, im = lanes_forward(work[m, 0, rows, :], work[m, 1, rows, :], forms)
                re, im = pointwise(m, half, rows, re, im, slots)
                re, im = lanes_inverse(re, im, forms)
                work[m, 0, rows, :], work[m, 1, rows, :] = re, im

    def rows_back(m):
        u, v = rows_inverse(work[m, 0], work[m, 1], forms)
        return (
            jnp.concatenate([u[:HALF] + v[:HALF], u[:HALF] - v[:HALF]], axis=0),
            jnp.concatenate([u[HALF:] + v[HALF:], u[HALF:] - v[HALF:]], axis=0),
        )

    def propagate(m, half, rows, re, im, slots):
        return cmul(kernel[0, rows, :], kernel[1, rows, :], re, im)

    def propagate_back(m, half, rows, re, im, slots):
        return cmul_conj(kernel[0, rows, :], kernel[1, rows, :], re, im)

    def residual(m, half, rows, re, im, slots):
        every = pl.ds(half, HALF, stride=2)
        at = slots[m]
        rows_of = jnp.concatenate([measured[at, 0, every, :], measured[at, 1, every, :]], axis=1)
        high, low = split(rows_of)
        wanted = jnp.dot(high, shuffle[...], preferred_element_type=f32)
        wanted += jnp.dot(low, shuffle[...], preferred_element_type=f32)
        scale = re * re + im * im - wanted
        return scale * re, scale * im

    def tile_copy(m, j):
        return pltpu.make_async_copy(tile.at[m], tiles.at[j], tile_sem.at[m])

    def write(m, j):
        _, row, _, _, back = slot_of(table, j)
        low = row // SUB

        def send(out, offset):
            def body(group, carry):
                rows = pl.ds(pl.multiple_of(group * SUB, SUB), SUB)
                for plane in range(4):
                    out[offset + group, plane] = tile[m, plane, rows, :]
                return carry

            return body

        tile_copy(m, j).start()

        @pl.when(is_a)
        def _():
            lax.fori_loop(0, (row + SUB - 1) // SUB, send(back_a, back), 0)

        @pl.when(jnp.logical_not(is_a))
        def _():
            lax.fori_loop(low, GROUPS, send(back_b, back - low), 0)

    def pair(p, carry):
        two = 2 * p + 1 < found
        first = chosen[2 * p]
        second = jnp.where(two, chosen[jnp.minimum(2 * p + 1, CAP - 1)], first)

        @pl.when(p > 0)
        def _():
            tile_copy(0, chosen[2 * p - 2]).wait()
            tile_copy(1, chosen[2 * p - 1]).wait()

        arrive(first)

        @pl.when(two)
        def _():
            arrive(second)

        load(0, first)
        load(1, second)
        for m in range(2):
            re, im = cmul(beam[m, 0], beam[m, 1], tile[m, 0], tile[m, 1])
            store_rows(m, *rows_forward(re, im, forms))
        middle(propagate)
        for m in range(2):
            re, im = rows_back(m)
            entered[m, 0], entered[m, 1] = re, im
            re, im = cmul(re, im, tile[m, 2], tile[m, 3])
            store_rows(m, *rows_forward(re, im, forms))
        middle(residual, (first, second))
        for m in range(2):
            br, bi = rows_back(m)
            re, im = cmul_conj(tile[m, 2], tile[m, 3], br, bi)
            tile[m, 2], tile[m, 3] = cmul_conj(entered[m, 0], entered[m, 1], br, bi)
            store_rows(m, *rows_forward(re, im, forms))
        middle(propagate_back)
        for m in range(2):
            br, bi = rows_back(m)
            tile[m, 0], tile[m, 1] = cmul_conj(beam[m, 0], beam[m, 1], br, bi)
        write(0, first)

        @pl.when(two)
        def _():
            write(1, second)

        return carry

    lax.fori_loop(0, (found + 1) // 2, pair, 0)

    @pl.when(found > 0)
    def _():
        tile_copy(0, 0).wait()

    @pl.when(jnp.logical_and(found > 0, jnp.bitwise_and(found, 1) == 0))
    def _():
        tile_copy(1, 0).wait()


def add_back(role, table, got, total, planes):
    is_a = role[0] == 0
    theirs = jnp.where(is_a, AT_B, AT_A)
    for j in range(CAP):
        state, row, col, _, back = slot_of(table, j)

        @pl.when(state == theirs)
        def _():
            starts, shift = lane_blocks(col)
            low = row // SUB
            base = jnp.where(is_a, back - low, back)
            sublane = lax.broadcasted_iota(jnp.int32, (SUB, LANES), 0)

            def body(group, carry):
                below = (group * SUB + sublane < row).astype(jnp.int32)
                own = below == jnp.where(is_a, 0, 1)
                for plane in planes:
                    lf = jnp.where(own, got[base + group, plane, :, :LANES], 0.0)
                    rt = jnp.where(own, got[base + group, plane, :, LANES:], 0.0)
                    add_group(total, plane, group, starts, shift, lf, rt)
                return carry

            lax.fori_loop(jnp.where(is_a, low, 0), jnp.where(is_a, GROUPS, (row + SUB - 1) // SUB), body, 0)


def sum_kernel(
    role_in, table_in, role_out, table_out, in_back, tiles_in, tiles_out, total, got, tile, got_sem, tile_sem
):
    pltpu.make_async_copy(in_back, got, got_sem).start()
    sublane = lax.broadcasted_iota(jnp.int32, (SUB, LANES), 0)
    kinds = ((role_in, table_in, tiles_in), (role_out, table_out, tiles_out))
    for k, (role, table, tiles) in enumerate(kinds):
        mine = jnp.where(role[0] == 0, AT_A, AT_B)
        for j in range(CAP):

            @pl.when(table[FIELDS * j] == mine)
            def _():
                pltpu.make_async_copy(tiles.at[j], tile.at[k * CAP + j], tile_sem.at[k * CAP + j]).start()

    total[...] = jnp.zeros_like(total)
    pltpu.make_async_copy(in_back, got, got_sem).wait()
    add_back(role_in, table_in, got, total, range(4))
    for k, (role, table, tiles) in enumerate(kinds):
        is_a = role[0] == 0
        mine = jnp.where(is_a, AT_A, AT_B)
        for j in range(CAP):
            state, row, col, _, _ = slot_of(table, j)

            @pl.when(state == mine)
            def _():
                at = k * CAP + j
                pltpu.make_async_copy(tiles.at[j], tile.at[at], tile_sem.at[at]).wait()
                starts, shift = lane_blocks(col)
                low = row // SUB

                def body(group, carry):
                    below = (group * SUB + sublane < row).astype(jnp.int32)
                    own = below == jnp.where(is_a, 0, 1)
                    rows = pl.ds(pl.multiple_of(group * SUB, SUB), SUB)
                    for plane in range(4):
                        lf = jnp.where(own, tile[at, plane, rows, :LANES], 0.0)
                        rt = jnp.where(own, tile[at, plane, rows, LANES:], 0.0)
                        add_group(total, plane, group, starts, shift, lf, rt)
                    return carry

                lax.fori_loop(
                    jnp.where(is_a, low, 0), jnp.where(is_a, GROUPS, (row + SUB - 1) // SUB), body, 0
                )


def finish_kernel(role, table, total_in, out_a, out_b, grad, total, got, got_sem, out_sem):
    is_a = role[0] == 0

    @pl.when(is_a)
    def _():
        copy = pltpu.make_async_copy(out_b, got.at[pl.ds(0, CAP_BACK_B)], got_sem)
        copy.start()
        copy.wait()

    @pl.when(jnp.logical_not(is_a))
    def _():
        copy = pltpu.make_async_copy(out_a, got, got_sem)
        copy.start()
        copy.wait()

    for plane in range(4):
        total[plane] = total_in[plane]
        add_back(role, table, got, total, (plane,))
        pltpu.make_async_copy(total.at[plane], grad.at[plane], out_sem.at[plane]).start()
    for plane in range(4):
        pltpu.make_async_copy(total.at[plane], grad.at[plane], out_sem.at[plane]).wait()


def spec(space):
    return pl.BlockSpec(memory_space=space)


def vmem(mib):
    return pltpu.CompilerParams(vmem_limit_bytes=mib << 20)


def packed(groups):
    return jax.ShapeDtypeStruct((groups, 4, SUB, WIN), f32)


def run_slots(joint, role, table, field, intensity, probe, kernel, tables, from_b, from_a):
    backs = (CAP_BACK_A,) if joint else (CAP_BACK_A, CAP_BACK_B)
    return pl.pallas_call(
        functools.partial(slots_kernel, joint),
        out_shape=tuple(packed(n) for n in backs) + (jax.ShapeDtypeStruct((CAP, 4, WIN, WIN), f32),),
        in_specs=[spec(SM)] * 2 + [spec(HB)] * 2 + [spec(VM)] * 4 + [spec(pl.ANY)] * 2,
        out_specs=(spec(VM),) * len(backs) + (spec(HB),),
        scratch_shapes=[
            pltpu.VMEM((CAP, 4, WIN, WIDE), f32),
            pltpu.VMEM((CAP_FWD, 4, SUB, WIN), f32),
            pltpu.VMEM((2, 4, WIN, WIN), f32),
            pltpu.VMEM((CAP, 2, WIN, LANES), f32),
            pltpu.VMEM((4, 2 * WIN, LANES), f32),
            pltpu.VMEM((2, 2, WIN, WIN), f32),
            pltpu.VMEM((2, 2, WIN, WIN), f32),
            pltpu.VMEM((2, 2, WIN, WIN), f32),
            pltpu.SMEM((CAP,), jnp.int32),
            pltpu.SemaphoreType.DMA((CAP,)),
            pltpu.SemaphoreType.DMA((CAP, 2)),
            pltpu.SemaphoreType.DMA,
            pltpu.SemaphoreType.DMA((2,)),
        ],
        cost_estimate=CHEAP,
        compiler_params=vmem(32),
    )(role, table, field, intensity, probe, kernel, *tables, from_b, from_a)


def shards(obj_field, probe_wave, prop_phase, win_offsets, live_counts, intensity):
    field = pltpu.with_memory_space_constraint(obj_field.reshape((4,) + obj_field.shape[2:]), HB)
    count = lax.axis_size("row")
    within = [(i, i + 1) for i in range(0, count - 1, 2)]
    across = [(i, i + 1) for i in range(1, count - 1, 2)]
    back = lambda pairs: [(b, a) for a, b in pairs]
    move = lambda x, pairs: lax.ppermute(x, "row", pairs)
    odd = jnp.bitwise_and(lax.axis_index("row"), 1)
    role_in = odd.reshape(1)
    role_out = (1 - odd).reshape(1)

    flag = odd.reshape(1)
    own = jnp.concatenate([win_offsets.reshape(-1), live_counts, jnp.zeros((INFO - 2 * CAP - 1,), jnp.int32)])
    maps = pltpu.with_memory_space_constraint(intensity.reshape(CAP, INT_GROUPS, 4, SUB, WIN), HB)
    intensity = pltpu.with_memory_space_constraint(intensity, HB)
    before = move(own, within + across)
    table = jax.ShapeDtypeStruct((CAP * FIELDS,), jnp.int32)
    inner, outer, table_in, table_out = pl.pallas_call(
        pack_kernel,
        out_shape=(packed(CAP_FWD), packed(CAP_FWD), table, table),
        in_specs=[spec(SM)] * 3 + [spec(HB)] * 2,
        out_specs=(spec(VM), spec(VM), spec(SM), spec(SM)),
        scratch_shapes=[
            pltpu.VMEM((2 * CAP, 4, WIN, WIDE), f32),
            pltpu.SemaphoreType.DMA((2 * CAP,)),
            pltpu.SemaphoreType.DMA((CAP,)),
        ],
        cost_estimate=CHEAP,
        compiler_params=vmem(24),
    )(flag, own, before, field, maps)
    out_from = move(outer, across + back(across))
    in_from = move(inner, within + back(within))

    forms, shuffle = (jnp.asarray(t) for t in make_tables())
    kernel = pl.pallas_call(
        prepare_kernel,
        out_shape=jax.ShapeDtypeStruct((2, WIN, WIN), f32),
        in_specs=[spec(VM)] * 2,
        out_specs=spec(VM),
        scratch_shapes=[pltpu.VMEM((2, WIN, LANES), f32)],
        cost_estimate=CHEAP,
        compiler_params=vmem(8),
    )(jnp.stack([jnp.cos(prop_phase), jnp.sin(prop_phase)]), shuffle)

    args = (field, intensity, probe_wave, kernel, (forms, shuffle))
    in_back, tiles_in = run_slots(True, role_in, table_in, *args, in_from, in_from)
    in_back = move(in_back, within + back(within))
    out_back_a, out_back_b, tiles_out = run_slots(False, role_out, table_out, *args, out_from, out_from)
    out_a = move(out_back_a, across)
    out_b = move(out_back_b, back(across))
    total = pl.pallas_call(
        sum_kernel,
        out_shape=jax.ShapeDtypeStruct(field.shape, f32),
        in_specs=[spec(SM)] * 4 + [spec(pl.ANY)] * 3,
        out_specs=spec(VM),
        scratch_shapes=[
            pltpu.VMEM((CAP_BACK_A, 4, SUB, WIN), f32),
            pltpu.VMEM((2 * CAP, 4, WIN, WIN), f32),
            pltpu.SemaphoreType.DMA,
            pltpu.SemaphoreType.DMA((2 * CAP,)),
        ],
        cost_estimate=CHEAP,
        compiler_params=vmem(20),
    )(role_in, table_in, role_out, table_out, in_back, tiles_in, tiles_out)
    grad = pl.pallas_call(
        finish_kernel,
        out_shape=jax.ShapeDtypeStruct(field.shape, f32),
        in_specs=[spec(SM)] * 2 + [spec(VM)] + [spec(pl.ANY)] * 2,
        out_specs=spec(HB),
        scratch_shapes=[
            pltpu.VMEM(field.shape, f32),
            pltpu.VMEM((CAP_BACK_A, 4, SUB, WIN), f32),
            pltpu.SemaphoreType.DMA,
            pltpu.SemaphoreType.DMA((4,)),
        ],
        cost_estimate=CHEAP,
        compiler_params=vmem(16),
    )(role_out, table_out, total, out_a, out_b)
    return grad.reshape(obj_field.shape)


def solution(mesh):
    in_specs = (
        P(None, None, ("groups", "row"), None),
        P("groups", None, None),
        P(),
        P(("groups", "row"), None),
        P(("groups", "row")),
        P(("groups", "row"), None, None),
    )
    out_specs = P(None, None, ("groups", "row"), None)
    return jax.shard_map(shards, mesh=mesh, in_specs=in_specs, out_specs=out_specs, check_vma=False)
```

```python
import functools

import jax
import jax.numpy as jnp
import numpy as np
from jax import lax
from jax.experimental import pallas as pl
from jax.experimental.pallas import tpu as pltpu
from jax.sharding import PartitionSpec as P

WIN = 256
HALF = WIN // 2
LANES = 128
SUB = 8
CAP = 4
GROUPS = WIN // SUB
INT_GROUPS = GROUPS // 4
CAP_WIDE = 48
CAP_NARROW = 28
NARROW_SLOTS = 2
UNEVEN = 24
DEAD, AT_A, AT_B = 0, 1, 2
FIELDS = 8
f32 = jnp.float32
bf16 = jnp.bfloat16
VM = pltpu.MemorySpace.VMEM
SM = pltpu.MemorySpace.SMEM
HB = pltpu.MemorySpace.HBM
CHEAP = pl.CostEstimate(flops=1, transcendentals=0, bytes_accessed=1)


def real_tables():
    k = np.arange(HALF)[:, None]
    n = np.arange(HALF)[None, :]
    out = []
    for odd in (0, 1):
        angle = 2.0 * np.pi * (((2 * k + odd) * n) % WIN) / WIN
        c, s = np.cos(angle) / 16.0, np.sin(angle) / 16.0
        out.append(np.block([[c, s], [-s, c]]))
    return out


def high_low(table):
    high = table.astype(np.float32).astype(bf16)
    low = (table - high.astype(np.float64)).astype(np.float32).astype(bf16)
    return high, low


def make_tables():
    even, odd = real_tables()
    forms = np.stack([np.stack(high_low(m)) for m in (even, odd, even.T, odd.T)])
    order = np.concatenate([np.arange(0, WIN, 2), np.arange(1, WIN, 2)])
    shuffle = np.zeros((WIN, WIN), np.float32)
    shuffle[order, np.arange(WIN)] = 1.0
    return forms, shuffle.astype(bf16)


EVEN, ODD, EVEN_T, ODD_T = range(4)


def split(x):
    high = x.astype(bf16)
    return high, (x - high.astype(f32)).astype(bf16)


def left_mul(forms, which, x):
    high, low = split(x)
    t_high, t_low = forms[which, 0], forms[which, 1]
    wide = jnp.concatenate([t_high, t_low, t_high], axis=1)
    return jnp.dot(wide, jnp.concatenate([high, high, low], axis=0), preferred_element_type=f32)


def right_mul(x, forms, which):
    high, low = split(x)
    t_high, t_low = forms[which, 0], forms[which, 1]
    tall = jnp.concatenate([t_high, t_high, t_low], axis=0)
    return jnp.dot(jnp.concatenate([high, low, high], axis=1), tall, preferred_element_type=f32)


def rows_forward(re, im, forms):
    tr, br, ti, bi = re[:HALF], re[HALF:], im[:HALF], im[HALF:]
    e = left_mul(forms, EVEN, jnp.concatenate([tr + br, ti + bi], axis=0))
    o = left_mul(forms, ODD, jnp.concatenate([tr - br, ti - bi], axis=0))
    return e, o


def rows_inverse(re, im, forms):
    u = left_mul(forms, EVEN_T, jnp.concatenate([re[:HALF], im[:HALF]], axis=0))
    v = left_mul(forms, ODD_T, jnp.concatenate([re[HALF:], im[HALF:]], axis=0))
    return u, v


def lanes_forward(re, im, forms):
    lr, rr, li, ri = re[:, :HALF], re[:, HALF:], im[:, :HALF], im[:, HALF:]
    e = right_mul(jnp.concatenate([lr + rr, li + ri], axis=1), forms, EVEN_T)
    o = right_mul(jnp.concatenate([lr - rr, li - ri], axis=1), forms, ODD_T)
    return (
        jnp.concatenate([e[:, :HALF], o[:, :HALF]], axis=1),
        jnp.concatenate([e[:, HALF:], o[:, HALF:]], axis=1),
    )


def lanes_inverse(re, im, forms):
    u = right_mul(jnp.concatenate([re[:, :HALF], im[:, :HALF]], axis=1), forms, EVEN)
    v = right_mul(jnp.concatenate([re[:, HALF:], im[:, HALF:]], axis=1), forms, ODD)
    return (
        jnp.concatenate([u[:, :HALF] + v[:, :HALF], u[:, :HALF] - v[:, :HALF]], axis=1),
        jnp.concatenate([u[:, HALF:] + v[:, HALF:], u[:, HALF:] - v[:, HALF:]], axis=1),
    )


def cmul(ar, ai, br, bi):
    return ar * br - ai * bi, ar * bi + ai * br


def cmul_conj(ar, ai, br, bi):
    return ar * br + ai * bi, ar * bi - ai * br


INFO = 16


def decide(info, table, first_slot, last_slot, cap):
    count = info[2 * CAP]
    rows = [jnp.bitwise_and(info[2 * j], WIN - 1) for j in range(CAP)]
    last_slot = jnp.minimum(last_slot, count)
    used = [jnp.logical_and(j >= first_slot, j < last_slot).astype(jnp.int32) for j in range(CAP)]
    on_a = [used[j] * ((rows[j] + SUB - 1) // SUB) for j in range(CAP)]
    on_b = [used[j] * (GROUPS - rows[j] // SUB + INT_GROUPS) for j in range(CAP)]
    best, chosen = jnp.int32(10000), jnp.int32(0)
    for mask in range(1 << CAP):
        total_a = jnp.int32(0)
        total_b = jnp.int32(0)
        slots_a = jnp.int32(0)
        slots_b = jnp.int32(0)
        for j in range(CAP):
            if mask >> j & 1:
                total_b = total_b + on_b[j]
                slots_b = slots_b + used[j]
            else:
                total_a = total_a + on_a[j]
                slots_a = slots_a + used[j]
        cost = jnp.maximum(total_a, total_b)
        cost = cost + jnp.where(cost > cap, 1000, 0)
        cost = cost + jnp.where(jnp.maximum(slots_a, slots_b) > 2, UNEVEN, 0)
        better = cost < best
        best = jnp.where(better, cost, best)
        chosen = jnp.where(better, mask, chosen)
    at_a = jnp.int32(0)
    at_b = jnp.int32(0)
    back = jnp.int32(0)
    for j in range(CAP):
        to_b = jnp.bitwise_and(chosen >> j, 1) * used[j]
        to_b = jnp.where(rows[j] == 0, 0, to_b)
        to_a = used[j] - to_b
        table[FIELDS * j] = to_a * AT_A + to_b * AT_B
        table[FIELDS * j + 1] = rows[j]
        table[FIELDS * j + 2] = info[2 * j + 1]
        table[FIELDS * j + 3] = jnp.where(to_b == 1, at_b, at_a)
        table[FIELDS * j + 4] = jnp.where(to_b == 1, back, at_a)
        at_a = at_a + to_a * on_a[j]
        at_b = at_b + to_b * on_b[j]
        back = back + to_b * (on_b[j] - INT_GROUPS)


def slot_of(table, j):
    base = FIELDS * j
    return table[base], table[base + 1], table[base + 2], table[base + 3], table[base + 4]


def lane_blocks(col):
    first = col // LANES
    starts = [jnp.minimum(first + k, 7) * LANES for k in range(3)]
    return [pl.multiple_of(start, LANES) for start in starts], jnp.bitwise_and(col, LANES - 1)


WIDE = 3 * LANES


def near_columns(col):
    first = jnp.minimum(col // LANES, 5)
    skip = col // LANES - first
    starts = [pl.multiple_of(jnp.minimum(skip + k, 2) * LANES, LANES) for k in range(3)]
    return pl.ds(pl.multiple_of(first * LANES, LANES), WIDE), starts, jnp.bitwise_and(col, LANES - 1)


def lane_iota():
    return lax.broadcasted_iota(jnp.int32, (SUB, LANES), 1)


def load_group(field, plane, group, starts, shift):
    rows = pl.ds(pl.multiple_of(group * SUB, SUB), SUB)
    first = field[plane, rows, pl.ds(starts[0], LANES)]
    second = field[plane, rows, pl.ds(starts[1], LANES)]
    third = field[plane, rows, pl.ds(starts[2], LANES)]
    return jnp.where(lane_iota() >= shift, first, third), second


def add_group(total, plane, group, starts, shift, left, right):
    rows = pl.ds(pl.multiple_of(group * SUB, SUB), SUB)
    inside = lane_iota() >= shift
    total[plane, rows, pl.ds(starts[0], LANES)] += jnp.where(inside, left, 0.0)
    total[plane, rows, pl.ds(starts[1], LANES)] += right
    total[plane, rows, pl.ds(starts[2], LANES)] += jnp.where(inside, 0.0, left)


def fetch_columns(table, wanted, field, held, sem, base):
    for j in range(CAP):

        @pl.when(table[FIELDS * j] == wanted)
        def _():
            columns, _, _ = near_columns(table[FIELDS * j + 2])
            pltpu.make_async_copy(field.at[:, :, columns], held.at[base + j], sem.at[base + j]).start()


def copy_groups(held, out, at, offset, low, high, starts, shift):
    def body(group, carry):
        for plane in range(4):
            left, right = load_group(held.at[at], plane, group, starts, shift)
            out[offset + group, plane, :, :LANES] = left
            out[offset + group, plane, :, LANES:] = right
        return carry

    lax.fori_loop(low, high, body, 0)


def pack_to_b(table, field, intensity, out, held, sem, int_sem, base):
    def intensity_copy(j):
        _, row, _, start, _ = slot_of(table, j)
        after = start + GROUPS - row // SUB
        return pltpu.make_async_copy(intensity.at[j], out.at[pl.ds(after, INT_GROUPS)], int_sem.at[j])

    for j in range(CAP):

        @pl.when(table[FIELDS * j] == AT_B)
        def _():
            intensity_copy(j).start()

    for j in range(CAP):
        state, row, col, start, _ = slot_of(table, j)

        @pl.when(state == AT_B)
        def _():
            columns, starts, shift = near_columns(col)
            at = base + j
            pltpu.make_async_copy(field.at[:, :, columns], held.at[at], sem.at[at]).wait()
            copy_groups(held, out, at, start - row // SUB, row // SUB, GROUPS, starts, shift)
            intensity_copy(j).wait()


def pack_to_a(table, field, out, held, sem, base):
    for j in range(CAP):
        state, row, col, start, _ = slot_of(table, j)

        @pl.when(state == AT_A)
        def _():
            columns, starts, shift = near_columns(col)
            at = base + j
            pltpu.make_async_copy(field.at[:, :, columns], held.at[at], sem.at[at]).wait()
            copy_groups(held, out, at, start, 0, (row + SUB - 1) // SUB, starts, shift)


def pack_kernel(
    flags, own, before, field, intensity, inner, wide, narrow, table_in, table_out, held, sem, int_sem
):
    turn = flags[2]
    is_narrow = flags[1] == 1
    first_slot = jnp.where(is_narrow, NARROW_SLOTS * turn, CAP * turn)
    last_slot = jnp.where(is_narrow, NARROW_SLOTS * (turn + 1), CAP)
    cap = jnp.where(is_narrow, CAP_NARROW, CAP_WIDE)

    def outward(pack):
        @pl.when(is_narrow)
        def _():
            pack(narrow)

        @pl.when(jnp.logical_not(is_narrow))
        def _():
            pack(wide)

    @pl.when(flags[0] == 0)
    def _():
        decide(before, table_out, first_slot, last_slot, cap)
        fetch_columns(table_out, AT_A, field, held, sem, 0)
        decide(own, table_in, CAP * turn, CAP, CAP_WIDE)
        fetch_columns(table_in, AT_B, field, held, sem, CAP)
        outward(lambda out: pack_to_a(table_out, field, out, held, sem, 0))
        pack_to_b(table_in, field, intensity, inner, held, sem, int_sem, CAP)

    @pl.when(flags[0] == 1)
    def _():
        decide(own, table_out, first_slot, last_slot, cap)
        fetch_columns(table_out, AT_B, field, held, sem, 0)
        decide(before, table_in, CAP * turn, CAP, CAP_WIDE)
        fetch_columns(table_in, AT_A, field, held, sem, CAP)
        outward(lambda out: pack_to_b(table_out, field, intensity, out, held, sem, int_sem, 0))
        pack_to_a(table_in, field, inner, held, sem, CAP)


def prepare_kernel(phases, shuffle, out, halves):
    for plane in range(2):
        halves[0] = phases[plane, :, :LANES]
        halves[1] = phases[plane, :, LANES:]
        for part in range(2):
            every = pl.ds(part, HALF, stride=2)
            x = jnp.concatenate([halves[0, every, :], halves[1, every, :]], axis=1)
            high = x.astype(bf16)
            rest = x - high.astype(f32)
            middle, low = split(rest)
            total = jnp.dot(high, shuffle[...], preferred_element_type=f32)
            total += jnp.dot(middle, shuffle[...], preferred_element_type=f32)
            total += jnp.dot(low, shuffle[...], preferred_element_type=f32)
            out[plane, part * HALF : (part + 1) * HALF, :] = total


def fetch_pieces(is_narrow, wide, narrow, got, sem):
    @pl.when(is_narrow)
    def _():
        pltpu.make_async_copy(narrow, got.at[pl.ds(0, CAP_NARROW)], sem).start()

    @pl.when(jnp.logical_not(is_narrow))
    def _():
        pltpu.make_async_copy(wide, got, sem).start()


def await_pieces(is_narrow, wide, narrow, got, sem):
    @pl.when(is_narrow)
    def _():
        pltpu.make_async_copy(narrow, got.at[pl.ds(0, CAP_NARROW)], sem).wait()

    @pl.when(jnp.logical_not(is_narrow))
    def _():
        pltpu.make_async_copy(wide, got, sem).wait()


def slots_kernel(between, flags, table, field, intensity, probe, kernel, forms, shuffle, wide, *rest):
    narrow = rest[0] if between else wide
    back_wide, back_narrow = (rest[1], rest[2]) if between else (rest[0], rest[0])
    tiles, held, got, tile, measured, twice, beam, work, entered, chosen = rest[3 if between else 1 : -4]
    held_sem, int_sem, got_sem, tile_sem = rest[-4:]
    is_a = flags[0] == (1 if between else 0)
    is_narrow = jnp.logical_and(between, flags[1] == 1)
    mine = jnp.where(is_a, AT_A, AT_B)
    if between:
        fetch_pieces(is_narrow, wide, narrow, got, got_sem)
    else:
        pltpu.make_async_copy(wide, got, got_sem).start()
    fetch_columns(table, mine, field, held, held_sem, 0)

    def intensity_copies(j):
        return [
            pltpu.make_async_copy(
                intensity.at[j, :, pl.ds(part * LANES, LANES)], measured.at[j, part], int_sem.at[j, part]
            )
            for part in range(2)
        ]

    for j in range(CAP):

        @pl.when(jnp.logical_and(is_a, table[FIELDS * j] == AT_A))
        def _():
            for copy in intensity_copies(j):
                copy.start()

    for plane in range(2):
        for part in range(2):
            cut = probe[plane, :, part * LANES : (part + 1) * LANES]
            twice[2 * plane + part, :WIN] = cut
            twice[2 * plane + part, WIN:] = cut
    found = jnp.int32(0)
    for j in range(CAP):
        chosen[j] = 0
    for j in range(CAP):
        state = table[FIELDS * j]

        @pl.when(state == mine)
        def _():
            chosen[found] = j

        found = found + (state == mine).astype(jnp.int32)
    if between:
        await_pieces(is_narrow, wide, narrow, got, got_sem)
    else:
        pltpu.make_async_copy(wide, got, got_sem).wait()
    sublane = lax.broadcasted_iota(jnp.int32, (SUB, LANES), 0)

    def load(m, j):
        _, row, col, start, _ = slot_of(table, j)
        columns, starts, shift = near_columns(col)
        low = row // SUB
        high = (row + SUB - 1) // SUB
        base = jnp.where(is_a, start, start - low)

        def own_groups(group, carry):
            rows = pl.ds(pl.multiple_of(group * SUB, SUB), SUB)
            for plane in range(4):
                lf, rt = load_group(held.at[j], plane, group, starts, shift)
                tile[m, plane, rows, :LANES] = lf
                tile[m, plane, rows, LANES:] = rt
            return carry

        def their_groups(group, carry):
            rows = pl.ds(pl.multiple_of(group * SUB, SUB), SUB)
            for plane in range(4):
                tile[m, plane, rows, :] = got[base + group, plane]
            return carry

        lax.fori_loop(jnp.where(is_a, 0, low), jnp.where(is_a, high, GROUPS), their_groups, 0)
        lax.fori_loop(jnp.where(is_a, high, 0), jnp.where(is_a, GROUPS, low), own_groups, 0)

        @pl.when(low < high)
        def _():
            own = (low * SUB + sublane < row).astype(jnp.int32) == jnp.where(is_a, 0, 1)
            rows = pl.ds(pl.multiple_of(low * SUB, SUB), SUB)
            for plane in range(4):
                lf, rt = load_group(held.at[j], plane, low, starts, shift)
                tile[m, plane, rows, :LANES] = jnp.where(own, lf, tile[m, plane, rows, :LANES])
                tile[m, plane, rows, LANES:] = jnp.where(own, rt, tile[m, plane, rows, LANES:])

        @pl.when(jnp.logical_not(is_a))
        def _():
            after = start + GROUPS - low

            def unpack(group, carry):
                for plane in range(4):
                    rows = pl.ds(pl.multiple_of((group * 4 + plane) * SUB, SUB), SUB)
                    measured[j, 0, rows, :] = got[after + group, plane, :, :LANES]
                    measured[j, 1, rows, :] = got[after + group, plane, :, LANES:]
                return carry

            lax.fori_loop(0, INT_GROUPS, unpack, 0)

        for plane in range(2):
            parts = [twice[2 * plane + part, pl.ds(WIN - row, WIN), :] for part in range(2)]
            beam[m, plane] = pltpu.roll(jnp.concatenate(parts, axis=1), shift, 1)

    def arrive(j):
        columns, _, _ = near_columns(table[FIELDS * j + 2])
        pltpu.make_async_copy(field.at[:, :, columns], held.at[j], held_sem.at[j]).wait()

        @pl.when(is_a)
        def _():
            for copy in intensity_copies(j):
                copy.wait()

    def store_rows(m, e, o):
        work[m, 0, :HALF], work[m, 1, :HALF] = e[:HALF], e[HALF:]
        work[m, 0, HALF:], work[m, 1, HALF:] = o[:HALF], o[HALF:]

    def middle(pointwise, slots=None):
        for half in range(2):
            rows = pl.ds(half * HALF, HALF)
            for m in range(2):
                re, im = lanes_forward(work[m, 0, rows, :], work[m, 1, rows, :], forms)
                re, im = pointwise(m, half, rows, re, im, slots)
                re, im = lanes_inverse(re, im, forms)
                work[m, 0, rows, :], work[m, 1, rows, :] = re, im

    def rows_back(m):
        u, v = rows_inverse(work[m, 0], work[m, 1], forms)
        return (
            jnp.concatenate([u[:HALF] + v[:HALF], u[:HALF] - v[:HALF]], axis=0),
            jnp.concatenate([u[HALF:] + v[HALF:], u[HALF:] - v[HALF:]], axis=0),
        )

    def propagate(m, half, rows, re, im, slots):
        return cmul(kernel[0, rows, :], kernel[1, rows, :], re, im)

    def propagate_back(m, half, rows, re, im, slots):
        return cmul_conj(kernel[0, rows, :], kernel[1, rows, :], re, im)

    def residual(m, half, rows, re, im, slots):
        every = pl.ds(half, HALF, stride=2)
        at = slots[m]
        rows_of = jnp.concatenate([measured[at, 0, every, :], measured[at, 1, every, :]], axis=1)
        high, low = split(rows_of)
        wanted = jnp.dot(high, shuffle[...], preferred_element_type=f32)
        wanted += jnp.dot(low, shuffle[...], preferred_element_type=f32)
        scale = re * re + im * im - wanted
        return scale * re, scale * im

    def tile_copy(m, j):
        return pltpu.make_async_copy(tile.at[m], tiles.at[j], tile_sem.at[m])

    def write(m, j):
        _, row, _, _, back = slot_of(table, j)
        low = row // SUB

        def send(out, offset):
            def body(group, carry):
                rows = pl.ds(pl.multiple_of(group * SUB, SUB), SUB)
                for plane in range(4):
                    out[offset + group, plane] = tile[m, plane, rows, :]
                return carry

            return body

        tile_copy(m, j).start()

        offset = jnp.where(is_a, back, back - low)
        lower = jnp.where(is_a, 0, low)
        upper = jnp.where(is_a, (row + SUB - 1) // SUB, GROUPS)
        if between:

            @pl.when(is_narrow)
            def _():
                lax.fori_loop(lower, upper, send(back_narrow, offset), 0)

            @pl.when(jnp.logical_not(is_narrow))
            def _():
                lax.fori_loop(lower, upper, send(back_wide, offset), 0)

        else:
            lax.fori_loop(lower, upper, send(back_wide, offset), 0)

    def pair(p, carry):
        two = 2 * p + 1 < found
        first = chosen[2 * p]
        second = jnp.where(two, chosen[jnp.minimum(2 * p + 1, CAP - 1)], first)

        @pl.when(p > 0)
        def _():
            tile_copy(0, chosen[2 * p - 2]).wait()
            tile_copy(1, chosen[2 * p - 1]).wait()

        arrive(first)

        @pl.when(two)
        def _():
            arrive(second)

        load(0, first)
        load(1, second)
        for m in range(2):
            re, im = cmul(beam[m, 0], beam[m, 1], tile[m, 0], tile[m, 1])
            store_rows(m, *rows_forward(re, im, forms))
        middle(propagate)
        for m in range(2):
            re, im = rows_back(m)
            entered[m, 0], entered[m, 1] = re, im
            re, im = cmul(re, im, tile[m, 2], tile[m, 3])
            store_rows(m, *rows_forward(re, im, forms))
        middle(residual, (first, second))
        for m in range(2):
            br, bi = rows_back(m)
            re, im = cmul_conj(tile[m, 2], tile[m, 3], br, bi)
            tile[m, 2], tile[m, 3] = cmul_conj(entered[m, 0], entered[m, 1], br, bi)
            store_rows(m, *rows_forward(re, im, forms))
        middle(propagate_back)
        for m in range(2):
            br, bi = rows_back(m)
            tile[m, 0], tile[m, 1] = cmul_conj(beam[m, 0], beam[m, 1], br, bi)
        write(0, first)

        @pl.when(two)
        def _():
            write(1, second)

        return carry

    lax.fori_loop(0, (found + 1) // 2, pair, 0)

    @pl.when(found > 0)
    def _():
        tile_copy(0, 0).wait()

    @pl.when(jnp.logical_and(found > 0, jnp.bitwise_and(found, 1) == 0))
    def _():
        tile_copy(1, 0).wait()


def add_back(is_a, table, got, total, planes):
    theirs = jnp.where(is_a, AT_B, AT_A)
    for j in range(CAP):
        state, row, col, _, back = slot_of(table, j)

        @pl.when(state == theirs)
        def _():
            starts, shift = lane_blocks(col)
            low = row // SUB
            base = jnp.where(is_a, back - low, back)
            sublane = lax.broadcasted_iota(jnp.int32, (SUB, LANES), 0)

            def body(group, carry):
                below = (group * SUB + sublane < row).astype(jnp.int32)
                own = below == jnp.where(is_a, 0, 1)
                for plane in planes:
                    lf = jnp.where(own, got[base + group, plane, :, :LANES], 0.0)
                    rt = jnp.where(own, got[base + group, plane, :, LANES:], 0.0)
                    add_group(total, plane, group, starts, shift, lf, rt)
                return carry

            lax.fori_loop(jnp.where(is_a, low, 0), jnp.where(is_a, GROUPS, (row + SUB - 1) // SUB), body, 0)


def sum_kernel(
    flags, table_in, table_out, in_back, tiles_in, tiles_out, grad, total, got, tile, got_sem, tile_sem, total_sem
):
    pltpu.make_async_copy(in_back, got, got_sem).start()
    sublane = lax.broadcasted_iota(jnp.int32, (SUB, LANES), 0)
    kinds = ((flags[0] == 0, table_in, tiles_in), (flags[0] == 1, table_out, tiles_out))
    for k, (is_a, table, tiles) in enumerate(kinds):
        mine = jnp.where(is_a, AT_A, AT_B)
        for j in range(CAP):

            @pl.when(table[FIELDS * j] == mine)
            def _():
                pltpu.make_async_copy(tiles.at[j], tile.at[k * CAP + j], tile_sem.at[k * CAP + j]).start()

    @pl.when(flags[2] == 0)
    def _():
        total[...] = jnp.zeros_like(total)

    @pl.when(flags[2] > 0)
    def _():
        copy = pltpu.make_async_copy(grad, total, total_sem)
        copy.start()
        copy.wait()

    pltpu.make_async_copy(in_back, got, got_sem).wait()
    add_back(flags[0] == 0, table_in, got, total, range(4))
    for k, (is_a, table, tiles) in enumerate(kinds):
        mine = jnp.where(is_a, AT_A, AT_B)
        for j in range(CAP):
            state, row, col, _, _ = slot_of(table, j)

            @pl.when(state == mine)
            def _():
                at = k * CAP + j
                pltpu.make_async_copy(tiles.at[j], tile.at[at], tile_sem.at[at]).wait()
                starts, shift = lane_blocks(col)
                low = row // SUB

                def body(group, carry):
                    below = (group * SUB + sublane < row).astype(jnp.int32)
                    own = below == jnp.where(is_a, 0, 1)
                    rows = pl.ds(pl.multiple_of(group * SUB, SUB), SUB)
                    for plane in range(4):
                        lf = jnp.where(own, tile[at, plane, rows, :LANES], 0.0)
                        rt = jnp.where(own, tile[at, plane, rows, LANES:], 0.0)
                        add_group(total, plane, group, starts, shift, lf, rt)
                    return carry

                lax.fori_loop(
                    jnp.where(is_a, low, 0), jnp.where(is_a, GROUPS, (row + SUB - 1) // SUB), body, 0
                )


def finish_kernel(flags, table, total_in, wide, narrow, grad, total, got, got_sem, out_sem):
    is_narrow = flags[1] == 1
    fetch_pieces(is_narrow, wide, narrow, got, got_sem)
    await_pieces(is_narrow, wide, narrow, got, got_sem)
    for plane in range(4):
        total[plane] = total_in[plane]
        add_back(flags[0] == 1, table, got, total, (plane,))
        pltpu.make_async_copy(total.at[plane], grad.at[plane], out_sem.at[plane]).start()
    for plane in range(4):
        pltpu.make_async_copy(total.at[plane], grad.at[plane], out_sem.at[plane]).wait()


def spec(space):
    return pl.BlockSpec(memory_space=space)


def vmem(mib):
    return pltpu.CompilerParams(vmem_limit_bytes=mib << 20)


def packed(groups):
    return jax.ShapeDtypeStruct((groups, 4, SUB, WIN), f32)


def run_slots(flags, table, field, intensity, probe, kernel, tables, *pieces):
    between = len(pieces) == 2
    backs = (CAP_WIDE, CAP_NARROW)[: len(pieces)]
    return pl.pallas_call(
        functools.partial(slots_kernel, between),
        out_shape=tuple(packed(n) for n in backs) + (jax.ShapeDtypeStruct((CAP, 4, WIN, WIN), f32),),
        in_specs=[spec(SM)] * 2 + [spec(HB)] * 2 + [spec(VM)] * 4 + [spec(pl.ANY)] * len(pieces),
        out_specs=(spec(VM),) * len(backs) + (spec(HB),),
        scratch_shapes=[
            pltpu.VMEM((CAP, 4, WIN, WIDE), f32),
            pltpu.VMEM((CAP_WIDE, 4, SUB, WIN), f32),
            pltpu.VMEM((2, 4, WIN, WIN), f32),
            pltpu.VMEM((CAP, 2, WIN, LANES), f32),
            pltpu.VMEM((4, 2 * WIN, LANES), f32),
            pltpu.VMEM((2, 2, WIN, WIN), f32),
            pltpu.VMEM((2, 2, WIN, WIN), f32),
            pltpu.VMEM((2, 2, WIN, WIN), f32),
            pltpu.SMEM((CAP,), jnp.int32),
            pltpu.SemaphoreType.DMA((CAP,)),
            pltpu.SemaphoreType.DMA((CAP, 2)),
            pltpu.SemaphoreType.DMA,
            pltpu.SemaphoreType.DMA((2,)),
        ],
        cost_estimate=CHEAP,
        compiler_params=vmem(32),
    )(flags, table, field, intensity, probe, kernel, *tables, *pieces)


def both_ways(pairs):
    return pairs + [(b, a) for a, b in pairs]


def one_round(turn, grad, field, maps, intensity, probe_wave, prop_phase, own, before):
    count = lax.axis_size("row")
    within = both_ways([(i, i + 1) for i in range(0, count - 1, 2)])
    wide_pairs = both_ways([(i, i + 1) for i in range(1, count - 1, 4)])
    narrow_pairs = both_ways([(i, i + 1) for i in range(3, count - 1, 4)])
    move = lambda x, pairs: lax.ppermute(x, "row", pairs)
    place = lax.axis_index("row")
    odd = jnp.bitwise_and(place, 1)
    is_narrow = (jnp.bitwise_and(place + 1, 2) == 0).astype(jnp.int32)
    flags = jnp.stack([odd, is_narrow, turn])

    table = jax.ShapeDtypeStruct((CAP * FIELDS,), jnp.int32)
    inner, wide, narrow, table_in, table_out = pl.pallas_call(
        pack_kernel,
        out_shape=(packed(CAP_WIDE), packed(CAP_WIDE), packed(CAP_NARROW), table, table),
        in_specs=[spec(SM)] * 3 + [spec(HB)] * 2,
        out_specs=(spec(VM),) * 3 + (spec(SM),) * 2,
        scratch_shapes=[
            pltpu.VMEM((2 * CAP, 4, WIN, WIDE), f32),
            pltpu.SemaphoreType.DMA((2 * CAP,)),
            pltpu.SemaphoreType.DMA((CAP,)),
        ],
        cost_estimate=CHEAP,
        compiler_params=vmem(24),
    )(flags, own, before, field, maps)
    wide = move(wide, wide_pairs)
    narrow = move(narrow, narrow_pairs)
    inner = move(inner, within)

    forms, shuffle = (jnp.asarray(t) for t in make_tables())
    kernel = pl.pallas_call(
        prepare_kernel,
        out_shape=jax.ShapeDtypeStruct((2, WIN, WIN), f32),
        in_specs=[spec(VM)] * 2,
        out_specs=spec(VM),
        scratch_shapes=[pltpu.VMEM((2, WIN, LANES), f32)],
        cost_estimate=CHEAP,
        compiler_params=vmem(8),
    )(jnp.stack([jnp.cos(prop_phase), jnp.sin(prop_phase)]), shuffle)

    args = (field, intensity, probe_wave, kernel, (forms, shuffle))
    in_back, tiles_in = run_slots(flags, table_in, *args, inner)
    in_back = move(in_back, within)
    back_wide, back_narrow, tiles_out = run_slots(flags, table_out, *args, wide, narrow)
    back_wide = move(back_wide, wide_pairs)
    back_narrow = move(back_narrow, narrow_pairs)
    total = pl.pallas_call(
        sum_kernel,
        out_shape=jax.ShapeDtypeStruct(field.shape, f32),
        in_specs=[spec(SM)] * 3 + [spec(pl.ANY)] * 3 + [spec(HB)],
        out_specs=spec(VM),
        scratch_shapes=[
            pltpu.VMEM((CAP_WIDE, 4, SUB, WIN), f32),
            pltpu.VMEM((2 * CAP, 4, WIN, WIN), f32),
            pltpu.SemaphoreType.DMA,
            pltpu.SemaphoreType.DMA((2 * CAP,)),
            pltpu.SemaphoreType.DMA,
        ],
        cost_estimate=CHEAP,
        compiler_params=vmem(20),
    )(flags, table_in, table_out, in_back, tiles_in, tiles_out, grad)
    return pl.pallas_call(
        finish_kernel,
        out_shape=jax.ShapeDtypeStruct(field.shape, f32),
        in_specs=[spec(SM)] * 2 + [spec(VM)] + [spec(pl.ANY)] * 2,
        out_specs=spec(HB),
        scratch_shapes=[
            pltpu.VMEM(field.shape, f32),
            pltpu.VMEM((CAP_WIDE, 4, SUB, WIN), f32),
            pltpu.SemaphoreType.DMA,
            pltpu.SemaphoreType.DMA((4,)),
        ],
        cost_estimate=CHEAP,
        compiler_params=vmem(16),
    )(flags, table_out, total, back_wide, back_narrow)


def shards(obj_field, probe_wave, prop_phase, win_offsets, live_counts, intensity):
    field = pltpu.with_memory_space_constraint(obj_field.reshape((4,) + obj_field.shape[2:]), HB)
    maps = pltpu.with_memory_space_constraint(intensity.reshape(CAP, INT_GROUPS, 4, SUB, WIN), HB)
    intensity = pltpu.with_memory_space_constraint(intensity, HB)
    count = lax.axis_size("row")
    own = jnp.concatenate([win_offsets.reshape(-1), live_counts, jnp.zeros((INFO - 2 * CAP - 1,), jnp.int32)])
    before = lax.ppermute(own, "row", [(i, i + 1) for i in range(count - 1)])
    narrow_first = jnp.bitwise_and(lax.axis_index("row"), 3) == 3
    left_over = jnp.logical_and(narrow_first, live_counts[0] > NARROW_SLOTS).astype(jnp.int32)

    def body(state):
        turn, _, grad = state
        again = lax.pmax(left_over * (1 - turn), ("groups", "row"))
        grad = one_round(turn, grad, field, maps, intensity, probe_wave, prop_phase, own, before)
        return turn + 1, again, grad

    empty = pl.pallas_call(
        lambda out: None,
        out_shape=jax.ShapeDtypeStruct(field.shape, f32),
        out_specs=spec(HB),
    )()
    _, _, grad = lax.while_loop(lambda state: state[1] > 0, body, (jnp.int32(0), jnp.int32(1), empty))
    return grad.reshape(obj_field.shape)


def solution(mesh):
    in_specs = (
        P(None, None, ("groups", "row"), None),
        P("groups", None, None),
        P(),
        P(("groups", "row"), None),
        P(("groups", "row")),
        P(("groups", "row"), None, None),
    )
    out_specs = P(None, None, ("groups", "row"), None)
    return jax.shard_map(shards, mesh=mesh, in_specs=in_specs, out_specs=out_specs, check_vma=False)
```

```python
import functools

import jax
import jax.numpy as jnp
import numpy as np
from jax import lax
from jax.experimental import pallas as pl
from jax.experimental.pallas import tpu as pltpu
from jax.sharding import PartitionSpec as P

WIN = 256
HALF = WIN // 2
LANES = 128
SUB = 8
CAP = 4
GROUPS = WIN // SUB
INT_GROUPS = GROUPS // 4
CAP_WIDE = 48
CAP_NARROW = 28
NARROW_SLOTS = 2
UNEVEN = 24
DEAD, AT_A, AT_B = 0, 1, 2
FIELDS = 8
f32 = jnp.float32
bf16 = jnp.bfloat16
VM = pltpu.MemorySpace.VMEM
SM = pltpu.MemorySpace.SMEM
HB = pltpu.MemorySpace.HBM
CHEAP = pl.CostEstimate(flops=1, transcendentals=0, bytes_accessed=1)


def real_tables():
    k = np.arange(HALF)[:, None]
    n = np.arange(HALF)[None, :]
    out = []
    for odd in (0, 1):
        angle = 2.0 * np.pi * (((2 * k + odd) * n) % WIN) / WIN
        c, s = np.cos(angle) / 16.0, np.sin(angle) / 16.0
        out.append(np.block([[c, s], [-s, c]]))
    return out


def high_low(table):
    high = table.astype(np.float32).astype(bf16)
    low = (table - high.astype(np.float64)).astype(np.float32).astype(bf16)
    return high, low


def make_tables():
    even, odd = real_tables()
    forms = np.stack([np.stack(high_low(m)) for m in (even, odd, even.T, odd.T)])
    order = np.concatenate([np.arange(0, WIN, 2), np.arange(1, WIN, 2)])
    shuffle = np.zeros((WIN, WIN), np.float32)
    shuffle[order, np.arange(WIN)] = 1.0
    return forms, shuffle.astype(bf16)


EVEN, ODD, EVEN_T, ODD_T = range(4)


def split(x):
    high = x.astype(bf16)
    return high, (x - high.astype(f32)).astype(bf16)


def left_mul(forms, which, x):
    high, low = split(x)
    t_high, t_low = forms[which, 0], forms[which, 1]
    wide = jnp.concatenate([t_high, t_low, t_high], axis=1)
    return jnp.dot(wide, jnp.concatenate([high, high, low], axis=0), preferred_element_type=f32)


def right_mul(x, forms, which):
    high, low = split(x)
    t_high, t_low = forms[which, 0], forms[which, 1]
    tall = jnp.concatenate([t_high, t_high, t_low], axis=0)
    return jnp.dot(jnp.concatenate([high, low, high], axis=1), tall, preferred_element_type=f32)


def rows_forward(re, im, forms):
    tr, br, ti, bi = re[:HALF], re[HALF:], im[:HALF], im[HALF:]
    e = left_mul(forms, EVEN, jnp.concatenate([tr + br, ti + bi], axis=0))
    o = left_mul(forms, ODD, jnp.concatenate([tr - br, ti - bi], axis=0))
    return e, o


def rows_inverse(re, im, forms):
    u = left_mul(forms, EVEN_T, jnp.concatenate([re[:HALF], im[:HALF]], axis=0))
    v = left_mul(forms, ODD_T, jnp.concatenate([re[HALF:], im[HALF:]], axis=0))
    return u, v


def lanes_forward(re, im, forms):
    lr, rr, li, ri = re[:, :HALF], re[:, HALF:], im[:, :HALF], im[:, HALF:]
    e = right_mul(jnp.concatenate([lr + rr, li + ri], axis=1), forms, EVEN_T)
    o = right_mul(jnp.concatenate([lr - rr, li - ri], axis=1), forms, ODD_T)
    return (
        jnp.concatenate([e[:, :HALF], o[:, :HALF]], axis=1),
        jnp.concatenate([e[:, HALF:], o[:, HALF:]], axis=1),
    )


def lanes_inverse(re, im, forms):
    u = right_mul(jnp.concatenate([re[:, :HALF], im[:, :HALF]], axis=1), forms, EVEN)
    v = right_mul(jnp.concatenate([re[:, HALF:], im[:, HALF:]], axis=1), forms, ODD)
    return (
        jnp.concatenate([u[:, :HALF] + v[:, :HALF], u[:, :HALF] - v[:, :HALF]], axis=1),
        jnp.concatenate([u[:, HALF:] + v[:, HALF:], u[:, HALF:] - v[:, HALF:]], axis=1),
    )


def cmul(ar, ai, br, bi):
    return ar * br - ai * bi, ar * bi + ai * br


def cmul_conj(ar, ai, br, bi):
    return ar * br + ai * bi, ar * bi - ai * br


INFO = 16


def decide(info, table, first_slot, last_slot, cap):
    count = info[2 * CAP]
    rows = [jnp.bitwise_and(info[2 * j], WIN - 1) for j in range(CAP)]
    last_slot = jnp.minimum(last_slot, count)
    used = [jnp.logical_and(j >= first_slot, j < last_slot).astype(jnp.int32) for j in range(CAP)]
    on_a = [used[j] * ((rows[j] + SUB - 1) // SUB) for j in range(CAP)]
    on_b = [used[j] * (GROUPS - rows[j] // SUB + INT_GROUPS) for j in range(CAP)]
    best, chosen = jnp.int32(10000), jnp.int32(0)
    for mask in range(1 << CAP):
        total_a = jnp.int32(0)
        total_b = jnp.int32(0)
        slots_a = jnp.int32(0)
        slots_b = jnp.int32(0)
        for j in range(CAP):
            if mask >> j & 1:
                total_b = total_b + on_b[j]
                slots_b = slots_b + used[j]
            else:
                total_a = total_a + on_a[j]
                slots_a = slots_a + used[j]
        cost = jnp.maximum(total_a, total_b)
        cost = cost + jnp.where(cost > cap, 1000, 0)
        cost = cost + jnp.where(jnp.maximum(slots_a, slots_b) > 2, UNEVEN, 0)
        better = cost < best
        best = jnp.where(better, cost, best)
        chosen = jnp.where(better, mask, chosen)
    at_a = jnp.int32(0)
    at_b = jnp.int32(0)
    back = jnp.int32(0)
    for j in range(CAP):
        to_b = jnp.bitwise_and(chosen >> j, 1) * used[j]
        to_b = jnp.where(rows[j] == 0, 0, to_b)
        to_a = used[j] - to_b
        table[FIELDS * j] = to_a * AT_A + to_b * AT_B
        table[FIELDS * j + 1] = rows[j]
        table[FIELDS * j + 2] = info[2 * j + 1]
        table[FIELDS * j + 3] = jnp.where(to_b == 1, at_b, at_a)
        table[FIELDS * j + 4] = jnp.where(to_b == 1, back, at_a)
        at_a = at_a + to_a * on_a[j]
        at_b = at_b + to_b * on_b[j]
        back = back + to_b * (on_b[j] - INT_GROUPS)


def slot_of(table, j):
    base = FIELDS * j
    return table[base], table[base + 1], table[base + 2], table[base + 3], table[base + 4]


def lane_blocks(col):
    first = col // LANES
    starts = [jnp.minimum(first + k, 7) * LANES for k in range(3)]
    return [pl.multiple_of(start, LANES) for start in starts], jnp.bitwise_and(col, LANES - 1)


WIDE = 3 * LANES


def near_columns(col):
    first = jnp.minimum(col // LANES, 5)
    skip = col // LANES - first
    starts = [pl.multiple_of(jnp.minimum(skip + k, 2) * LANES, LANES) for k in range(3)]
    return pl.ds(pl.multiple_of(first * LANES, LANES), WIDE), starts, jnp.bitwise_and(col, LANES - 1)


def lane_iota():
    return lax.broadcasted_iota(jnp.int32, (SUB, LANES), 1)


def load_group(field, plane, group, starts, shift):
    rows = pl.ds(pl.multiple_of(group * SUB, SUB), SUB)
    first = field[plane, rows, pl.ds(starts[0], LANES)]
    second = field[plane, rows, pl.ds(starts[1], LANES)]
    third = field[plane, rows, pl.ds(starts[2], LANES)]
    return jnp.where(lane_iota() >= shift, first, third), second


def add_group(total, plane, group, starts, shift, left, right):
    rows = pl.ds(pl.multiple_of(group * SUB, SUB), SUB)
    inside = lane_iota() >= shift
    total[plane, rows, pl.ds(starts[0], LANES)] += jnp.where(inside, left, 0.0)
    total[plane, rows, pl.ds(starts[1], LANES)] += right
    total[plane, rows, pl.ds(starts[2], LANES)] += jnp.where(inside, 0.0, left)


def fetch_columns(table, wanted, field, held, sem, base):
    for j in range(CAP):

        @pl.when(table[FIELDS * j] == wanted)
        def _():
            columns, _, _ = near_columns(table[FIELDS * j + 2])
            pltpu.make_async_copy(field.at[:, :, columns], held.at[base + j], sem.at[base + j]).start()


def copy_groups(held, out, at, offset, low, high, starts, shift):
    def body(group, carry):
        for plane in range(4):
            left, right = load_group(held.at[at], plane, group, starts, shift)
            out[offset + group, plane, :, :LANES] = left
            out[offset + group, plane, :, LANES:] = right
        return carry

    lax.fori_loop(low, high, body, 0)


def pack_to_b(table, field, intensity, out, held, sem, int_sem, base):
    def intensity_copy(j):
        _, row, _, start, _ = slot_of(table, j)
        after = start + GROUPS - row // SUB
        return pltpu.make_async_copy(intensity.at[j], out.at[pl.ds(after, INT_GROUPS)], int_sem.at[j])

    for j in range(CAP):

        @pl.when(table[FIELDS * j] == AT_B)
        def _():
            intensity_copy(j).start()

    for j in range(CAP):
        state, row, col, start, _ = slot_of(table, j)

        @pl.when(state == AT_B)
        def _():
            columns, starts, shift = near_columns(col)
            at = base + j
            pltpu.make_async_copy(field.at[:, :, columns], held.at[at], sem.at[at]).wait()
            copy_groups(held, out, at, start - row // SUB, row // SUB, GROUPS, starts, shift)
            intensity_copy(j).wait()


def pack_to_a(table, field, out, held, sem, base):
    for j in range(CAP):
        state, row, col, start, _ = slot_of(table, j)

        @pl.when(state == AT_A)
        def _():
            columns, starts, shift = near_columns(col)
            at = base + j
            pltpu.make_async_copy(field.at[:, :, columns], held.at[at], sem.at[at]).wait()
            copy_groups(held, out, at, start, 0, (row + SUB - 1) // SUB, starts, shift)


def pack_kernel(
    flags, own, before, field, intensity, inner, wide, narrow, table_in, table_out, held, sem, int_sem
):
    turn = flags[2]
    is_narrow = flags[1] == 1
    first_slot = jnp.where(is_narrow, NARROW_SLOTS * turn, CAP * turn)
    last_slot = jnp.where(is_narrow, NARROW_SLOTS * (turn + 1), CAP)
    cap = jnp.where(is_narrow, CAP_NARROW, CAP_WIDE)

    def outward(pack):
        @pl.when(is_narrow)
        def _():
            pack(narrow)

        @pl.when(jnp.logical_not(is_narrow))
        def _():
            pack(wide)

    @pl.when(flags[0] == 0)
    def _():
        decide(before, table_out, first_slot, last_slot, cap)
        fetch_columns(table_out, AT_A, field, held, sem, 0)
        decide(own, table_in, CAP * turn, CAP, CAP_WIDE)
        fetch_columns(table_in, AT_B, field, held, sem, CAP)
        outward(lambda out: pack_to_a(table_out, field, out, held, sem, 0))
        pack_to_b(table_in, field, intensity, inner, held, sem, int_sem, CAP)

    @pl.when(flags[0] == 1)
    def _():
        decide(own, table_out, first_slot, last_slot, cap)
        fetch_columns(table_out, AT_B, field, held, sem, 0)
        decide(before, table_in, CAP * turn, CAP, CAP_WIDE)
        fetch_columns(table_in, AT_A, field, held, sem, CAP)
        outward(lambda out: pack_to_b(table_out, field, intensity, out, held, sem, int_sem, 0))
        pack_to_a(table_in, field, inner, held, sem, CAP)


def prepare_kernel(phases, shuffle, out, halves):
    for plane in range(2):
        halves[0] = phases[plane, :, :LANES]
        halves[1] = phases[plane, :, LANES:]
        for part in range(2):
            every = pl.ds(part, HALF, stride=2)
            x = jnp.concatenate([halves[0, every, :], halves[1, every, :]], axis=1)
            high = x.astype(bf16)
            rest = x - high.astype(f32)
            middle, low = split(rest)
            total = jnp.dot(high, shuffle[...], preferred_element_type=f32)
            total += jnp.dot(middle, shuffle[...], preferred_element_type=f32)
            total += jnp.dot(low, shuffle[...], preferred_element_type=f32)
            out[plane, part * HALF : (part + 1) * HALF, :] = total


def fetch_pieces(is_narrow, wide, narrow, got, sem):
    @pl.when(is_narrow)
    def _():
        pltpu.make_async_copy(narrow, got.at[pl.ds(0, CAP_NARROW)], sem).start()

    @pl.when(jnp.logical_not(is_narrow))
    def _():
        pltpu.make_async_copy(wide, got, sem).start()


def await_pieces(is_narrow, wide, narrow, got, sem):
    @pl.when(is_narrow)
    def _():
        pltpu.make_async_copy(narrow, got.at[pl.ds(0, CAP_NARROW)], sem).wait()

    @pl.when(jnp.logical_not(is_narrow))
    def _():
        pltpu.make_async_copy(wide, got, sem).wait()


def slots_kernel(between, flags, table, field, intensity, probe, kernel, forms, shuffle, wide, *rest):
    narrow = rest[0] if between else wide
    back_wide, back_narrow = (rest[1], rest[2]) if between else (rest[0], rest[0])
    tiles, held, got, tile, measured, twice, beam, work, entered, chosen = rest[3 if between else 1 : -4]
    held_sem, int_sem, got_sem, tile_sem = rest[-4:]
    is_a = flags[0] == (1 if between else 0)
    is_narrow = jnp.logical_and(between, flags[1] == 1)
    mine = jnp.where(is_a, AT_A, AT_B)
    if between:
        fetch_pieces(is_narrow, wide, narrow, got, got_sem)
    else:
        pltpu.make_async_copy(wide, got, got_sem).start()
    fetch_columns(table, mine, field, held, held_sem, 0)

    def intensity_copies(j):
        return [
            pltpu.make_async_copy(
                intensity.at[j, :, pl.ds(part * LANES, LANES)], measured.at[j, part], int_sem.at[j, part]
            )
            for part in range(2)
        ]

    for j in range(CAP):

        @pl.when(jnp.logical_and(is_a, table[FIELDS * j] == AT_A))
        def _():
            for copy in intensity_copies(j):
                copy.start()

    for plane in range(2):
        for part in range(2):
            cut = probe[plane, :, part * LANES : (part + 1) * LANES]
            twice[2 * plane + part, :WIN] = cut
            twice[2 * plane + part, WIN:] = cut
    found = jnp.int32(0)
    for j in range(CAP):
        chosen[j] = 0
    for j in range(CAP):
        state = table[FIELDS * j]

        @pl.when(state == mine)
        def _():
            chosen[found] = j

        found = found + (state == mine).astype(jnp.int32)
    if between:
        await_pieces(is_narrow, wide, narrow, got, got_sem)
    else:
        pltpu.make_async_copy(wide, got, got_sem).wait()
    sublane = lax.broadcasted_iota(jnp.int32, (SUB, LANES), 0)

    def load(m, j):
        _, row, col, start, _ = slot_of(table, j)
        columns, starts, shift = near_columns(col)
        low = row // SUB
        high = (row + SUB - 1) // SUB
        base = jnp.where(is_a, start, start - low)

        def own_groups(group, carry):
            rows = pl.ds(pl.multiple_of(group * SUB, SUB), SUB)
            for plane in range(4):
                lf, rt = load_group(held.at[j], plane, group, starts, shift)
                tile[m, plane, rows, :LANES] = lf
                tile[m, plane, rows, LANES:] = rt
            return carry

        def their_groups(group, carry):
            rows = pl.ds(pl.multiple_of(group * SUB, SUB), SUB)
            for plane in range(4):
                tile[m, plane, rows, :] = got[base + group, plane]
            return carry

        lax.fori_loop(jnp.where(is_a, 0, low), jnp.where(is_a, high, GROUPS), their_groups, 0)
        lax.fori_loop(jnp.where(is_a, high, 0), jnp.where(is_a, GROUPS, low), own_groups, 0)

        @pl.when(low < high)
        def _():
            own = (low * SUB + sublane < row).astype(jnp.int32) == jnp.where(is_a, 0, 1)
            rows = pl.ds(pl.multiple_of(low * SUB, SUB), SUB)
            for plane in range(4):
                lf, rt = load_group(held.at[j], plane, low, starts, shift)
                tile[m, plane, rows, :LANES] = jnp.where(own, lf, tile[m, plane, rows, :LANES])
                tile[m, plane, rows, LANES:] = jnp.where(own, rt, tile[m, plane, rows, LANES:])

        @pl.when(jnp.logical_not(is_a))
        def _():
            after = start + GROUPS - low

            def unpack(group, carry):
                for plane in range(4):
                    rows = pl.ds(pl.multiple_of((group * 4 + plane) * SUB, SUB), SUB)
                    measured[j, 0, rows, :] = got[after + group, plane, :, :LANES]
                    measured[j, 1, rows, :] = got[after + group, plane, :, LANES:]
                return carry

            lax.fori_loop(0, INT_GROUPS, unpack, 0)

        for plane in range(2):
            parts = [twice[2 * plane + part, pl.ds(WIN - row, WIN), :] for part in range(2)]
            beam[m, plane] = pltpu.roll(jnp.concatenate(parts, axis=1), shift, 1)

    def arrive(j):
        columns, _, _ = near_columns(table[FIELDS * j + 2])
        pltpu.make_async_copy(field.at[:, :, columns], held.at[j], held_sem.at[j]).wait()

        @pl.when(is_a)
        def _():
            for copy in intensity_copies(j):
                copy.wait()

    def store_rows(m, e, o):
        work[m, 0, :HALF], work[m, 1, :HALF] = e[:HALF], e[HALF:]
        work[m, 0, HALF:], work[m, 1, HALF:] = o[:HALF], o[HALF:]

    def middle(pointwise, slots=None):
        for half in range(2):
            rows = pl.ds(half * HALF, HALF)
            for m in range(2):
                re, im = lanes_forward(work[m, 0, rows, :], work[m, 1, rows, :], forms)
                re, im = pointwise(m, half, rows, re, im, slots)
                re, im = lanes_inverse(re, im, forms)
                work[m, 0, rows, :], work[m, 1, rows, :] = re, im

    def rows_back(m):
        u, v = rows_inverse(work[m, 0], work[m, 1], forms)
        return (
            jnp.concatenate([u[:HALF] + v[:HALF], u[:HALF] - v[:HALF]], axis=0),
            jnp.concatenate([u[HALF:] + v[HALF:], u[HALF:] - v[HALF:]], axis=0),
        )

    def propagate(m, half, rows, re, im, slots):
        return cmul(kernel[0, rows, :], kernel[1, rows, :], re, im)

    def propagate_back(m, half, rows, re, im, slots):
        return cmul_conj(kernel[0, rows, :], kernel[1, rows, :], re, im)

    def residual(m, half, rows, re, im, slots):
        every = pl.ds(half, HALF, stride=2)
        at = slots[m]
        rows_of = jnp.concatenate([measured[at, 0, every, :], measured[at, 1, every, :]], axis=1)
        high, low = split(rows_of)
        wanted = jnp.dot(high, shuffle[...], preferred_element_type=f32)
        wanted += jnp.dot(low, shuffle[...], preferred_element_type=f32)
        scale = re * re + im * im - wanted
        return scale * re, scale * im

    def tile_copy(m, j):
        return pltpu.make_async_copy(tile.at[m], tiles.at[j], tile_sem.at[m])

    def write(m, j):
        _, row, _, _, back = slot_of(table, j)
        low = row // SUB

        def send(out, offset):
            def body(group, carry):
                rows = pl.ds(pl.multiple_of(group * SUB, SUB), SUB)
                for plane in range(4):
                    out[offset + group, plane] = tile[m, plane, rows, :]
                return carry

            return body

        tile_copy(m, j).start()

        offset = jnp.where(is_a, back, back - low)
        lower = jnp.where(is_a, 0, low)
        upper = jnp.where(is_a, (row + SUB - 1) // SUB, GROUPS)
        if between:

            @pl.when(is_narrow)
            def _():
                lax.fori_loop(lower, upper, send(back_narrow, offset), 0)

            @pl.when(jnp.logical_not(is_narrow))
            def _():
                lax.fori_loop(lower, upper, send(back_wide, offset), 0)

        else:
            lax.fori_loop(lower, upper, send(back_wide, offset), 0)

    def pair(p, carry):
        two = 2 * p + 1 < found
        first = chosen[2 * p]
        second = jnp.where(two, chosen[jnp.minimum(2 * p + 1, CAP - 1)], first)

        @pl.when(p > 0)
        def _():
            tile_copy(0, chosen[2 * p - 2]).wait()
            tile_copy(1, chosen[2 * p - 1]).wait()

        arrive(first)

        @pl.when(two)
        def _():
            arrive(second)

        load(0, first)
        load(1, second)
        for m in range(2):
            re, im = cmul(beam[m, 0], beam[m, 1], tile[m, 0], tile[m, 1])
            store_rows(m, *rows_forward(re, im, forms))
        middle(propagate)
        for m in range(2):
            re, im = rows_back(m)
            entered[m, 0], entered[m, 1] = re, im
            re, im = cmul(re, im, tile[m, 2], tile[m, 3])
            store_rows(m, *rows_forward(re, im, forms))
        middle(residual, (first, second))
        for m in range(2):
            br, bi = rows_back(m)
            re, im = cmul_conj(tile[m, 2], tile[m, 3], br, bi)
            tile[m, 2], tile[m, 3] = cmul_conj(entered[m, 0], entered[m, 1], br, bi)
            store_rows(m, *rows_forward(re, im, forms))
        middle(propagate_back)
        for m in range(2):
            br, bi = rows_back(m)
            tile[m, 0], tile[m, 1] = cmul_conj(beam[m, 0], beam[m, 1], br, bi)
        write(0, first)

        @pl.when(two)
        def _():
            write(1, second)

        return carry

    lax.fori_loop(0, (found + 1) // 2, pair, 0)

    @pl.when(found > 0)
    def _():
        tile_copy(0, 0).wait()

    @pl.when(jnp.logical_and(found > 0, jnp.bitwise_and(found, 1) == 0))
    def _():
        tile_copy(1, 0).wait()


def add_back(is_a, table, got, total, planes):
    theirs = jnp.where(is_a, AT_B, AT_A)
    for j in range(CAP):
        state, row, col, _, back = slot_of(table, j)

        @pl.when(state == theirs)
        def _():
            starts, shift = lane_blocks(col)
            low = row // SUB
            base = jnp.where(is_a, back - low, back)
            sublane = lax.broadcasted_iota(jnp.int32, (SUB, LANES), 0)

            def body(group, carry):
                below = (group * SUB + sublane < row).astype(jnp.int32)
                own = below == jnp.where(is_a, 0, 1)
                for plane in planes:
                    lf = jnp.where(own, got[base + group, plane, :, :LANES], 0.0)
                    rt = jnp.where(own, got[base + group, plane, :, LANES:], 0.0)
                    add_group(total, plane, group, starts, shift, lf, rt)
                return carry

            lax.fori_loop(jnp.where(is_a, low, 0), jnp.where(is_a, GROUPS, (row + SUB - 1) // SUB), body, 0)


def sum_kernel(
    flags, table_in, table_out, in_back, tiles_in, tiles_out, grad, total, got, tile, got_sem, tile_sem, total_sem
):
    pltpu.make_async_copy(in_back, got, got_sem).start()
    sublane = lax.broadcasted_iota(jnp.int32, (SUB, LANES), 0)
    kinds = ((flags[0] == 0, table_in, tiles_in), (flags[0] == 1, table_out, tiles_out))
    for k, (is_a, table, tiles) in enumerate(kinds):
        mine = jnp.where(is_a, AT_A, AT_B)
        for j in range(CAP):

            @pl.when(table[FIELDS * j] == mine)
            def _():
                pltpu.make_async_copy(tiles.at[j], tile.at[k * CAP + j], tile_sem.at[k * CAP + j]).start()

    @pl.when(flags[2] == 0)
    def _():
        total[...] = jnp.zeros_like(total)

    @pl.when(flags[2] > 0)
    def _():
        copy = pltpu.make_async_copy(grad, total, total_sem)
        copy.start()
        copy.wait()

    pltpu.make_async_copy(in_back, got, got_sem).wait()
    add_back(flags[0] == 0, table_in, got, total, range(4))
    for k, (is_a, table, tiles) in enumerate(kinds):
        mine = jnp.where(is_a, AT_A, AT_B)
        for j in range(CAP):
            state, row, col, _, _ = slot_of(table, j)

            @pl.when(state == mine)
            def _():
                at = k * CAP + j
                pltpu.make_async_copy(tiles.at[j], tile.at[at], tile_sem.at[at]).wait()
                starts, shift = lane_blocks(col)
                low = row // SUB

                def body(group, carry):
                    below = (group * SUB + sublane < row).astype(jnp.int32)
                    own = below == jnp.where(is_a, 0, 1)
                    rows = pl.ds(pl.multiple_of(group * SUB, SUB), SUB)
                    for plane in range(4):
                        lf = jnp.where(own, tile[at, plane, rows, :LANES], 0.0)
                        rt = jnp.where(own, tile[at, plane, rows, LANES:], 0.0)
                        add_group(total, plane, group, starts, shift, lf, rt)
                    return carry

                lax.fori_loop(
                    jnp.where(is_a, low, 0), jnp.where(is_a, GROUPS, (row + SUB - 1) // SUB), body, 0
                )


def finish_kernel(flags, table, total_in, wide, narrow, grad, total, got, got_sem, out_sem):
    is_narrow = flags[1] == 1
    fetch_pieces(is_narrow, wide, narrow, got, got_sem)
    await_pieces(is_narrow, wide, narrow, got, got_sem)
    for plane in range(4):
        total[plane] = total_in[plane]
        add_back(flags[0] == 1, table, got, total, (plane,))
        pltpu.make_async_copy(total.at[plane], grad.at[plane], out_sem.at[plane]).start()
    for plane in range(4):
        pltpu.make_async_copy(total.at[plane], grad.at[plane], out_sem.at[plane]).wait()


def spec(space):
    return pl.BlockSpec(memory_space=space)


def vmem(mib):
    return pltpu.CompilerParams(vmem_limit_bytes=mib << 20)


def packed(groups):
    return jax.ShapeDtypeStruct((groups, 4, SUB, WIN), f32)


def run_slots(flags, table, field, intensity, probe, kernel, tables, *pieces):
    between = len(pieces) == 2
    backs = (CAP_WIDE, CAP_NARROW)[: len(pieces)]
    return pl.pallas_call(
        functools.partial(slots_kernel, between),
        out_shape=tuple(packed(n) for n in backs) + (HB((CAP, 4, WIN, WIN), f32),),
        in_specs=[spec(SM)] * 2 + [spec(HB)] * 2 + [spec(VM)] * 4 + [spec(pl.ANY)] * len(pieces),
        out_specs=(spec(VM),) * len(backs) + (spec(HB),),
        scratch_shapes=[
            pltpu.VMEM((CAP, 4, WIN, WIDE), f32),
            pltpu.VMEM((CAP_WIDE, 4, SUB, WIN), f32),
            pltpu.VMEM((2, 4, WIN, WIN), f32),
            pltpu.VMEM((CAP, 2, WIN, LANES), f32),
            pltpu.VMEM((4, 2 * WIN, LANES), f32),
            pltpu.VMEM((2, 2, WIN, WIN), f32),
            pltpu.VMEM((2, 2, WIN, WIN), f32),
            pltpu.VMEM((2, 2, WIN, WIN), f32),
            pltpu.SMEM((CAP,), jnp.int32),
            pltpu.SemaphoreType.DMA((CAP,)),
            pltpu.SemaphoreType.DMA((CAP, 2)),
            pltpu.SemaphoreType.DMA,
            pltpu.SemaphoreType.DMA((2,)),
        ],
        cost_estimate=CHEAP,
        compiler_params=vmem(32),
    )(flags, table, field, intensity, probe, kernel, *tables, *pieces)


def both_ways(pairs):
    return pairs + [(b, a) for a, b in pairs]


def everywhere(value, after):
    axes = ("groups", "row")
    value = pl.pallas_call(
        note_kernel,
        out_shape=jax.ShapeDtypeStruct((SUB, LANES), jnp.int32),
        in_specs=[spec(SM), spec(HB)],
        out_specs=spec(VM),
        cost_estimate=CHEAP,
    )(value.reshape(1), after)
    count = lax.axis_size("groups") * lax.axis_size("row")
    copies = jnp.broadcast_to(value[None, :1], (count, 1, LANES))
    return jnp.max(lax.all_to_all(copies, axes, 0, 0, tiled=True))


def note_kernel(value, after, out):
    del after
    out[...] = jnp.full(out.shape, value[0], jnp.int32)


def one_round(turn, grad, left_over, field, maps, intensity, probe_wave, prop_phase, own, before):
    count = lax.axis_size("row")
    within = both_ways([(i, i + 1) for i in range(0, count - 1, 2)])
    wide_pairs = both_ways([(i, i + 1) for i in range(1, count - 1, 4)])
    narrow_pairs = both_ways([(i, i + 1) for i in range(3, count - 1, 4)])
    move = lambda x, pairs: lax.ppermute(x, "row", pairs)
    place = lax.axis_index("row")
    odd = jnp.bitwise_and(place, 1)
    is_narrow = (jnp.bitwise_and(place + 1, 2) == 0).astype(jnp.int32)
    flags = jnp.stack([odd, is_narrow, turn])

    table = jax.ShapeDtypeStruct((CAP * FIELDS,), jnp.int32)
    inner, wide, narrow, table_in, table_out = pl.pallas_call(
        pack_kernel,
        out_shape=(packed(CAP_WIDE), packed(CAP_WIDE), packed(CAP_NARROW), table, table),
        in_specs=[spec(SM)] * 3 + [spec(HB)] * 2,
        out_specs=(spec(VM),) * 3 + (spec(SM),) * 2,
        scratch_shapes=[
            pltpu.VMEM((2 * CAP, 4, WIN, WIDE), f32),
            pltpu.SemaphoreType.DMA((2 * CAP,)),
            pltpu.SemaphoreType.DMA((CAP,)),
        ],
        cost_estimate=CHEAP,
        compiler_params=vmem(24),
    )(flags, own, before, field, maps)
    wide = move(wide, wide_pairs)
    narrow = move(narrow, narrow_pairs)
    inner = move(inner, within)

    forms, shuffle = (jnp.asarray(t) for t in make_tables())
    kernel = pl.pallas_call(
        prepare_kernel,
        out_shape=jax.ShapeDtypeStruct((2, WIN, WIN), f32),
        in_specs=[spec(VM)] * 2,
        out_specs=spec(VM),
        scratch_shapes=[pltpu.VMEM((2, WIN, LANES), f32)],
        cost_estimate=CHEAP,
        compiler_params=vmem(8),
    )(jnp.stack([jnp.cos(prop_phase), jnp.sin(prop_phase)]), shuffle)

    args = (field, intensity, probe_wave, kernel, (forms, shuffle))
    in_back, tiles_in = run_slots(flags, table_in, *args, inner)
    in_back = move(in_back, within)
    back_wide, back_narrow, tiles_out = run_slots(flags, table_out, *args, wide, narrow)
    tiles_in = pltpu.with_memory_space_constraint(tiles_in, HB)
    tiles_out = pltpu.with_memory_space_constraint(tiles_out, HB)
    again = everywhere(left_over * (1 - turn), tiles_out)
    back_wide = move(back_wide, wide_pairs)
    back_narrow = move(back_narrow, narrow_pairs)
    total = pl.pallas_call(
        sum_kernel,
        out_shape=jax.ShapeDtypeStruct(field.shape, f32),
        in_specs=[spec(SM)] * 3 + [spec(pl.ANY)] * 3 + [spec(HB)],
        out_specs=spec(VM),
        scratch_shapes=[
            pltpu.VMEM((CAP_WIDE, 4, SUB, WIN), f32),
            pltpu.VMEM((2 * CAP, 4, WIN, WIN), f32),
            pltpu.SemaphoreType.DMA,
            pltpu.SemaphoreType.DMA((2 * CAP,)),
            pltpu.SemaphoreType.DMA,
        ],
        cost_estimate=CHEAP,
        compiler_params=vmem(20),
    )(flags, table_in, table_out, in_back, tiles_in, tiles_out, grad)
    grad = pl.pallas_call(
        finish_kernel,
        out_shape=jax.ShapeDtypeStruct(field.shape, f32),
        in_specs=[spec(SM)] * 2 + [spec(VM)] + [spec(pl.ANY)] * 2,
        out_specs=spec(HB),
        scratch_shapes=[
            pltpu.VMEM(field.shape, f32),
            pltpu.VMEM((CAP_WIDE, 4, SUB, WIN), f32),
            pltpu.SemaphoreType.DMA,
            pltpu.SemaphoreType.DMA((4,)),
        ],
        cost_estimate=CHEAP,
        compiler_params=vmem(16),
    )(flags, table_out, total, back_wide, back_narrow)
    return grad, again


def shards(obj_field, probe_wave, prop_phase, win_offsets, live_counts, intensity):
    field = pltpu.with_memory_space_constraint(obj_field.reshape((4,) + obj_field.shape[2:]), HB)
    maps = pltpu.with_memory_space_constraint(intensity.reshape(CAP, INT_GROUPS, 4, SUB, WIN), HB)
    intensity = pltpu.with_memory_space_constraint(intensity, HB)
    count = lax.axis_size("row")
    own = jnp.concatenate([win_offsets.reshape(-1), live_counts, jnp.zeros((INFO - 2 * CAP - 1,), jnp.int32)])
    before = lax.ppermute(own, "row", [(i, i + 1) for i in range(count - 1)])
    narrow_first = jnp.bitwise_and(lax.axis_index("row"), 3) == 3
    left_over = jnp.logical_and(narrow_first, live_counts[0] > NARROW_SLOTS).astype(jnp.int32)

    def body(state):
        turn, _, grad = state
        grad, again = one_round(turn, grad, left_over, field, maps, intensity, probe_wave, prop_phase, own, before)
        return turn + 1, again, grad

    empty = pl.pallas_call(
        lambda out: None,
        out_shape=jax.ShapeDtypeStruct(field.shape, f32),
        out_specs=spec(HB),
    )()
    _, _, grad = lax.while_loop(lambda state: state[1] > 0, body, (jnp.int32(0), jnp.int32(1), empty))
    return grad.reshape(obj_field.shape)


def solution(mesh):
    in_specs = (
        P(None, None, ("groups", "row"), None),
        P("groups", None, None),
        P(),
        P(("groups", "row"), None),
        P(("groups", "row")),
        P(("groups", "row"), None, None),
    )
    out_specs = P(None, None, ("groups", "row"), None)
    return jax.shard_map(shards, mesh=mesh, in_specs=in_specs, out_specs=out_specs, check_vma=False)
```

```python
import functools

import jax
import jax.numpy as jnp
import numpy as np
from jax import lax
from jax.experimental import pallas as pl
from jax.experimental.pallas import tpu as pltpu
from jax.sharding import PartitionSpec as P

WIN = 256
HALF = WIN // 2
LANES = 128
SUB = 8
CAP = 4
GROUPS = WIN // SUB
INT_GROUPS = GROUPS // 4
CAP_WIDE = 48
CAP_NARROW = 28
NARROW_SLOTS = 2
UNEVEN = 24
DEAD, AT_A, AT_B = 0, 1, 2
FIELDS = 8
f32 = jnp.float32
bf16 = jnp.bfloat16
VM = pltpu.MemorySpace.VMEM
SM = pltpu.MemorySpace.SMEM
HB = pltpu.MemorySpace.HBM
CHEAP = pl.CostEstimate(flops=1, transcendentals=0, bytes_accessed=1)


def real_tables():
    k = np.arange(HALF)[:, None]
    n = np.arange(HALF)[None, :]
    out = []
    for odd in (0, 1):
        angle = 2.0 * np.pi * (((2 * k + odd) * n) % WIN) / WIN
        c, s = np.cos(angle) / 16.0, np.sin(angle) / 16.0
        out.append(np.block([[c, s], [-s, c]]))
    return out


def high_low(table):
    high = table.astype(np.float32).astype(bf16)
    low = (table - high.astype(np.float64)).astype(np.float32).astype(bf16)
    return high, low


def make_tables():
    even, odd = real_tables()
    forms = np.stack([np.stack(high_low(m)) for m in (even, odd, even.T, odd.T)])
    order = np.concatenate([np.arange(0, WIN, 2), np.arange(1, WIN, 2)])
    shuffle = np.zeros((WIN, WIN), np.float32)
    shuffle[order, np.arange(WIN)] = 1.0
    return forms, shuffle.astype(bf16)


EVEN, ODD, EVEN_T, ODD_T = range(4)


def split(x):
    high = x.astype(bf16)
    return high, (x - high.astype(f32)).astype(bf16)


def left_mul(forms, which, x):
    high, low = split(x)
    t_high, t_low = forms[which, 0], forms[which, 1]
    wide = jnp.concatenate([t_high, t_low, t_high], axis=1)
    return jnp.dot(wide, jnp.concatenate([high, high, low], axis=0), preferred_element_type=f32)


def right_mul(x, forms, which):
    high, low = split(x)
    t_high, t_low = forms[which, 0], forms[which, 1]
    tall = jnp.concatenate([t_high, t_high, t_low], axis=0)
    return jnp.dot(jnp.concatenate([high, low, high], axis=1), tall, preferred_element_type=f32)


def rows_forward(re, im, forms):
    tr, br, ti, bi = re[:HALF], re[HALF:], im[:HALF], im[HALF:]
    e = left_mul(forms, EVEN, jnp.concatenate([tr + br, ti + bi], axis=0))
    o = left_mul(forms, ODD, jnp.concatenate([tr - br, ti - bi], axis=0))
    return e, o


def rows_inverse(re, im, forms):
    u = left_mul(forms, EVEN_T, jnp.concatenate([re[:HALF], im[:HALF]], axis=0))
    v = left_mul(forms, ODD_T, jnp.concatenate([re[HALF:], im[HALF:]], axis=0))
    return u, v


def lanes_forward(re, im, forms):
    lr, rr, li, ri = re[:, :HALF], re[:, HALF:], im[:, :HALF], im[:, HALF:]
    e = right_mul(jnp.concatenate([lr + rr, li + ri], axis=1), forms, EVEN_T)
    o = right_mul(jnp.concatenate([lr - rr, li - ri], axis=1), forms, ODD_T)
    return (
        jnp.concatenate([e[:, :HALF], o[:, :HALF]], axis=1),
        jnp.concatenate([e[:, HALF:], o[:, HALF:]], axis=1),
    )


def lanes_inverse(re, im, forms):
    u = right_mul(jnp.concatenate([re[:, :HALF], im[:, :HALF]], axis=1), forms, EVEN)
    v = right_mul(jnp.concatenate([re[:, HALF:], im[:, HALF:]], axis=1), forms, ODD)
    return (
        jnp.concatenate([u[:, :HALF] + v[:, :HALF], u[:, :HALF] - v[:, :HALF]], axis=1),
        jnp.concatenate([u[:, HALF:] + v[:, HALF:], u[:, HALF:] - v[:, HALF:]], axis=1),
    )


def cmul(ar, ai, br, bi):
    return ar * br - ai * bi, ar * bi + ai * br


def cmul_conj(ar, ai, br, bi):
    return ar * br + ai * bi, ar * bi - ai * br


INFO = 16


def decide(info, table, first_slot, last_slot, cap):
    count = info[2 * CAP]
    rows = [jnp.bitwise_and(info[2 * j], WIN - 1) for j in range(CAP)]
    last_slot = jnp.minimum(last_slot, count)
    used = [jnp.logical_and(j >= first_slot, j < last_slot).astype(jnp.int32) for j in range(CAP)]
    on_a = [used[j] * ((rows[j] + SUB - 1) // SUB) for j in range(CAP)]
    on_b = [used[j] * (GROUPS - rows[j] // SUB + INT_GROUPS) for j in range(CAP)]
    best, chosen = jnp.int32(10000), jnp.int32(0)
    for mask in range(1 << CAP):
        total_a = jnp.int32(0)
        total_b = jnp.int32(0)
        slots_a = jnp.int32(0)
        slots_b = jnp.int32(0)
        for j in range(CAP):
            if mask >> j & 1:
                total_b = total_b + on_b[j]
                slots_b = slots_b + used[j]
            else:
                total_a = total_a + on_a[j]
                slots_a = slots_a + used[j]
        cost = jnp.maximum(total_a, total_b)
        cost = cost + jnp.where(cost > cap, 1000, 0)
        cost = cost + jnp.where(jnp.maximum(slots_a, slots_b) > 2, UNEVEN, 0)
        better = cost < best
        best = jnp.where(better, cost, best)
        chosen = jnp.where(better, mask, chosen)
    at_a = jnp.int32(0)
    at_b = jnp.int32(0)
    back = jnp.int32(0)
    for j in range(CAP):
        to_b = jnp.bitwise_and(chosen >> j, 1) * used[j]
        to_b = jnp.where(rows[j] == 0, 0, to_b)
        to_a = used[j] - to_b
        table[FIELDS * j] = to_a * AT_A + to_b * AT_B
        table[FIELDS * j + 1] = rows[j]
        table[FIELDS * j + 2] = info[2 * j + 1]
        table[FIELDS * j + 3] = jnp.where(to_b == 1, at_b, at_a)
        table[FIELDS * j + 4] = jnp.where(to_b == 1, back, at_a)
        at_a = at_a + to_a * on_a[j]
        at_b = at_b + to_b * on_b[j]
        back = back + to_b * (on_b[j] - INT_GROUPS)


def slot_of(table, j):
    base = FIELDS * j
    return table[base], table[base + 1], table[base + 2], table[base + 3], table[base + 4]


def lane_blocks(col):
    first = col // LANES
    starts = [jnp.minimum(first + k, 7) * LANES for k in range(3)]
    return [pl.multiple_of(start, LANES) for start in starts], jnp.bitwise_and(col, LANES - 1)


WIDE = 3 * LANES


def near_columns(col):
    first = jnp.minimum(col // LANES, 5)
    skip = col // LANES - first
    starts = [pl.multiple_of(jnp.minimum(skip + k, 2) * LANES, LANES) for k in range(3)]
    return pl.ds(pl.multiple_of(first * LANES, LANES), WIDE), starts, jnp.bitwise_and(col, LANES - 1)


def lane_iota():
    return lax.broadcasted_iota(jnp.int32, (SUB, LANES), 1)


def load_group(field, plane, group, starts, shift):
    rows = pl.ds(pl.multiple_of(group * SUB, SUB), SUB)
    first = field[plane, rows, pl.ds(starts[0], LANES)]
    second = field[plane, rows, pl.ds(starts[1], LANES)]
    third = field[plane, rows, pl.ds(starts[2], LANES)]
    return jnp.where(lane_iota() >= shift, first, third), second


def add_group(total, plane, group, starts, shift, left, right):
    rows = pl.ds(pl.multiple_of(group * SUB, SUB), SUB)
    inside = lane_iota() >= shift
    total[plane, rows, pl.ds(starts[0], LANES)] += jnp.where(inside, left, 0.0)
    total[plane, rows, pl.ds(starts[1], LANES)] += right
    total[plane, rows, pl.ds(starts[2], LANES)] += jnp.where(inside, 0.0, left)


def fetch_columns(table, wanted, field, held, sem, base):
    for j in range(CAP):

        @pl.when(table[FIELDS * j] == wanted)
        def _():
            columns, _, _ = near_columns(table[FIELDS * j + 2])
            pltpu.make_async_copy(field.at[:, :, columns], held.at[base + j], sem.at[base + j]).start()


def copy_groups(held, out, at, offset, low, high, starts, shift):
    def body(group, carry):
        for plane in range(4):
            left, right = load_group(held.at[at], plane, group, starts, shift)
            out[offset + group, plane, :, :LANES] = left
            out[offset + group, plane, :, LANES:] = right
        return carry

    lax.fori_loop(low, high, body, 0)


def pack_to_b(table, field, intensity, out, held, sem, int_sem, base):
    def intensity_copy(j):
        _, row, _, start, _ = slot_of(table, j)
        after = start + GROUPS - row // SUB
        return pltpu.make_async_copy(intensity.at[j], out.at[pl.ds(after, INT_GROUPS)], int_sem.at[j])

    for j in range(CAP):

        @pl.when(table[FIELDS * j] == AT_B)
        def _():
            intensity_copy(j).start()

    for j in range(CAP):
        state, row, col, start, _ = slot_of(table, j)

        @pl.when(state == AT_B)
        def _():
            columns, starts, shift = near_columns(col)
            at = base + j
            pltpu.make_async_copy(field.at[:, :, columns], held.at[at], sem.at[at]).wait()
            copy_groups(held, out, at, start - row // SUB, row // SUB, GROUPS, starts, shift)
            intensity_copy(j).wait()


def pack_to_a(table, field, out, held, sem, base):
    for j in range(CAP):
        state, row, col, start, _ = slot_of(table, j)

        @pl.when(state == AT_A)
        def _():
            columns, starts, shift = near_columns(col)
            at = base + j
            pltpu.make_async_copy(field.at[:, :, columns], held.at[at], sem.at[at]).wait()
            copy_groups(held, out, at, start, 0, (row + SUB - 1) // SUB, starts, shift)


def pack_kernel(
    flags, own, before, field, intensity, inner, wide, narrow, note, table_in, table_out, held, sem, int_sem
):
    turn = flags[2]
    is_narrow = flags[1] == 1
    note[...] = jnp.full(note.shape, flags[3], jnp.int32)
    first_slot = jnp.where(is_narrow, NARROW_SLOTS * turn, CAP * turn)
    last_slot = jnp.where(is_narrow, NARROW_SLOTS * (turn + 1), CAP)
    cap = jnp.where(is_narrow, CAP_NARROW, CAP_WIDE)

    def outward(pack):
        @pl.when(is_narrow)
        def _():
            pack(narrow)

        @pl.when(jnp.logical_not(is_narrow))
        def _():
            pack(wide)

    @pl.when(flags[0] == 0)
    def _():
        decide(before, table_out, first_slot, last_slot, cap)
        fetch_columns(table_out, AT_A, field, held, sem, 0)
        decide(own, table_in, CAP * turn, CAP, CAP_WIDE)
        fetch_columns(table_in, AT_B, field, held, sem, CAP)
        outward(lambda out: pack_to_a(table_out, field, out, held, sem, 0))
        pack_to_b(table_in, field, intensity, inner, held, sem, int_sem, CAP)

    @pl.when(flags[0] == 1)
    def _():
        decide(own, table_out, first_slot, last_slot, cap)
        fetch_columns(table_out, AT_B, field, held, sem, 0)
        decide(before, table_in, CAP * turn, CAP, CAP_WIDE)
        fetch_columns(table_in, AT_A, field, held, sem, CAP)
        outward(lambda out: pack_to_b(table_out, field, intensity, out, held, sem, int_sem, 0))
        pack_to_a(table_in, field, inner, held, sem, CAP)


def prepare_kernel(phases, shuffle, out, halves):
    for plane in range(2):
        halves[0] = phases[plane, :, :LANES]
        halves[1] = phases[plane, :, LANES:]
        for part in range(2):
            every = pl.ds(part, HALF, stride=2)
            x = jnp.concatenate([halves[0, every, :], halves[1, every, :]], axis=1)
            high = x.astype(bf16)
            rest = x - high.astype(f32)
            middle, low = split(rest)
            total = jnp.dot(high, shuffle[...], preferred_element_type=f32)
            total += jnp.dot(middle, shuffle[...], preferred_element_type=f32)
            total += jnp.dot(low, shuffle[...], preferred_element_type=f32)
            out[plane, part * HALF : (part + 1) * HALF, :] = total


def fetch_pieces(is_narrow, wide, narrow, got, sem):
    @pl.when(is_narrow)
    def _():
        pltpu.make_async_copy(narrow, got.at[pl.ds(0, CAP_NARROW)], sem).start()

    @pl.when(jnp.logical_not(is_narrow))
    def _():
        pltpu.make_async_copy(wide, got, sem).start()


def await_pieces(is_narrow, wide, narrow, got, sem):
    @pl.when(is_narrow)
    def _():
        pltpu.make_async_copy(narrow, got.at[pl.ds(0, CAP_NARROW)], sem).wait()

    @pl.when(jnp.logical_not(is_narrow))
    def _():
        pltpu.make_async_copy(wide, got, sem).wait()


def slots_kernel(between, flags, table, field, intensity, probe, kernel, forms, shuffle, wide, *rest):
    narrow = rest[0] if between else wide
    back_wide, back_narrow = (rest[1], rest[2]) if between else (rest[0], rest[0])
    tiles, held, got, tile, measured, twice, beam, work, entered, chosen = rest[3 if between else 1 : -4]
    held_sem, int_sem, got_sem, tile_sem = rest[-4:]
    is_a = flags[0] == (1 if between else 0)
    is_narrow = jnp.logical_and(between, flags[1] == 1)
    mine = jnp.where(is_a, AT_A, AT_B)
    if between:
        fetch_pieces(is_narrow, wide, narrow, got, got_sem)
    else:
        pltpu.make_async_copy(wide, got, got_sem).start()
    fetch_columns(table, mine, field, held, held_sem, 0)

    def intensity_copies(j):
        return [
            pltpu.make_async_copy(
                intensity.at[j, :, pl.ds(part * LANES, LANES)], measured.at[j, part], int_sem.at[j, part]
            )
            for part in range(2)
        ]

    for j in range(CAP):

        @pl.when(jnp.logical_and(is_a, table[FIELDS * j] == AT_A))
        def _():
            for copy in intensity_copies(j):
                copy.start()

    for plane in range(2):
        for part in range(2):
            cut = probe[plane, :, part * LANES : (part + 1) * LANES]
            twice[2 * plane + part, :WIN] = cut
            twice[2 * plane + part, WIN:] = cut
    found = jnp.int32(0)
    for j in range(CAP):
        chosen[j] = 0
    for j in range(CAP):
        state = table[FIELDS * j]

        @pl.when(state == mine)
        def _():
            chosen[found] = j

        found = found + (state == mine).astype(jnp.int32)
    if between:
        await_pieces(is_narrow, wide, narrow, got, got_sem)
    else:
        pltpu.make_async_copy(wide, got, got_sem).wait()
    sublane = lax.broadcasted_iota(jnp.int32, (SUB, LANES), 0)

    def load(m, j):
        _, row, col, start, _ = slot_of(table, j)
        columns, starts, shift = near_columns(col)
        low = row // SUB
        high = (row + SUB - 1) // SUB
        base = jnp.where(is_a, start, start - low)

        def own_groups(group, carry):
            rows = pl.ds(pl.multiple_of(group * SUB, SUB), SUB)
            for plane in range(4):
                lf, rt = load_group(held.at[j], plane, group, starts, shift)
                tile[m, plane, rows, :LANES] = lf
                tile[m, plane, rows, LANES:] = rt
            return carry

        def their_groups(group, carry):
            rows = pl.ds(pl.multiple_of(group * SUB, SUB), SUB)
            for plane in range(4):
                tile[m, plane, rows, :] = got[base + group, plane]
            return carry

        lax.fori_loop(jnp.where(is_a, 0, low), jnp.where(is_a, high, GROUPS), their_groups, 0)
        lax.fori_loop(jnp.where(is_a, high, 0), jnp.where(is_a, GROUPS, low), own_groups, 0)

        @pl.when(low < high)
        def _():
            own = (low * SUB + sublane < row).astype(jnp.int32) == jnp.where(is_a, 0, 1)
            rows = pl.ds(pl.multiple_of(low * SUB, SUB), SUB)
            for plane in range(4):
                lf, rt = load_group(held.at[j], plane, low, starts, shift)
                tile[m, plane, rows, :LANES] = jnp.where(own, lf, tile[m, plane, rows, :LANES])
                tile[m, plane, rows, LANES:] = jnp.where(own, rt, tile[m, plane, rows, LANES:])

        @pl.when(jnp.logical_not(is_a))
        def _():
            after = start + GROUPS - low

            def unpack(group, carry):
                for plane in range(4):
                    rows = pl.ds(pl.multiple_of((group * 4 + plane) * SUB, SUB), SUB)
                    measured[j, 0, rows, :] = got[after + group, plane, :, :LANES]
                    measured[j, 1, rows, :] = got[after + group, plane, :, LANES:]
                return carry

            lax.fori_loop(0, INT_GROUPS, unpack, 0)

        for plane in range(2):
            parts = [twice[2 * plane + part, pl.ds(WIN - row, WIN), :] for part in range(2)]
            beam[m, plane] = pltpu.roll(jnp.concatenate(parts, axis=1), shift, 1)

    def arrive(j):
        columns, _, _ = near_columns(table[FIELDS * j + 2])
        pltpu.make_async_copy(field.at[:, :, columns], held.at[j], held_sem.at[j]).wait()

        @pl.when(is_a)
        def _():
            for copy in intensity_copies(j):
                copy.wait()

    def store_rows(m, e, o):
        work[m, 0, :HALF], work[m, 1, :HALF] = e[:HALF], e[HALF:]
        work[m, 0, HALF:], work[m, 1, HALF:] = o[:HALF], o[HALF:]

    def middle(pointwise, slots=None):
        for half in range(2):
            rows = pl.ds(half * HALF, HALF)
            for m in range(2):
                re, im = lanes_forward(work[m, 0, rows, :], work[m, 1, rows, :], forms)
                re, im = pointwise(m, half, rows, re, im, slots)
                re, im = lanes_inverse(re, im, forms)
                work[m, 0, rows, :], work[m, 1, rows, :] = re, im

    def rows_back(m):
        u, v = rows_inverse(work[m, 0], work[m, 1], forms)
        return (
            jnp.concatenate([u[:HALF] + v[:HALF], u[:HALF] - v[:HALF]], axis=0),
            jnp.concatenate([u[HALF:] + v[HALF:], u[HALF:] - v[HALF:]], axis=0),
        )

    def propagate(m, half, rows, re, im, slots):
        return cmul(kernel[0, rows, :], kernel[1, rows, :], re, im)

    def propagate_back(m, half, rows, re, im, slots):
        return cmul_conj(kernel[0, rows, :], kernel[1, rows, :], re, im)

    def residual(m, half, rows, re, im, slots):
        every = pl.ds(half, HALF, stride=2)
        at = slots[m]
        rows_of = jnp.concatenate([measured[at, 0, every, :], measured[at, 1, every, :]], axis=1)
        high, low = split(rows_of)
        wanted = jnp.dot(high, shuffle[...], preferred_element_type=f32)
        wanted += jnp.dot(low, shuffle[...], preferred_element_type=f32)
        scale = re * re + im * im - wanted
        return scale * re, scale * im

    def tile_copy(m, j):
        return pltpu.make_async_copy(tile.at[m], tiles.at[j], tile_sem.at[m])

    def write(m, j):
        _, row, _, _, back = slot_of(table, j)
        low = row // SUB

        def send(out, offset):
            def body(group, carry):
                rows = pl.ds(pl.multiple_of(group * SUB, SUB), SUB)
                for plane in range(4):
                    out[offset + group, plane] = tile[m, plane, rows, :]
                return carry

            return body

        tile_copy(m, j).start()

        offset = jnp.where(is_a, back, back - low)
        lower = jnp.where(is_a, 0, low)
        upper = jnp.where(is_a, (row + SUB - 1) // SUB, GROUPS)
        if between:

            @pl.when(is_narrow)
            def _():
                lax.fori_loop(lower, upper, send(back_narrow, offset), 0)

            @pl.when(jnp.logical_not(is_narrow))
            def _():
                lax.fori_loop(lower, upper, send(back_wide, offset), 0)

        else:
            lax.fori_loop(lower, upper, send(back_wide, offset), 0)

    def pair(p, carry):
        two = 2 * p + 1 < found
        first = chosen[2 * p]
        second = jnp.where(two, chosen[jnp.minimum(2 * p + 1, CAP - 1)], first)

        @pl.when(p > 0)
        def _():
            tile_copy(0, chosen[2 * p - 2]).wait()
            tile_copy(1, chosen[2 * p - 1]).wait()

        arrive(first)

        @pl.when(two)
        def _():
            arrive(second)

        load(0, first)
        load(1, second)
        for m in range(2):
            re, im = cmul(beam[m, 0], beam[m, 1], tile[m, 0], tile[m, 1])
            store_rows(m, *rows_forward(re, im, forms))
        middle(propagate)
        for m in range(2):
            re, im = rows_back(m)
            entered[m, 0], entered[m, 1] = re, im
            re, im = cmul(re, im, tile[m, 2], tile[m, 3])
            store_rows(m, *rows_forward(re, im, forms))
        middle(residual, (first, second))
        for m in range(2):
            br, bi = rows_back(m)
            re, im = cmul_conj(tile[m, 2], tile[m, 3], br, bi)
            tile[m, 2], tile[m, 3] = cmul_conj(entered[m, 0], entered[m, 1], br, bi)
            store_rows(m, *rows_forward(re, im, forms))
        middle(propagate_back)
        for m in range(2):
            br, bi = rows_back(m)
            tile[m, 0], tile[m, 1] = cmul_conj(beam[m, 0], beam[m, 1], br, bi)
        write(0, first)

        @pl.when(two)
        def _():
            write(1, second)

        return carry

    lax.fori_loop(0, (found + 1) // 2, pair, 0)

    @pl.when(found > 0)
    def _():
        tile_copy(0, 0).wait()

    @pl.when(jnp.logical_and(found > 0, jnp.bitwise_and(found, 1) == 0))
    def _():
        tile_copy(1, 0).wait()


def add_back(is_a, table, got, total, planes):
    theirs = jnp.where(is_a, AT_B, AT_A)
    for j in range(CAP):
        state, row, col, _, back = slot_of(table, j)

        @pl.when(state == theirs)
        def _():
            starts, shift = lane_blocks(col)
            low = row // SUB
            base = jnp.where(is_a, back - low, back)
            sublane = lax.broadcasted_iota(jnp.int32, (SUB, LANES), 0)

            def body(group, carry):
                below = (group * SUB + sublane < row).astype(jnp.int32)
                own = below == jnp.where(is_a, 0, 1)
                for plane in planes:
                    lf = jnp.where(own, got[base + group, plane, :, :LANES], 0.0)
                    rt = jnp.where(own, got[base + group, plane, :, LANES:], 0.0)
                    add_group(total, plane, group, starts, shift, lf, rt)
                return carry

            lax.fori_loop(jnp.where(is_a, low, 0), jnp.where(is_a, GROUPS, (row + SUB - 1) // SUB), body, 0)


def sum_kernel(
    flags, table_in, table_out, in_back, tiles_in, tiles_out, grad, total, got, tile, got_sem, tile_sem, total_sem
):
    pltpu.make_async_copy(in_back, got, got_sem).start()
    sublane = lax.broadcasted_iota(jnp.int32, (SUB, LANES), 0)
    kinds = ((flags[0] == 0, table_in, tiles_in), (flags[0] == 1, table_out, tiles_out))
    for k, (is_a, table, tiles) in enumerate(kinds):
        mine = jnp.where(is_a, AT_A, AT_B)
        for j in range(CAP):

            @pl.when(table[FIELDS * j] == mine)
            def _():
                pltpu.make_async_copy(tiles.at[j], tile.at[k * CAP + j], tile_sem.at[k * CAP + j]).start()

    @pl.when(flags[2] == 0)
    def _():
        total[...] = jnp.zeros_like(total)

    @pl.when(flags[2] > 0)
    def _():
        copy = pltpu.make_async_copy(grad, total, total_sem)
        copy.start()
        copy.wait()

    pltpu.make_async_copy(in_back, got, got_sem).wait()
    add_back(flags[0] == 0, table_in, got, total, range(4))
    for k, (is_a, table, tiles) in enumerate(kinds):
        mine = jnp.where(is_a, AT_A, AT_B)
        for j in range(CAP):
            state, row, col, _, _ = slot_of(table, j)

            @pl.when(state == mine)
            def _():
                at = k * CAP + j
                pltpu.make_async_copy(tiles.at[j], tile.at[at], tile_sem.at[at]).wait()
                starts, shift = lane_blocks(col)
                low = row // SUB

                def body(group, carry):
                    below = (group * SUB + sublane < row).astype(jnp.int32)
                    own = below == jnp.where(is_a, 0, 1)
                    rows = pl.ds(pl.multiple_of(group * SUB, SUB), SUB)
                    for plane in range(4):
                        lf = jnp.where(own, tile[at, plane, rows, :LANES], 0.0)
                        rt = jnp.where(own, tile[at, plane, rows, LANES:], 0.0)
                        add_group(total, plane, group, starts, shift, lf, rt)
                    return carry

                lax.fori_loop(
                    jnp.where(is_a, low, 0), jnp.where(is_a, GROUPS, (row + SUB - 1) // SUB), body, 0
                )


def finish_kernel(flags, table, total_in, wide, narrow, grad, total, got, got_sem, out_sem):
    is_narrow = flags[1] == 1
    fetch_pieces(is_narrow, wide, narrow, got, got_sem)
    await_pieces(is_narrow, wide, narrow, got, got_sem)
    for plane in range(4):
        total[plane] = total_in[plane]
        add_back(flags[0] == 1, table, got, total, (plane,))
        pltpu.make_async_copy(total.at[plane], grad.at[plane], out_sem.at[plane]).start()
    for plane in range(4):
        pltpu.make_async_copy(total.at[plane], grad.at[plane], out_sem.at[plane]).wait()


def spec(space):
    return pl.BlockSpec(memory_space=space)


def vmem(mib):
    return pltpu.CompilerParams(vmem_limit_bytes=mib << 20)


def packed(groups):
    return jax.ShapeDtypeStruct((groups, 4, SUB, WIN), f32)


def run_slots(flags, table, field, intensity, probe, kernel, tables, *pieces):
    between = len(pieces) == 2
    backs = (CAP_WIDE, CAP_NARROW)[: len(pieces)]
    return pl.pallas_call(
        functools.partial(slots_kernel, between),
        out_shape=tuple(packed(n) for n in backs) + (HB((CAP, 4, WIN, WIN), f32),),
        in_specs=[spec(SM)] * 2 + [spec(HB)] * 2 + [spec(VM)] * 4 + [spec(pl.ANY)] * len(pieces),
        out_specs=(spec(VM),) * len(backs) + (spec(HB),),
        scratch_shapes=[
            pltpu.VMEM((CAP, 4, WIN, WIDE), f32),
            pltpu.VMEM((CAP_WIDE, 4, SUB, WIN), f32),
            pltpu.VMEM((2, 4, WIN, WIN), f32),
            pltpu.VMEM((CAP, 2, WIN, LANES), f32),
            pltpu.VMEM((4, 2 * WIN, LANES), f32),
            pltpu.VMEM((2, 2, WIN, WIN), f32),
            pltpu.VMEM((2, 2, WIN, WIN), f32),
            pltpu.VMEM((2, 2, WIN, WIN), f32),
            pltpu.SMEM((CAP,), jnp.int32),
            pltpu.SemaphoreType.DMA((CAP,)),
            pltpu.SemaphoreType.DMA((CAP, 2)),
            pltpu.SemaphoreType.DMA,
            pltpu.SemaphoreType.DMA((2,)),
        ],
        cost_estimate=CHEAP,
        compiler_params=vmem(24),
    )(flags, table, field, intensity, probe, kernel, *tables, *pieces)


def both_ways(pairs):
    return pairs + [(b, a) for a, b in pairs]


def everywhere(note):
    axes = ("groups", "row")
    count = lax.axis_size("groups") * lax.axis_size("row")
    copies = jnp.broadcast_to(note[None, :1], (count, 1, LANES))
    return jnp.max(lax.all_to_all(copies, axes, 0, 0, tiled=True))


def one_round(turn, grad, left_over, field, maps, intensity, probe_wave, prop_phase, own, before):
    count = lax.axis_size("row")
    within = both_ways([(i, i + 1) for i in range(0, count - 1, 2)])
    wide_pairs = both_ways([(i, i + 1) for i in range(1, count - 1, 4)])
    narrow_pairs = both_ways([(i, i + 1) for i in range(3, count - 1, 4)])
    move = lambda x, pairs: lax.ppermute(x, "row", pairs)
    place = lax.axis_index("row")
    odd = jnp.bitwise_and(place, 1)
    is_narrow = (jnp.bitwise_and(place + 1, 2) == 0).astype(jnp.int32)
    flags = jnp.stack([odd, is_narrow, turn, left_over * (1 - turn)])

    table = jax.ShapeDtypeStruct((CAP * FIELDS,), jnp.int32)
    inner, wide, narrow, note, table_in, table_out = pl.pallas_call(
        pack_kernel,
        out_shape=(
            packed(CAP_WIDE),
            packed(CAP_WIDE),
            packed(CAP_NARROW),
            jax.ShapeDtypeStruct((SUB, LANES), jnp.int32),
            table,
            table,
        ),
        in_specs=[spec(SM)] * 3 + [spec(HB)] * 2,
        out_specs=(spec(VM),) * 4 + (spec(SM),) * 2,
        scratch_shapes=[
            pltpu.VMEM((2 * CAP, 4, WIN, WIDE), f32),
            pltpu.SemaphoreType.DMA((2 * CAP,)),
            pltpu.SemaphoreType.DMA((CAP,)),
        ],
        cost_estimate=CHEAP,
        compiler_params=vmem(24),
    )(flags, own, before, field, maps)
    wide = move(wide, wide_pairs)
    narrow = move(narrow, narrow_pairs)
    inner = move(inner, within)
    again = everywhere(note)
    flags = jnp.stack([odd, is_narrow, turn, again])

    forms, shuffle = (jnp.asarray(t) for t in make_tables())
    kernel = pl.pallas_call(
        prepare_kernel,
        out_shape=jax.ShapeDtypeStruct((2, WIN, WIN), f32),
        in_specs=[spec(VM)] * 2,
        out_specs=spec(VM),
        scratch_shapes=[pltpu.VMEM((2, WIN, LANES), f32)],
        cost_estimate=CHEAP,
        compiler_params=vmem(8),
    )(jnp.stack([jnp.cos(prop_phase), jnp.sin(prop_phase)]), shuffle)

    args = (field, intensity, probe_wave, kernel, (forms, shuffle))
    in_back, tiles_in = run_slots(flags, table_in, *args, inner)
    in_back = move(in_back, within)
    back_wide, back_narrow, tiles_out = run_slots(flags, table_out, *args, wide, narrow)
    tiles_in = pltpu.with_memory_space_constraint(tiles_in, HB)
    tiles_out = pltpu.with_memory_space_constraint(tiles_out, HB)
    back_wide = move(back_wide, wide_pairs)
    back_narrow = move(back_narrow, narrow_pairs)
    total = pl.pallas_call(
        sum_kernel,
        out_shape=jax.ShapeDtypeStruct(field.shape, f32),
        in_specs=[spec(SM)] * 3 + [spec(pl.ANY)] * 3 + [spec(HB)],
        out_specs=spec(VM),
        scratch_shapes=[
            pltpu.VMEM((CAP_WIDE, 4, SUB, WIN), f32),
            pltpu.VMEM((2 * CAP, 4, WIN, WIN), f32),
            pltpu.SemaphoreType.DMA,
            pltpu.SemaphoreType.DMA((2 * CAP,)),
            pltpu.SemaphoreType.DMA,
        ],
        cost_estimate=CHEAP,
        compiler_params=vmem(20),
    )(flags, table_in, table_out, in_back, tiles_in, tiles_out, grad)
    grad = pl.pallas_call(
        finish_kernel,
        out_shape=jax.ShapeDtypeStruct(field.shape, f32),
        in_specs=[spec(SM)] * 2 + [spec(VM)] + [spec(pl.ANY)] * 2,
        out_specs=spec(HB),
        scratch_shapes=[
            pltpu.VMEM(field.shape, f32),
            pltpu.VMEM((CAP_WIDE, 4, SUB, WIN), f32),
            pltpu.SemaphoreType.DMA,
            pltpu.SemaphoreType.DMA((4,)),
        ],
        cost_estimate=CHEAP,
        compiler_params=vmem(16),
    )(flags, table_out, total, back_wide, back_narrow)
    return grad, again


def shards(obj_field, probe_wave, prop_phase, win_offsets, live_counts, intensity):
    field = pltpu.with_memory_space_constraint(obj_field.reshape((4,) + obj_field.shape[2:]), HB)
    maps = pltpu.with_memory_space_constraint(intensity.reshape(CAP, INT_GROUPS, 4, SUB, WIN), HB)
    intensity = pltpu.with_memory_space_constraint(intensity, HB)
    count = lax.axis_size("row")
    own = jnp.concatenate([win_offsets.reshape(-1), live_counts, jnp.zeros((INFO - 2 * CAP - 1,), jnp.int32)])
    before = lax.ppermute(own, "row", [(i, i + 1) for i in range(count - 1)])
    narrow_first = jnp.bitwise_and(lax.axis_index("row"), 3) == 3
    left_over = jnp.logical_and(narrow_first, live_counts[0] > NARROW_SLOTS).astype(jnp.int32)

    def body(state):
        turn, _, grad = state
        grad, again = one_round(turn, grad, left_over, field, maps, intensity, probe_wave, prop_phase, own, before)
        return turn + 1, again, grad

    empty = pl.pallas_call(
        lambda out: None,
        out_shape=jax.ShapeDtypeStruct(field.shape, f32),
        out_specs=spec(HB),
    )()
    _, _, grad = lax.while_loop(lambda state: state[1] > 0, body, (jnp.int32(0), jnp.int32(1), empty))
    return grad.reshape(obj_field.shape)


def solution(mesh):
    in_specs = (
        P(None, None, ("groups", "row"), None),
        P("groups", None, None),
        P(),
        P(("groups", "row"), None),
        P(("groups", "row")),
        P(("groups", "row"), None, None),
    )
    out_specs = P(None, None, ("groups", "row"), None)
    return jax.shard_map(shards, mesh=mesh, in_specs=in_specs, out_specs=out_specs, check_vma=False)
```

```python
import functools

import jax
import jax.numpy as jnp
import numpy as np
from jax import lax
from jax.experimental import pallas as pl
from jax.experimental.pallas import tpu as pltpu
from jax.sharding import PartitionSpec as P

WIN = 256
HALF = WIN // 2
LANES = 128
SUB = 8
CAP = 4
GROUPS = WIN // SUB
INT_GROUPS = GROUPS // 4
CAP_WIDE = 48
CAP_NARROW = 28
NARROW_SLOTS = 2
UNEVEN = 24
DEAD, AT_A, AT_B = 0, 1, 2
FIELDS = 8
f32 = jnp.float32
bf16 = jnp.bfloat16
VM = pltpu.MemorySpace.VMEM
SM = pltpu.MemorySpace.SMEM
HB = pltpu.MemorySpace.HBM
CHEAP = pl.CostEstimate(flops=1, transcendentals=0, bytes_accessed=1)


def real_tables():
    k = np.arange(HALF)[:, None]
    n = np.arange(HALF)[None, :]
    out = []
    for odd in (0, 1):
        angle = 2.0 * np.pi * (((2 * k + odd) * n) % WIN) / WIN
        c, s = np.cos(angle) / 16.0, np.sin(angle) / 16.0
        out.append(np.block([[c, s], [-s, c]]))
    return out


def high_low(table):
    high = table.astype(np.float32).astype(bf16)
    low = (table - high.astype(np.float64)).astype(np.float32).astype(bf16)
    return high, low


def make_tables():
    even, odd = real_tables()
    forms = np.stack([np.stack(high_low(m)) for m in (even, odd, even.T, odd.T)])
    order = np.concatenate([np.arange(0, WIN, 2), np.arange(1, WIN, 2)])
    shuffle = np.zeros((WIN, WIN), np.float32)
    shuffle[order, np.arange(WIN)] = 1.0
    return forms, shuffle.astype(bf16)


EVEN, ODD, EVEN_T, ODD_T = range(4)


def split(x):
    high = x.astype(bf16)
    return high, (x - high.astype(f32)).astype(bf16)


def left_mul(forms, which, x):
    high, low = split(x)
    t_high, t_low = forms[which, 0], forms[which, 1]
    wide = jnp.concatenate([t_high, t_low, t_high], axis=1)
    return jnp.dot(wide, jnp.concatenate([high, high, low], axis=0), preferred_element_type=f32)


def right_mul(x, forms, which):
    high, low = split(x)
    t_high, t_low = forms[which, 0], forms[which, 1]
    tall = jnp.concatenate([t_high, t_high, t_low], axis=0)
    return jnp.dot(jnp.concatenate([high, low, high], axis=1), tall, preferred_element_type=f32)


def rows_forward(re, im, forms):
    tr, br, ti, bi = re[:HALF], re[HALF:], im[:HALF], im[HALF:]
    e = left_mul(forms, EVEN, jnp.concatenate([tr + br, ti + bi], axis=0))
    o = left_mul(forms, ODD, jnp.concatenate([tr - br, ti - bi], axis=0))
    return e, o


def rows_inverse(re, im, forms):
    u = left_mul(forms, EVEN_T, jnp.concatenate([re[:HALF], im[:HALF]], axis=0))
    v = left_mul(forms, ODD_T, jnp.concatenate([re[HALF:], im[HALF:]], axis=0))
    return u, v


def lanes_forward(re, im, forms):
    lr, rr, li, ri = re[:, :HALF], re[:, HALF:], im[:, :HALF], im[:, HALF:]
    e = right_mul(jnp.concatenate([lr + rr, li + ri], axis=1), forms, EVEN_T)
    o = right_mul(jnp.concatenate([lr - rr, li - ri], axis=1), forms, ODD_T)
    return (
        jnp.concatenate([e[:, :HALF], o[:, :HALF]], axis=1),
        jnp.concatenate([e[:, HALF:], o[:, HALF:]], axis=1),
    )


def lanes_inverse(re, im, forms):
    u = right_mul(jnp.concatenate([re[:, :HALF], im[:, :HALF]], axis=1), forms, EVEN)
    v = right_mul(jnp.concatenate([re[:, HALF:], im[:, HALF:]], axis=1), forms, ODD)
    return (
        jnp.concatenate([u[:, :HALF] + v[:, :HALF], u[:, :HALF] - v[:, :HALF]], axis=1),
        jnp.concatenate([u[:, HALF:] + v[:, HALF:], u[:, HALF:] - v[:, HALF:]], axis=1),
    )


def cmul(ar, ai, br, bi):
    return ar * br - ai * bi, ar * bi + ai * br


def cmul_conj(ar, ai, br, bi):
    return ar * br + ai * bi, ar * bi - ai * br


INFO = LANES
PLACE = 2 * CAP


def decide(info, who, table, first_slot, last_slot, cap):
    count = jnp.where(who < 0, 0, info[jnp.maximum(who, 0), PLACE])
    who = jnp.maximum(who, 0)
    rows = [jnp.bitwise_and(info[who, 2 * j], WIN - 1) for j in range(CAP)]
    last_slot = jnp.minimum(last_slot, count)
    used = [jnp.logical_and(j >= first_slot, j < last_slot).astype(jnp.int32) for j in range(CAP)]
    on_a = [used[j] * ((rows[j] + SUB - 1) // SUB) for j in range(CAP)]
    on_b = [used[j] * (GROUPS - rows[j] // SUB + INT_GROUPS) for j in range(CAP)]
    best, chosen = jnp.int32(10000), jnp.int32(0)
    for mask in range(1 << CAP):
        total_a = jnp.int32(0)
        total_b = jnp.int32(0)
        slots_a = jnp.int32(0)
        slots_b = jnp.int32(0)
        for j in range(CAP):
            if mask >> j & 1:
                total_b = total_b + on_b[j]
                slots_b = slots_b + used[j]
            else:
                total_a = total_a + on_a[j]
                slots_a = slots_a + used[j]
        cost = jnp.maximum(total_a, total_b)
        cost = cost + jnp.where(cost > cap, 1000, 0)
        cost = cost + jnp.where(jnp.maximum(slots_a, slots_b) > 2, UNEVEN, 0)
        better = cost < best
        best = jnp.where(better, cost, best)
        chosen = jnp.where(better, mask, chosen)
    at_a = jnp.int32(0)
    at_b = jnp.int32(0)
    back = jnp.int32(0)
    for j in range(CAP):
        to_b = jnp.bitwise_and(chosen >> j, 1) * used[j]
        to_b = jnp.where(rows[j] == 0, 0, to_b)
        to_a = used[j] - to_b
        table[FIELDS * j] = to_a * AT_A + to_b * AT_B
        table[FIELDS * j + 1] = rows[j]
        table[FIELDS * j + 2] = info[who, 2 * j + 1]
        table[FIELDS * j + 3] = jnp.where(to_b == 1, at_b, at_a)
        table[FIELDS * j + 4] = jnp.where(to_b == 1, back, at_a)
        at_a = at_a + to_a * on_a[j]
        at_b = at_b + to_b * on_b[j]
        back = back + to_b * (on_b[j] - INT_GROUPS)


def slot_of(table, j):
    base = FIELDS * j
    return table[base], table[base + 1], table[base + 2], table[base + 3], table[base + 4]


def lane_blocks(col):
    first = col // LANES
    starts = [jnp.minimum(first + k, 7) * LANES for k in range(3)]
    return [pl.multiple_of(start, LANES) for start in starts], jnp.bitwise_and(col, LANES - 1)


WIDE = 3 * LANES


def near_columns(col):
    first = jnp.minimum(col // LANES, 5)
    skip = col // LANES - first
    starts = [pl.multiple_of(jnp.minimum(skip + k, 2) * LANES, LANES) for k in range(3)]
    return pl.ds(pl.multiple_of(first * LANES, LANES), WIDE), starts, jnp.bitwise_and(col, LANES - 1)


def lane_iota():
    return lax.broadcasted_iota(jnp.int32, (SUB, LANES), 1)


def load_group(field, plane, group, starts, shift):
    rows = pl.ds(pl.multiple_of(group * SUB, SUB), SUB)
    first = field[plane, rows, pl.ds(starts[0], LANES)]
    second = field[plane, rows, pl.ds(starts[1], LANES)]
    third = field[plane, rows, pl.ds(starts[2], LANES)]
    return jnp.where(lane_iota() >= shift, first, third), second


def add_group(total, plane, group, starts, shift, left, right):
    rows = pl.ds(pl.multiple_of(group * SUB, SUB), SUB)
    inside = lane_iota() >= shift
    total[plane, rows, pl.ds(starts[0], LANES)] += jnp.where(inside, left, 0.0)
    total[plane, rows, pl.ds(starts[1], LANES)] += right
    total[plane, rows, pl.ds(starts[2], LANES)] += jnp.where(inside, 0.0, left)


def fetch_columns(table, wanted, field, held, sem, base):
    for j in range(CAP):

        @pl.when(table[FIELDS * j] == wanted)
        def _():
            columns, _, _ = near_columns(table[FIELDS * j + 2])
            pltpu.make_async_copy(field.at[:, :, columns], held.at[base + j], sem.at[base + j]).start()


def copy_groups(held, out, at, offset, low, high, starts, shift):
    def body(group, carry):
        for plane in range(4):
            left, right = load_group(held.at[at], plane, group, starts, shift)
            out[offset + group, plane, :, :LANES] = left
            out[offset + group, plane, :, LANES:] = right
        return carry

    lax.fori_loop(low, high, body, 0)


def pack_to_b(table, field, intensity, out, held, sem, int_sem, base):
    def intensity_copy(j):
        _, row, _, start, _ = slot_of(table, j)
        after = start + GROUPS - row // SUB
        return pltpu.make_async_copy(intensity.at[j], out.at[pl.ds(after, INT_GROUPS)], int_sem.at[j])

    for j in range(CAP):

        @pl.when(table[FIELDS * j] == AT_B)
        def _():
            intensity_copy(j).start()

    for j in range(CAP):
        state, row, col, start, _ = slot_of(table, j)

        @pl.when(state == AT_B)
        def _():
            columns, starts, shift = near_columns(col)
            at = base + j
            pltpu.make_async_copy(field.at[:, :, columns], held.at[at], sem.at[at]).wait()
            copy_groups(held, out, at, start - row // SUB, row // SUB, GROUPS, starts, shift)
            intensity_copy(j).wait()


def pack_to_a(table, field, out, held, sem, base):
    for j in range(CAP):
        state, row, col, start, _ = slot_of(table, j)

        @pl.when(state == AT_A)
        def _():
            columns, starts, shift = near_columns(col)
            at = base + j
            pltpu.make_async_copy(field.at[:, :, columns], held.at[at], sem.at[at]).wait()
            copy_groups(held, out, at, start, 0, (row + SUB - 1) // SUB, starts, shift)


def pack_kernel(
    flags, info, field, intensity, inner, wide, narrow, table_in, table_out, again, held, sem, int_sem
):
    turn = flags[2]
    is_narrow = flags[1] == 1
    own, before = flags[3], flags[4]
    first_slot = jnp.where(is_narrow, NARROW_SLOTS * turn, CAP * turn)
    last_slot = jnp.where(is_narrow, NARROW_SLOTS * (turn + 1), CAP)
    cap = jnp.where(is_narrow, CAP_NARROW, CAP_WIDE)

    def outward(pack):
        @pl.when(is_narrow)
        def _():
            pack(narrow)

        @pl.when(jnp.logical_not(is_narrow))
        def _():
            pack(wide)

    @pl.when(flags[0] == 0)
    def _():
        decide(info, before, table_out, first_slot, last_slot, cap)
        fetch_columns(table_out, AT_A, field, held, sem, 0)
        decide(info, own, table_in, CAP * turn, CAP, CAP_WIDE)
        fetch_columns(table_in, AT_B, field, held, sem, CAP)
        outward(lambda out: pack_to_a(table_out, field, out, held, sem, 0))
        pack_to_b(table_in, field, intensity, inner, held, sem, int_sem, CAP)

    @pl.when(flags[0] == 1)
    def _():
        decide(info, own, table_out, first_slot, last_slot, cap)
        fetch_columns(table_out, AT_B, field, held, sem, 0)
        decide(info, before, table_in, CAP * turn, CAP, CAP_WIDE)
        fetch_columns(table_in, AT_A, field, held, sem, CAP)
        outward(lambda out: pack_to_b(table_out, field, intensity, out, held, sem, int_sem, 0))
        pack_to_a(table_in, field, inner, held, sem, CAP)

    def check(k, most):
        narrow_first = jnp.bitwise_and(k, 3) == 3
        return jnp.maximum(most, jnp.where(narrow_first, info[k, PLACE], 0))

    most = lax.fori_loop(0, info.shape[0], check, jnp.int32(0))
    again[0] = jnp.logical_and(turn == 0, most > NARROW_SLOTS).astype(jnp.int32)


def prepare_kernel(phases, shuffle, out, halves):
    for plane in range(2):
        halves[0] = phases[plane, :, :LANES]
        halves[1] = phases[plane, :, LANES:]
        for part in range(2):
            every = pl.ds(part, HALF, stride=2)
            x = jnp.concatenate([halves[0, every, :], halves[1, every, :]], axis=1)
            high = x.astype(bf16)
            rest = x - high.astype(f32)
            middle, low = split(rest)
            total = jnp.dot(high, shuffle[...], preferred_element_type=f32)
            total += jnp.dot(middle, shuffle[...], preferred_element_type=f32)
            total += jnp.dot(low, shuffle[...], preferred_element_type=f32)
            out[plane, part * HALF : (part + 1) * HALF, :] = total


def fetch_pieces(is_narrow, wide, narrow, got, sem):
    @pl.when(is_narrow)
    def _():
        pltpu.make_async_copy(narrow, got.at[pl.ds(0, CAP_NARROW)], sem).start()

    @pl.when(jnp.logical_not(is_narrow))
    def _():
        pltpu.make_async_copy(wide, got, sem).start()


def await_pieces(is_narrow, wide, narrow, got, sem):
    @pl.when(is_narrow)
    def _():
        pltpu.make_async_copy(narrow, got.at[pl.ds(0, CAP_NARROW)], sem).wait()

    @pl.when(jnp.logical_not(is_narrow))
    def _():
        pltpu.make_async_copy(wide, got, sem).wait()


def slots_kernel(between, flags, table, field, intensity, probe, kernel, forms, shuffle, wide, *rest):
    narrow = rest[0] if between else wide
    back_wide, back_narrow = (rest[1], rest[2]) if between else (rest[0], rest[0])
    tiles, held, got, tile, measured, twice, beam, work, entered, chosen = rest[3 if between else 1 : -4]
    held_sem, int_sem, got_sem, tile_sem = rest[-4:]
    is_a = flags[0] == (1 if between else 0)
    is_narrow = jnp.logical_and(between, flags[1] == 1)
    mine = jnp.where(is_a, AT_A, AT_B)
    if between:
        fetch_pieces(is_narrow, wide, narrow, got, got_sem)
    else:
        pltpu.make_async_copy(wide, got, got_sem).start()
    fetch_columns(table, mine, field, held, held_sem, 0)

    def intensity_copies(j):
        return [
            pltpu.make_async_copy(
                intensity.at[j, :, pl.ds(part * LANES, LANES)], measured.at[j, part], int_sem.at[j, part]
            )
            for part in range(2)
        ]

    for j in range(CAP):

        @pl.when(jnp.logical_and(is_a, table[FIELDS * j] == AT_A))
        def _():
            for copy in intensity_copies(j):
                copy.start()

    for plane in range(2):
        for part in range(2):
            cut = probe[plane, :, part * LANES : (part + 1) * LANES]
            twice[2 * plane + part, :WIN] = cut
            twice[2 * plane + part, WIN:] = cut
    found = jnp.int32(0)
    for j in range(CAP):
        chosen[j] = 0
    for j in range(CAP):
        state = table[FIELDS * j]

        @pl.when(state == mine)
        def _():
            chosen[found] = j

        found = found + (state == mine).astype(jnp.int32)
    if between:
        await_pieces(is_narrow, wide, narrow, got, got_sem)
    else:
        pltpu.make_async_copy(wide, got, got_sem).wait()
    sublane = lax.broadcasted_iota(jnp.int32, (SUB, LANES), 0)

    def load(m, j):
        _, row, col, start, _ = slot_of(table, j)
        columns, starts, shift = near_columns(col)
        low = row // SUB
        high = (row + SUB - 1) // SUB
        base = jnp.where(is_a, start, start - low)

        def own_groups(group, carry):
            rows = pl.ds(pl.multiple_of(group * SUB, SUB), SUB)
            for plane in range(4):
                lf, rt = load_group(held.at[j], plane, group, starts, shift)
                tile[m, plane, rows, :LANES] = lf
                tile[m, plane, rows, LANES:] = rt
            return carry

        def their_groups(group, carry):
            rows = pl.ds(pl.multiple_of(group * SUB, SUB), SUB)
            for plane in range(4):
                tile[m, plane, rows, :] = got[base + group, plane]
            return carry

        lax.fori_loop(jnp.where(is_a, 0, low), jnp.where(is_a, high, GROUPS), their_groups, 0)
        lax.fori_loop(jnp.where(is_a, high, 0), jnp.where(is_a, GROUPS, low), own_groups, 0)

        @pl.when(low < high)
        def _():
            own = (low * SUB + sublane < row).astype(jnp.int32) == jnp.where(is_a, 0, 1)
            rows = pl.ds(pl.multiple_of(low * SUB, SUB), SUB)
            for plane in range(4):
                lf, rt = load_group(held.at[j], plane, low, starts, shift)
                tile[m, plane, rows, :LANES] = jnp.where(own, lf, tile[m, plane, rows, :LANES])
                tile[m, plane, rows, LANES:] = jnp.where(own, rt, tile[m, plane, rows, LANES:])

        @pl.when(jnp.logical_not(is_a))
        def _():
            after = start + GROUPS - low

            def unpack(group, carry):
                for plane in range(4):
                    rows = pl.ds(pl.multiple_of((group * 4 + plane) * SUB, SUB), SUB)
                    measured[j, 0, rows, :] = got[after + group, plane, :, :LANES]
                    measured[j, 1, rows, :] = got[after + group, plane, :, LANES:]
                return carry

            lax.fori_loop(0, INT_GROUPS, unpack, 0)

        for plane in range(2):
            parts = [twice[2 * plane + part, pl.ds(WIN - row, WIN), :] for part in range(2)]
            beam[m, plane] = pltpu.roll(jnp.concatenate(parts, axis=1), shift, 1)

    def arrive(j):
        columns, _, _ = near_columns(table[FIELDS * j + 2])
        pltpu.make_async_copy(field.at[:, :, columns], held.at[j], held_sem.at[j]).wait()

        @pl.when(is_a)
        def _():
            for copy in intensity_copies(j):
                copy.wait()

    def store_rows(m, e, o):
        work[m, 0, :HALF], work[m, 1, :HALF] = e[:HALF], e[HALF:]
        work[m, 0, HALF:], work[m, 1, HALF:] = o[:HALF], o[HALF:]

    def middle(pointwise, slots=None):
        for half in range(2):
            rows = pl.ds(half * HALF, HALF)
            for m in range(2):
                re, im = lanes_forward(work[m, 0, rows, :], work[m, 1, rows, :], forms)
                re, im = pointwise(m, half, rows, re, im, slots)
                re, im = lanes_inverse(re, im, forms)
                work[m, 0, rows, :], work[m, 1, rows, :] = re, im

    def rows_back(m):
        u, v = rows_inverse(work[m, 0], work[m, 1], forms)
        return (
            jnp.concatenate([u[:HALF] + v[:HALF], u[:HALF] - v[:HALF]], axis=0),
            jnp.concatenate([u[HALF:] + v[HALF:], u[HALF:] - v[HALF:]], axis=0),
        )

    def propagate(m, half, rows, re, im, slots):
        return cmul(kernel[0, rows, :], kernel[1, rows, :], re, im)

    def propagate_back(m, half, rows, re, im, slots):
        return cmul_conj(kernel[0, rows, :], kernel[1, rows, :], re, im)

    def residual(m, half, rows, re, im, slots):
        every = pl.ds(half, HALF, stride=2)
        at = slots[m]
        rows_of = jnp.concatenate([measured[at, 0, every, :], measured[at, 1, every, :]], axis=1)
        high, low = split(rows_of)
        wanted = jnp.dot(high, shuffle[...], preferred_element_type=f32)
        wanted += jnp.dot(low, shuffle[...], preferred_element_type=f32)
        scale = re * re + im * im - wanted
        return scale * re, scale * im

    def tile_copy(m, j):
        return pltpu.make_async_copy(tile.at[m], tiles.at[j], tile_sem.at[m])

    def write(m, j):
        _, row, _, _, back = slot_of(table, j)
        low = row // SUB

        def send(out, offset):
            def body(group, carry):
                rows = pl.ds(pl.multiple_of(group * SUB, SUB), SUB)
                for plane in range(4):
                    out[offset + group, plane] = tile[m, plane, rows, :]
                return carry

            return body

        tile_copy(m, j).start()

        offset = jnp.where(is_a, back, back - low)
        lower = jnp.where(is_a, 0, low)
        upper = jnp.where(is_a, (row + SUB - 1) // SUB, GROUPS)
        if between:

            @pl.when(is_narrow)
            def _():
                lax.fori_loop(lower, upper, send(back_narrow, offset), 0)

            @pl.when(jnp.logical_not(is_narrow))
            def _():
                lax.fori_loop(lower, upper, send(back_wide, offset), 0)

        else:
            lax.fori_loop(lower, upper, send(back_wide, offset), 0)

    def pair(p, carry):
        two = 2 * p + 1 < found
        first = chosen[2 * p]
        second = jnp.where(two, chosen[jnp.minimum(2 * p + 1, CAP - 1)], first)

        @pl.when(p > 0)
        def _():
            tile_copy(0, chosen[2 * p - 2]).wait()
            tile_copy(1, chosen[2 * p - 1]).wait()

        arrive(first)

        @pl.when(two)
        def _():
            arrive(second)

        load(0, first)
        load(1, second)
        for m in range(2):
            re, im = cmul(beam[m, 0], beam[m, 1], tile[m, 0], tile[m, 1])
            store_rows(m, *rows_forward(re, im, forms))
        middle(propagate)
        for m in range(2):
            re, im = rows_back(m)
            entered[m, 0], entered[m, 1] = re, im
            re, im = cmul(re, im, tile[m, 2], tile[m, 3])
            store_rows(m, *rows_forward(re, im, forms))
        middle(residual, (first, second))
        for m in range(2):
            br, bi = rows_back(m)
            re, im = cmul_conj(tile[m, 2], tile[m, 3], br, bi)
            tile[m, 2], tile[m, 3] = cmul_conj(entered[m, 0], entered[m, 1], br, bi)
            store_rows(m, *rows_forward(re, im, forms))
        middle(propagate_back)
        for m in range(2):
            br, bi = rows_back(m)
            tile[m, 0], tile[m, 1] = cmul_conj(beam[m, 0], beam[m, 1], br, bi)
        write(0, first)

        @pl.when(two)
        def _():
            write(1, second)

        return carry

    lax.fori_loop(0, (found + 1) // 2, pair, 0)

    @pl.when(found > 0)
    def _():
        tile_copy(0, 0).wait()

    @pl.when(jnp.logical_and(found > 0, jnp.bitwise_and(found, 1) == 0))
    def _():
        tile_copy(1, 0).wait()


def add_back(is_a, table, got, total, planes):
    theirs = jnp.where(is_a, AT_B, AT_A)
    for j in range(CAP):
        state, row, col, _, back = slot_of(table, j)

        @pl.when(state == theirs)
        def _():
            starts, shift = lane_blocks(col)
            low = row // SUB
            base = jnp.where(is_a, back - low, back)
            sublane = lax.broadcasted_iota(jnp.int32, (SUB, LANES), 0)

            def body(group, carry):
                below = (group * SUB + sublane < row).astype(jnp.int32)
                own = below == jnp.where(is_a, 0, 1)
                for plane in planes:
                    lf = jnp.where(own, got[base + group, plane, :, :LANES], 0.0)
                    rt = jnp.where(own, got[base + group, plane, :, LANES:], 0.0)
                    add_group(total, plane, group, starts, shift, lf, rt)
                return carry

            lax.fori_loop(jnp.where(is_a, low, 0), jnp.where(is_a, GROUPS, (row + SUB - 1) // SUB), body, 0)


def sum_kernel(
    flags, table_in, table_out, in_back, tiles_in, tiles_out, grad, total, got, tile, got_sem, tile_sem, total_sem
):
    pltpu.make_async_copy(in_back, got, got_sem).start()
    sublane = lax.broadcasted_iota(jnp.int32, (SUB, LANES), 0)
    kinds = ((flags[0] == 0, table_in, tiles_in), (flags[0] == 1, table_out, tiles_out))
    for k, (is_a, table, tiles) in enumerate(kinds):
        mine = jnp.where(is_a, AT_A, AT_B)
        for j in range(CAP):

            @pl.when(table[FIELDS * j] == mine)
            def _():
                pltpu.make_async_copy(tiles.at[j], tile.at[k * CAP + j], tile_sem.at[k * CAP + j]).start()

    @pl.when(flags[2] == 0)
    def _():
        total[...] = jnp.zeros_like(total)

    @pl.when(flags[2] > 0)
    def _():
        copy = pltpu.make_async_copy(grad, total, total_sem)
        copy.start()
        copy.wait()

    pltpu.make_async_copy(in_back, got, got_sem).wait()
    add_back(flags[0] == 0, table_in, got, total, range(4))
    for k, (is_a, table, tiles) in enumerate(kinds):
        mine = jnp.where(is_a, AT_A, AT_B)
        for j in range(CAP):
            state, row, col, _, _ = slot_of(table, j)

            @pl.when(state == mine)
            def _():
                at = k * CAP + j
                pltpu.make_async_copy(tiles.at[j], tile.at[at], tile_sem.at[at]).wait()
                starts, shift = lane_blocks(col)
                low = row // SUB

                def body(group, carry):
                    below = (group * SUB + sublane < row).astype(jnp.int32)
                    own = below == jnp.where(is_a, 0, 1)
                    rows = pl.ds(pl.multiple_of(group * SUB, SUB), SUB)
                    for plane in range(4):
                        lf = jnp.where(own, tile[at, plane, rows, :LANES], 0.0)
                        rt = jnp.where(own, tile[at, plane, rows, LANES:], 0.0)
                        add_group(total, plane, group, starts, shift, lf, rt)
                    return carry

                lax.fori_loop(
                    jnp.where(is_a, low, 0), jnp.where(is_a, GROUPS, (row + SUB - 1) // SUB), body, 0
                )


def finish_kernel(flags, table, total_in, wide, narrow, grad, total, got, got_sem, out_sem):
    is_narrow = flags[1] == 1
    fetch_pieces(is_narrow, wide, narrow, got, got_sem)
    await_pieces(is_narrow, wide, narrow, got, got_sem)
    for plane in range(4):
        total[plane] = total_in[plane]
        add_back(flags[0] == 1, table, got, total, (plane,))
        pltpu.make_async_copy(total.at[plane], grad.at[plane], out_sem.at[plane]).start()
    for plane in range(4):
        pltpu.make_async_copy(total.at[plane], grad.at[plane], out_sem.at[plane]).wait()


def spec(space):
    return pl.BlockSpec(memory_space=space)


def vmem(mib):
    return pltpu.CompilerParams(vmem_limit_bytes=mib << 20)


def packed(groups):
    return jax.ShapeDtypeStruct((groups, 4, SUB, WIN), f32)


def run_slots(flags, table, field, intensity, probe, kernel, tables, *pieces):
    between = len(pieces) == 2
    backs = (CAP_WIDE, CAP_NARROW)[: len(pieces)]
    return pl.pallas_call(
        functools.partial(slots_kernel, between),
        out_shape=tuple(packed(n) for n in backs) + (HB((CAP, 4, WIN, WIN), f32),),
        in_specs=[spec(SM)] * 2 + [spec(HB)] * 2 + [spec(VM)] * 4 + [spec(pl.ANY)] * len(pieces),
        out_specs=(spec(VM),) * len(backs) + (spec(HB),),
        scratch_shapes=[
            pltpu.VMEM((CAP, 4, WIN, WIDE), f32),
            pltpu.VMEM((CAP_WIDE, 4, SUB, WIN), f32),
            pltpu.VMEM((2, 4, WIN, WIN), f32),
            pltpu.VMEM((CAP, 2, WIN, LANES), f32),
            pltpu.VMEM((4, 2 * WIN, LANES), f32),
            pltpu.VMEM((2, 2, WIN, WIN), f32),
            pltpu.VMEM((2, 2, WIN, WIN), f32),
            pltpu.VMEM((2, 2, WIN, WIN), f32),
            pltpu.SMEM((CAP,), jnp.int32),
            pltpu.SemaphoreType.DMA((CAP,)),
            pltpu.SemaphoreType.DMA((CAP, 2)),
            pltpu.SemaphoreType.DMA,
            pltpu.SemaphoreType.DMA((2,)),
        ],
        cost_estimate=CHEAP,
        compiler_params=vmem(24),
    )(flags, table, field, intensity, probe, kernel, *tables, *pieces)


def both_ways(pairs):
    return pairs + [(b, a) for a, b in pairs]


def one_round(turn, grad, field, maps, intensity, probe_wave, prop_phase, info):
    count = lax.axis_size("row")
    within = both_ways([(i, i + 1) for i in range(0, count - 1, 2)])
    wide_pairs = both_ways([(i, i + 1) for i in range(1, count - 1, 4)])
    narrow_pairs = both_ways([(i, i + 1) for i in range(3, count - 1, 4)])
    move = lambda x, pairs: lax.ppermute(x, "row", pairs)
    place = lax.axis_index("row")
    odd = jnp.bitwise_and(place, 1)
    is_narrow = (jnp.bitwise_and(place + 1, 2) == 0).astype(jnp.int32)
    own = lax.axis_index("groups") * count + place
    flags = jnp.stack([odd, is_narrow, turn, own, jnp.where(place == 0, -1, own - 1)])
    prop_phase, _ = lax.optimization_barrier((prop_phase, turn))

    table = jax.ShapeDtypeStruct((CAP * FIELDS,), jnp.int32)
    inner, wide, narrow, table_in, table_out, again = pl.pallas_call(
        pack_kernel,
        out_shape=(
            packed(CAP_WIDE),
            packed(CAP_WIDE),
            packed(CAP_NARROW),
            table,
            table,
            jax.ShapeDtypeStruct((1,), jnp.int32),
        ),
        in_specs=[spec(SM)] * 2 + [spec(HB)] * 2,
        out_specs=(spec(VM),) * 3 + (spec(SM),) * 3,
        scratch_shapes=[
            pltpu.VMEM((2 * CAP, 4, WIN, WIDE), f32),
            pltpu.SemaphoreType.DMA((2 * CAP,)),
            pltpu.SemaphoreType.DMA((CAP,)),
        ],
        cost_estimate=CHEAP,
        compiler_params=vmem(24),
    )(flags, info, field, maps)
    wide = move(wide, wide_pairs)
    narrow = move(narrow, narrow_pairs)
    inner = move(inner, within)

    forms, shuffle = (jnp.asarray(t) for t in make_tables())
    kernel = pl.pallas_call(
        prepare_kernel,
        out_shape=jax.ShapeDtypeStruct((2, WIN, WIN), f32),
        in_specs=[spec(VM)] * 2,
        out_specs=spec(VM),
        scratch_shapes=[pltpu.VMEM((2, WIN, LANES), f32)],
        cost_estimate=CHEAP,
        compiler_params=vmem(8),
    )(jnp.stack([jnp.cos(prop_phase), jnp.sin(prop_phase)]), shuffle)

    args = (field, intensity, probe_wave, kernel, (forms, shuffle))
    in_back, tiles_in = run_slots(flags, table_in, *args, inner)
    in_back = move(in_back, within)
    back_wide, back_narrow, tiles_out = run_slots(flags, table_out, *args, wide, narrow)
    tiles_in = pltpu.with_memory_space_constraint(tiles_in, HB)
    tiles_out = pltpu.with_memory_space_constraint(tiles_out, HB)
    back_wide = move(back_wide, wide_pairs)
    back_narrow = move(back_narrow, narrow_pairs)
    total = pl.pallas_call(
        sum_kernel,
        out_shape=jax.ShapeDtypeStruct(field.shape, f32),
        in_specs=[spec(SM)] * 3 + [spec(pl.ANY)] * 3 + [spec(HB)],
        out_specs=spec(VM),
        scratch_shapes=[
            pltpu.VMEM((CAP_WIDE, 4, SUB, WIN), f32),
            pltpu.VMEM((2 * CAP, 4, WIN, WIN), f32),
            pltpu.SemaphoreType.DMA,
            pltpu.SemaphoreType.DMA((2 * CAP,)),
            pltpu.SemaphoreType.DMA,
        ],
        cost_estimate=CHEAP,
        compiler_params=vmem(20),
    )(flags, table_in, table_out, in_back, tiles_in, tiles_out, grad)
    grad = pl.pallas_call(
        finish_kernel,
        out_shape=jax.ShapeDtypeStruct(field.shape, f32),
        in_specs=[spec(SM)] * 2 + [spec(VM)] + [spec(pl.ANY)] * 2,
        out_specs=spec(HB),
        scratch_shapes=[
            pltpu.VMEM(field.shape, f32),
            pltpu.VMEM((CAP_WIDE, 4, SUB, WIN), f32),
            pltpu.SemaphoreType.DMA,
            pltpu.SemaphoreType.DMA((4,)),
        ],
        cost_estimate=CHEAP,
        compiler_params=vmem(16),
    )(flags, table_out, total, back_wide, back_narrow)
    return grad, again[0]


def shards(obj_field, probe_wave, prop_phase, win_offsets, live_counts, intensity):
    field = pltpu.with_memory_space_constraint(obj_field.reshape((4,) + obj_field.shape[2:]), HB)
    maps = pltpu.with_memory_space_constraint(intensity.reshape(CAP, INT_GROUPS, 4, SUB, WIN), HB)
    intensity = pltpu.with_memory_space_constraint(intensity, HB)
    axes = ("groups", "row")
    count = lax.axis_size("groups") * lax.axis_size("row")
    own = jnp.concatenate([win_offsets.reshape(-1), live_counts, jnp.zeros((INFO - PLACE - 1,), jnp.int32)])
    info = lax.all_to_all(jnp.broadcast_to(own, (count, 1, INFO)), axes, 0, 0, tiled=True).reshape(count, INFO)

    def body(state):
        turn, _, grad = state
        grad, again = one_round(turn, grad, field, maps, intensity, probe_wave, prop_phase, info)
        return turn + 1, again, grad

    empty = pl.pallas_call(
        lambda out: None,
        out_shape=jax.ShapeDtypeStruct(field.shape, f32),
        out_specs=spec(HB),
    )()
    _, _, grad = lax.while_loop(lambda state: state[1] > 0, body, (jnp.int32(0), jnp.int32(1), empty))
    return grad.reshape(obj_field.shape)


def solution(mesh):
    in_specs = (
        P(None, None, ("groups", "row"), None),
        P("groups", None, None),
        P(),
        P(("groups", "row"), None),
        P(("groups", "row")),
        P(("groups", "row"), None, None),
    )
    out_specs = P(None, None, ("groups", "row"), None)
    return jax.shard_map(shards, mesh=mesh, in_specs=in_specs, out_specs=out_specs, check_vma=False)
```

```python
import functools

import jax
import jax.numpy as jnp
import numpy as np
from jax import lax
from jax.experimental import pallas as pl
from jax.experimental.pallas import tpu as pltpu
from jax.sharding import PartitionSpec as P

WIN = 256
HALF = WIN // 2
LANES = 128
SUB = 8
CAP = 4
GROUPS = WIN // SUB
INT_GROUPS = GROUPS // 4
CAP_WIDE = 48
CAP_NARROW = 28
NARROW_SLOTS = 2
UNEVEN = 100
DEAD, AT_A, AT_B = 0, 1, 2
FIELDS = 8
f32 = jnp.float32
bf16 = jnp.bfloat16
VM = pltpu.MemorySpace.VMEM
SM = pltpu.MemorySpace.SMEM
HB = pltpu.MemorySpace.HBM
CHEAP = pl.CostEstimate(flops=1, transcendentals=0, bytes_accessed=1)


def real_tables():
    k = np.arange(HALF)[:, None]
    n = np.arange(HALF)[None, :]
    out = []
    for odd in (0, 1):
        angle = 2.0 * np.pi * (((2 * k + odd) * n) % WIN) / WIN
        c, s = np.cos(angle) / 16.0, np.sin(angle) / 16.0
        out.append(np.block([[c, s], [-s, c]]))
    return out


def high_low(table):
    high = table.astype(np.float32).astype(bf16)
    low = (table - high.astype(np.float64)).astype(np.float32).astype(bf16)
    return high, low


def make_tables():
    even, odd = real_tables()
    forms = np.stack([np.stack(high_low(m)) for m in (even, odd, even.T, odd.T)])
    order = np.concatenate([np.arange(0, WIN, 2), np.arange(1, WIN, 2)])
    shuffle = np.zeros((WIN, WIN), np.float32)
    shuffle[order, np.arange(WIN)] = 1.0
    return forms, shuffle.astype(bf16)


EVEN, ODD, EVEN_T, ODD_T = range(4)


def split(x):
    high = x.astype(bf16)
    return high, (x - high.astype(f32)).astype(bf16)


def left_mul(forms, which, x):
    high, low = split(x)
    t_high, t_low = forms[which, 0], forms[which, 1]
    wide = jnp.concatenate([t_high, t_low, t_high], axis=1)
    return jnp.dot(wide, jnp.concatenate([high, high, low], axis=0), preferred_element_type=f32)


def right_mul(x, forms, which):
    high, low = split(x)
    t_high, t_low = forms[which, 0], forms[which, 1]
    tall = jnp.concatenate([t_high, t_high, t_low], axis=0)
    return jnp.dot(jnp.concatenate([high, low, high], axis=1), tall, preferred_element_type=f32)


def rows_forward(re, im, forms):
    tr, br, ti, bi = re[:HALF], re[HALF:], im[:HALF], im[HALF:]
    e = left_mul(forms, EVEN, jnp.concatenate([tr + br, ti + bi], axis=0))
    o = left_mul(forms, ODD, jnp.concatenate([tr - br, ti - bi], axis=0))
    return e, o


def rows_inverse(re, im, forms):
    u = left_mul(forms, EVEN_T, jnp.concatenate([re[:HALF], im[:HALF]], axis=0))
    v = left_mul(forms, ODD_T, jnp.concatenate([re[HALF:], im[HALF:]], axis=0))
    return u, v


def lanes_forward(re, im, forms):
    lr, rr, li, ri = re[:, :HALF], re[:, HALF:], im[:, :HALF], im[:, HALF:]
    e = right_mul(jnp.concatenate([lr + rr, li + ri], axis=1), forms, EVEN_T)
    o = right_mul(jnp.concatenate([lr - rr, li - ri], axis=1), forms, ODD_T)
    return (
        jnp.concatenate([e[:, :HALF], o[:, :HALF]], axis=1),
        jnp.concatenate([e[:, HALF:], o[:, HALF:]], axis=1),
    )


def lanes_inverse(re, im, forms):
    u = right_mul(jnp.concatenate([re[:, :HALF], im[:, :HALF]], axis=1), forms, EVEN)
    v = right_mul(jnp.concatenate([re[:, HALF:], im[:, HALF:]], axis=1), forms, ODD)
    return (
        jnp.concatenate([u[:, :HALF] + v[:, :HALF], u[:, :HALF] - v[:, :HALF]], axis=1),
        jnp.concatenate([u[:, HALF:] + v[:, HALF:], u[:, HALF:] - v[:, HALF:]], axis=1),
    )


def cmul(ar, ai, br, bi):
    return ar * br - ai * bi, ar * bi + ai * br


def cmul_conj(ar, ai, br, bi):
    return ar * br + ai * bi, ar * bi - ai * br


INFO = LANES
PLACE = 2 * CAP


def decide(info, who, table, first_slot, last_slot, cap):
    count = jnp.where(who < 0, 0, info[jnp.maximum(who, 0), PLACE])
    who = jnp.maximum(who, 0)
    rows = [jnp.bitwise_and(info[who, 2 * j], WIN - 1) for j in range(CAP)]
    last_slot = jnp.minimum(last_slot, count)
    used = [jnp.logical_and(j >= first_slot, j < last_slot).astype(jnp.int32) for j in range(CAP)]
    on_a = [used[j] * ((rows[j] + SUB - 1) // SUB) for j in range(CAP)]
    on_b = [used[j] * (GROUPS - rows[j] // SUB + INT_GROUPS) for j in range(CAP)]
    best, chosen = jnp.int32(10000), jnp.int32(0)
    for mask in range(1 << CAP):
        total_a = jnp.int32(0)
        total_b = jnp.int32(0)
        slots_a = jnp.int32(0)
        slots_b = jnp.int32(0)
        for j in range(CAP):
            if mask >> j & 1:
                total_b = total_b + on_b[j]
                slots_b = slots_b + used[j]
            else:
                total_a = total_a + on_a[j]
                slots_a = slots_a + used[j]
        cost = jnp.maximum(total_a, total_b)
        cost = cost + jnp.where(cost > cap, 1000, 0)
        cost = cost + jnp.where(jnp.maximum(slots_a, slots_b) > 2, UNEVEN, 0)
        better = cost < best
        best = jnp.where(better, cost, best)
        chosen = jnp.where(better, mask, chosen)
    at_a = jnp.int32(0)
    at_b = jnp.int32(0)
    back = jnp.int32(0)
    for j in range(CAP):
        to_b = jnp.bitwise_and(chosen >> j, 1) * used[j]
        to_b = jnp.where(rows[j] == 0, 0, to_b)
        to_a = used[j] - to_b
        table[FIELDS * j] = to_a * AT_A + to_b * AT_B
        table[FIELDS * j + 1] = rows[j]
        table[FIELDS * j + 2] = info[who, 2 * j + 1]
        table[FIELDS * j + 3] = jnp.where(to_b == 1, at_b, at_a)
        table[FIELDS * j + 4] = jnp.where(to_b == 1, back, at_a)
        at_a = at_a + to_a * on_a[j]
        at_b = at_b + to_b * on_b[j]
        back = back + to_b * (on_b[j] - INT_GROUPS)


def slot_of(table, j):
    base = FIELDS * j
    return table[base], table[base + 1], table[base + 2], table[base + 3], table[base + 4]


def lane_blocks(col):
    first = col // LANES
    starts = [jnp.minimum(first + k, 7) * LANES for k in range(3)]
    return [pl.multiple_of(start, LANES) for start in starts], jnp.bitwise_and(col, LANES - 1)


WIDE = 3 * LANES


def near_columns(col):
    first = jnp.minimum(col // LANES, 5)
    skip = col // LANES - first
    starts = [pl.multiple_of(jnp.minimum(skip + k, 2) * LANES, LANES) for k in range(3)]
    return pl.ds(pl.multiple_of(first * LANES, LANES), WIDE), starts, jnp.bitwise_and(col, LANES - 1)


def lane_iota():
    return lax.broadcasted_iota(jnp.int32, (SUB, LANES), 1)


def load_group(field, plane, group, starts, shift):
    rows = pl.ds(pl.multiple_of(group * SUB, SUB), SUB)
    first = field[plane, rows, pl.ds(starts[0], LANES)]
    second = field[plane, rows, pl.ds(starts[1], LANES)]
    third = field[plane, rows, pl.ds(starts[2], LANES)]
    return jnp.where(lane_iota() >= shift, first, third), second


def add_group(total, plane, group, starts, shift, left, right):
    rows = pl.ds(pl.multiple_of(group * SUB, SUB), SUB)
    inside = lane_iota() >= shift
    total[plane, rows, pl.ds(starts[0], LANES)] += jnp.where(inside, left, 0.0)
    total[plane, rows, pl.ds(starts[1], LANES)] += right
    total[plane, rows, pl.ds(starts[2], LANES)] += jnp.where(inside, 0.0, left)


def fetch_columns(table, wanted, field, held, sem, base):
    for j in range(CAP):

        @pl.when(table[FIELDS * j] == wanted)
        def _():
            columns, _, _ = near_columns(table[FIELDS * j + 2])
            pltpu.make_async_copy(field.at[:, :, columns], held.at[base + j], sem.at[base + j]).start()


def copy_groups(held, out, at, offset, low, high, starts, shift):
    def body(group, carry):
        for plane in range(4):
            left, right = load_group(held.at[at], plane, group, starts, shift)
            out[offset + group, plane, :, :LANES] = left
            out[offset + group, plane, :, LANES:] = right
        return carry

    lax.fori_loop(low, high, body, 0)


def pack_to_b(table, field, intensity, out, held, sem, int_sem, base):
    def intensity_copy(j):
        _, row, _, start, _ = slot_of(table, j)
        after = start + GROUPS - row // SUB
        return pltpu.make_async_copy(intensity.at[j], out.at[pl.ds(after, INT_GROUPS)], int_sem.at[j])

    for j in range(CAP):

        @pl.when(table[FIELDS * j] == AT_B)
        def _():
            intensity_copy(j).start()

    for j in range(CAP):
        state, row, col, start, _ = slot_of(table, j)

        @pl.when(state == AT_B)
        def _():
            columns, starts, shift = near_columns(col)
            at = base + j
            pltpu.make_async_copy(field.at[:, :, columns], held.at[at], sem.at[at]).wait()
            copy_groups(held, out, at, start - row // SUB, row // SUB, GROUPS, starts, shift)
            intensity_copy(j).wait()


def pack_to_a(table, field, out, held, sem, base):
    for j in range(CAP):
        state, row, col, start, _ = slot_of(table, j)

        @pl.when(state == AT_A)
        def _():
            columns, starts, shift = near_columns(col)
            at = base + j
            pltpu.make_async_copy(field.at[:, :, columns], held.at[at], sem.at[at]).wait()
            copy_groups(held, out, at, start, 0, (row + SUB - 1) // SUB, starts, shift)


def pack_kernel(
    flags, info, field, intensity, inner, wide, narrow, table_in, table_out, again, held, sem, int_sem
):
    turn = flags[2]
    is_narrow = flags[1] == 1
    own, before = flags[3], flags[4]
    first_slot = jnp.where(is_narrow, NARROW_SLOTS * turn, CAP * turn)
    last_slot = jnp.where(is_narrow, NARROW_SLOTS * (turn + 1), CAP)
    cap = jnp.where(is_narrow, CAP_NARROW, CAP_WIDE)

    def outward(pack):
        @pl.when(is_narrow)
        def _():
            pack(narrow)

        @pl.when(jnp.logical_not(is_narrow))
        def _():
            pack(wide)

    @pl.when(flags[0] == 0)
    def _():
        decide(info, before, table_out, first_slot, last_slot, cap)
        fetch_columns(table_out, AT_A, field, held, sem, 0)
        decide(info, own, table_in, CAP * turn, CAP, CAP_WIDE)
        fetch_columns(table_in, AT_B, field, held, sem, CAP)
        outward(lambda out: pack_to_a(table_out, field, out, held, sem, 0))
        pack_to_b(table_in, field, intensity, inner, held, sem, int_sem, CAP)

    @pl.when(flags[0] == 1)
    def _():
        decide(info, own, table_out, first_slot, last_slot, cap)
        fetch_columns(table_out, AT_B, field, held, sem, 0)
        decide(info, before, table_in, CAP * turn, CAP, CAP_WIDE)
        fetch_columns(table_in, AT_A, field, held, sem, CAP)
        outward(lambda out: pack_to_b(table_out, field, intensity, out, held, sem, int_sem, 0))
        pack_to_a(table_in, field, inner, held, sem, CAP)

    def check(k, most):
        narrow_first = jnp.bitwise_and(k, 3) == 3
        return jnp.maximum(most, jnp.where(narrow_first, info[k, PLACE], 0))

    most = lax.fori_loop(0, info.shape[0], check, jnp.int32(0))
    again[0] = jnp.logical_and(turn == 0, most > NARROW_SLOTS).astype(jnp.int32)


def prepare_kernel(phases, shuffle, out, halves):
    for plane in range(2):
        halves[0] = phases[plane, :, :LANES]
        halves[1] = phases[plane, :, LANES:]
        for part in range(2):
            every = pl.ds(part, HALF, stride=2)
            x = jnp.concatenate([halves[0, every, :], halves[1, every, :]], axis=1)
            high = x.astype(bf16)
            rest = x - high.astype(f32)
            middle, low = split(rest)
            total = jnp.dot(high, shuffle[...], preferred_element_type=f32)
            total += jnp.dot(middle, shuffle[...], preferred_element_type=f32)
            total += jnp.dot(low, shuffle[...], preferred_element_type=f32)
            out[plane, part * HALF : (part + 1) * HALF, :] = total


def fetch_pieces(is_narrow, wide, narrow, got, sem):
    @pl.when(is_narrow)
    def _():
        pltpu.make_async_copy(narrow, got.at[pl.ds(0, CAP_NARROW)], sem).start()

    @pl.when(jnp.logical_not(is_narrow))
    def _():
        pltpu.make_async_copy(wide, got, sem).start()


def await_pieces(is_narrow, wide, narrow, got, sem):
    @pl.when(is_narrow)
    def _():
        pltpu.make_async_copy(narrow, got.at[pl.ds(0, CAP_NARROW)], sem).wait()

    @pl.when(jnp.logical_not(is_narrow))
    def _():
        pltpu.make_async_copy(wide, got, sem).wait()


def slots_kernel(between, flags, table, field, intensity, probe, kernel, forms, shuffle, wide, *rest):
    narrow = rest[0] if between else wide
    back_wide, back_narrow = (rest[1], rest[2]) if between else (rest[0], rest[0])
    tiles, held, got, tile, measured, twice, beam, work, entered, chosen = rest[3 if between else 1 : -4]
    held_sem, int_sem, got_sem, tile_sem = rest[-4:]
    is_a = flags[0] == (1 if between else 0)
    is_narrow = jnp.logical_and(between, flags[1] == 1)
    mine = jnp.where(is_a, AT_A, AT_B)
    if between:
        fetch_pieces(is_narrow, wide, narrow, got, got_sem)
    else:
        pltpu.make_async_copy(wide, got, got_sem).start()
    fetch_columns(table, mine, field, held, held_sem, 0)

    def intensity_copies(j):
        return [
            pltpu.make_async_copy(
                intensity.at[j, :, pl.ds(part * LANES, LANES)], measured.at[j, part], int_sem.at[j, part]
            )
            for part in range(2)
        ]

    for j in range(CAP):

        @pl.when(jnp.logical_and(is_a, table[FIELDS * j] == AT_A))
        def _():
            for copy in intensity_copies(j):
                copy.start()

    for plane in range(2):
        for part in range(2):
            cut = probe[plane, :, part * LANES : (part + 1) * LANES]
            twice[2 * plane + part, :WIN] = cut
            twice[2 * plane + part, WIN:] = cut
    found = jnp.int32(0)
    for j in range(CAP):
        chosen[j] = 0
    for j in range(CAP):
        state = table[FIELDS * j]

        @pl.when(state == mine)
        def _():
            chosen[found] = j

        found = found + (state == mine).astype(jnp.int32)
    if between:
        await_pieces(is_narrow, wide, narrow, got, got_sem)
    else:
        pltpu.make_async_copy(wide, got, got_sem).wait()
    sublane = lax.broadcasted_iota(jnp.int32, (SUB, LANES), 0)

    def load(m, j):
        _, row, col, start, _ = slot_of(table, j)
        columns, starts, shift = near_columns(col)
        low = row // SUB
        high = (row + SUB - 1) // SUB
        base = jnp.where(is_a, start, start - low)

        def own_groups(group, carry):
            rows = pl.ds(pl.multiple_of(group * SUB, SUB), SUB)
            for plane in range(4):
                lf, rt = load_group(held.at[j], plane, group, starts, shift)
                tile[m, plane, rows, :LANES] = lf
                tile[m, plane, rows, LANES:] = rt
            return carry

        def their_groups(group, carry):
            rows = pl.ds(pl.multiple_of(group * SUB, SUB), SUB)
            for plane in range(4):
                tile[m, plane, rows, :] = got[base + group, plane]
            return carry

        lax.fori_loop(jnp.where(is_a, 0, low), jnp.where(is_a, high, GROUPS), their_groups, 0)
        lax.fori_loop(jnp.where(is_a, high, 0), jnp.where(is_a, GROUPS, low), own_groups, 0)

        @pl.when(low < high)
        def _():
            own = (low * SUB + sublane < row).astype(jnp.int32) == jnp.where(is_a, 0, 1)
            rows = pl.ds(pl.multiple_of(low * SUB, SUB), SUB)
            for plane in range(4):
                lf, rt = load_group(held.at[j], plane, low, starts, shift)
                tile[m, plane, rows, :LANES] = jnp.where(own, lf, tile[m, plane, rows, :LANES])
                tile[m, plane, rows, LANES:] = jnp.where(own, rt, tile[m, plane, rows, LANES:])

        @pl.when(jnp.logical_not(is_a))
        def _():
            after = start + GROUPS - low

            def unpack(group, carry):
                for plane in range(4):
                    rows = pl.ds(pl.multiple_of((group * 4 + plane) * SUB, SUB), SUB)
                    measured[j, 0, rows, :] = got[after + group, plane, :, :LANES]
                    measured[j, 1, rows, :] = got[after + group, plane, :, LANES:]
                return carry

            lax.fori_loop(0, INT_GROUPS, unpack, 0)

        for plane in range(2):
            parts = [twice[2 * plane + part, pl.ds(WIN - row, WIN), :] for part in range(2)]
            beam[m, plane] = pltpu.roll(jnp.concatenate(parts, axis=1), shift, 1)

    def arrive(j):
        columns, _, _ = near_columns(table[FIELDS * j + 2])
        pltpu.make_async_copy(field.at[:, :, columns], held.at[j], held_sem.at[j]).wait()

        @pl.when(is_a)
        def _():
            for copy in intensity_copies(j):
                copy.wait()

    def store_rows(m, e, o):
        work[m, 0, :HALF], work[m, 1, :HALF] = e[:HALF], e[HALF:]
        work[m, 0, HALF:], work[m, 1, HALF:] = o[:HALF], o[HALF:]

    def middle(pointwise, members, slots=None):
        for half in range(2):
            rows = pl.ds(half * HALF, HALF)
            for m in range(members):
                re, im = lanes_forward(work[m, 0, rows, :], work[m, 1, rows, :], forms)
                re, im = pointwise(m, half, rows, re, im, slots)
                re, im = lanes_inverse(re, im, forms)
                work[m, 0, rows, :], work[m, 1, rows, :] = re, im

    def rows_back(m):
        u, v = rows_inverse(work[m, 0], work[m, 1], forms)
        return (
            jnp.concatenate([u[:HALF] + v[:HALF], u[:HALF] - v[:HALF]], axis=0),
            jnp.concatenate([u[HALF:] + v[HALF:], u[HALF:] - v[HALF:]], axis=0),
        )

    def propagate(m, half, rows, re, im, slots):
        return cmul(kernel[0, rows, :], kernel[1, rows, :], re, im)

    def propagate_back(m, half, rows, re, im, slots):
        return cmul_conj(kernel[0, rows, :], kernel[1, rows, :], re, im)

    def residual(m, half, rows, re, im, slots):
        every = pl.ds(half, HALF, stride=2)
        at = slots[m]
        rows_of = jnp.concatenate([measured[at, 0, every, :], measured[at, 1, every, :]], axis=1)
        high, low = split(rows_of)
        wanted = jnp.dot(high, shuffle[...], preferred_element_type=f32)
        wanted += jnp.dot(low, shuffle[...], preferred_element_type=f32)
        scale = re * re + im * im - wanted
        return scale * re, scale * im

    def tile_copy(m, j):
        return pltpu.make_async_copy(tile.at[m], tiles.at[j], tile_sem.at[m])

    def write(m, j):
        _, row, _, _, back = slot_of(table, j)
        low = row // SUB

        def send(out, offset):
            def body(group, carry):
                rows = pl.ds(pl.multiple_of(group * SUB, SUB), SUB)
                for plane in range(4):
                    out[offset + group, plane] = tile[m, plane, rows, :]
                return carry

            return body

        tile_copy(m, j).start()

        offset = jnp.where(is_a, back, back - low)
        lower = jnp.where(is_a, 0, low)
        upper = jnp.where(is_a, (row + SUB - 1) // SUB, GROUPS)
        if between:

            @pl.when(is_narrow)
            def _():
                lax.fori_loop(lower, upper, send(back_narrow, offset), 0)

            @pl.when(jnp.logical_not(is_narrow))
            def _():
                lax.fori_loop(lower, upper, send(back_wide, offset), 0)

        else:
            lax.fori_loop(lower, upper, send(back_wide, offset), 0)

    def run(p, members):
        full = 2 * p + members <= found
        last = jnp.where(full, 2 * p + members - 1, 2 * p)
        slots = [chosen[2 * p], chosen[last]][:members]

        @pl.when(p > 0)
        def _():
            tile_copy(0, 0).wait()
            tile_copy(1, 0).wait()

        arrive(slots[0])
        if members == 2:

            @pl.when(full)
            def _():
                arrive(slots[1])

        for m in range(members):
            load(m, slots[m])
        for m in range(members):
            re, im = cmul(beam[m, 0], beam[m, 1], tile[m, 0], tile[m, 1])
            store_rows(m, *rows_forward(re, im, forms))
        middle(propagate, members)
        for m in range(members):
            re, im = rows_back(m)
            entered[m, 0], entered[m, 1] = re, im
            re, im = cmul(re, im, tile[m, 2], tile[m, 3])
            store_rows(m, *rows_forward(re, im, forms))
        middle(residual, members, slots)
        for m in range(members):
            br, bi = rows_back(m)
            re, im = cmul_conj(tile[m, 2], tile[m, 3], br, bi)
            tile[m, 2], tile[m, 3] = cmul_conj(entered[m, 0], entered[m, 1], br, bi)
            store_rows(m, *rows_forward(re, im, forms))
        middle(propagate_back, members)
        for m in range(members):
            br, bi = rows_back(m)
            tile[m, 0], tile[m, 1] = cmul_conj(beam[m, 0], beam[m, 1], br, bi)
        write(0, slots[0])
        if members == 2:

            @pl.when(full)
            def _():
                write(1, slots[1])

    def pair(p, carry):
        run(p, 2)
        return carry

    alone = jnp.bitwise_and(found, 1) == 1
    if between:
        lax.fori_loop(0, found // 2, pair, 0)

        @pl.when(alone)
        def _():
            run(found // 2, 1)

    else:
        lax.fori_loop(0, (found + 1) // 2, pair, 0)

    @pl.when(found > 0)
    def _():
        tile_copy(0, 0).wait()

    @pl.when(jnp.logical_and(found > 0, jnp.logical_not(alone)))
    def _():
        tile_copy(1, 0).wait()


def add_back(is_a, table, got, total, planes):
    theirs = jnp.where(is_a, AT_B, AT_A)
    for j in range(CAP):
        state, row, col, _, back = slot_of(table, j)

        @pl.when(state == theirs)
        def _():
            starts, shift = lane_blocks(col)
            low = row // SUB
            base = jnp.where(is_a, back - low, back)
            sublane = lax.broadcasted_iota(jnp.int32, (SUB, LANES), 0)

            def body(group, carry):
                below = (group * SUB + sublane < row).astype(jnp.int32)
                own = below == jnp.where(is_a, 0, 1)
                for plane in planes:
                    lf = jnp.where(own, got[base + group, plane, :, :LANES], 0.0)
                    rt = jnp.where(own, got[base + group, plane, :, LANES:], 0.0)
                    add_group(total, plane, group, starts, shift, lf, rt)
                return carry

            lax.fori_loop(jnp.where(is_a, low, 0), jnp.where(is_a, GROUPS, (row + SUB - 1) // SUB), body, 0)


def sum_kernel(
    flags, table_in, table_out, in_back, tiles_in, tiles_out, grad, total, got, tile, got_sem, tile_sem, total_sem
):
    pltpu.make_async_copy(in_back, got, got_sem).start()
    sublane = lax.broadcasted_iota(jnp.int32, (SUB, LANES), 0)
    kinds = ((flags[0] == 0, table_in, tiles_in), (flags[0] == 1, table_out, tiles_out))
    for k, (is_a, table, tiles) in enumerate(kinds):
        mine = jnp.where(is_a, AT_A, AT_B)
        for j in range(CAP):

            @pl.when(table[FIELDS * j] == mine)
            def _():
                pltpu.make_async_copy(tiles.at[j], tile.at[k * CAP + j], tile_sem.at[k * CAP + j]).start()

    @pl.when(flags[2] == 0)
    def _():
        total[...] = jnp.zeros_like(total)

    @pl.when(flags[2] > 0)
    def _():
        copy = pltpu.make_async_copy(grad, total, total_sem)
        copy.start()
        copy.wait()

    pltpu.make_async_copy(in_back, got, got_sem).wait()
    add_back(flags[0] == 0, table_in, got, total, range(4))
    for k, (is_a, table, tiles) in enumerate(kinds):
        mine = jnp.where(is_a, AT_A, AT_B)
        for j in range(CAP):
            state, row, col, _, _ = slot_of(table, j)

            @pl.when(state == mine)
            def _():
                at = k * CAP + j
                pltpu.make_async_copy(tiles.at[j], tile.at[at], tile_sem.at[at]).wait()
                starts, shift = lane_blocks(col)
                low = row // SUB

                def body(group, carry):
                    below = (group * SUB + sublane < row).astype(jnp.int32)
                    own = below == jnp.where(is_a, 0, 1)
                    rows = pl.ds(pl.multiple_of(group * SUB, SUB), SUB)
                    for plane in range(4):
                        lf = jnp.where(own, tile[at, plane, rows, :LANES], 0.0)
                        rt = jnp.where(own, tile[at, plane, rows, LANES:], 0.0)
                        add_group(total, plane, group, starts, shift, lf, rt)
                    return carry

                lax.fori_loop(
                    jnp.where(is_a, low, 0), jnp.where(is_a, GROUPS, (row + SUB - 1) // SUB), body, 0
                )


def finish_kernel(flags, table, total_in, wide, narrow, grad, total, got, got_sem, out_sem):
    is_narrow = flags[1] == 1
    fetch_pieces(is_narrow, wide, narrow, got, got_sem)
    await_pieces(is_narrow, wide, narrow, got, got_sem)
    for plane in range(4):
        total[plane] = total_in[plane]
        add_back(flags[0] == 1, table, got, total, (plane,))
        pltpu.make_async_copy(total.at[plane], grad.at[plane], out_sem.at[plane]).start()
    for plane in range(4):
        pltpu.make_async_copy(total.at[plane], grad.at[plane], out_sem.at[plane]).wait()


def spec(space):
    return pl.BlockSpec(memory_space=space)


def vmem(mib):
    return pltpu.CompilerParams(vmem_limit_bytes=mib << 20)


def packed(groups):
    return jax.ShapeDtypeStruct((groups, 4, SUB, WIN), f32)


def run_slots(flags, table, field, intensity, probe, kernel, tables, *pieces):
    between = len(pieces) == 2
    backs = (CAP_WIDE, CAP_NARROW)[: len(pieces)]
    return pl.pallas_call(
        functools.partial(slots_kernel, between),
        out_shape=tuple(packed(n) for n in backs) + (HB((CAP, 4, WIN, WIN), f32),),
        in_specs=[spec(SM)] * 2 + [spec(HB)] * 2 + [spec(VM)] * 4 + [spec(pl.ANY)] * len(pieces),
        out_specs=(spec(VM),) * len(backs) + (spec(HB),),
        scratch_shapes=[
            pltpu.VMEM((CAP, 4, WIN, WIDE), f32),
            pltpu.VMEM((CAP_WIDE, 4, SUB, WIN), f32),
            pltpu.VMEM((2, 4, WIN, WIN), f32),
            pltpu.VMEM((CAP, 2, WIN, LANES), f32),
            pltpu.VMEM((4, 2 * WIN, LANES), f32),
            pltpu.VMEM((2, 2, WIN, WIN), f32),
            pltpu.VMEM((2, 2, WIN, WIN), f32),
            pltpu.VMEM((2, 2, WIN, WIN), f32),
            pltpu.SMEM((CAP,), jnp.int32),
            pltpu.SemaphoreType.DMA((CAP,)),
            pltpu.SemaphoreType.DMA((CAP, 2)),
            pltpu.SemaphoreType.DMA,
            pltpu.SemaphoreType.DMA((2,)),
        ],
        cost_estimate=CHEAP,
        compiler_params=vmem(24),
    )(flags, table, field, intensity, probe, kernel, *tables, *pieces)


def both_ways(pairs):
    return pairs + [(b, a) for a, b in pairs]


def one_round(turn, grad, field, maps, intensity, probe_wave, prop_phase, info):
    count = lax.axis_size("row")
    within = both_ways([(i, i + 1) for i in range(0, count - 1, 2)])
    wide_pairs = both_ways([(i, i + 1) for i in range(1, count - 1, 4)])
    narrow_pairs = both_ways([(i, i + 1) for i in range(3, count - 1, 4)])
    move = lambda x, pairs: lax.ppermute(x, "row", pairs)
    place = lax.axis_index("row")
    odd = jnp.bitwise_and(place, 1)
    is_narrow = (jnp.bitwise_and(place + 1, 2) == 0).astype(jnp.int32)
    own = lax.axis_index("groups") * count + place
    flags = jnp.stack([odd, is_narrow, turn, own, jnp.where(place == 0, -1, own - 1)])
    prop_phase, _ = lax.optimization_barrier((prop_phase, turn))

    table = jax.ShapeDtypeStruct((CAP * FIELDS,), jnp.int32)
    inner, wide, narrow, table_in, table_out, again = pl.pallas_call(
        pack_kernel,
        out_shape=(
            packed(CAP_WIDE),
            packed(CAP_WIDE),
            packed(CAP_NARROW),
            table,
            table,
            jax.ShapeDtypeStruct((1,), jnp.int32),
        ),
        in_specs=[spec(SM)] * 2 + [spec(HB)] * 2,
        out_specs=(spec(VM),) * 3 + (spec(SM),) * 3,
        scratch_shapes=[
            pltpu.VMEM((2 * CAP, 4, WIN, WIDE), f32),
            pltpu.SemaphoreType.DMA((2 * CAP,)),
            pltpu.SemaphoreType.DMA((CAP,)),
        ],
        cost_estimate=CHEAP,
        compiler_params=vmem(24),
    )(flags, info, field, maps)
    wide = move(wide, wide_pairs)
    narrow = move(narrow, narrow_pairs)
    inner = move(inner, within)

    forms, shuffle = (jnp.asarray(t) for t in make_tables())
    kernel = pl.pallas_call(
        prepare_kernel,
        out_shape=jax.ShapeDtypeStruct((2, WIN, WIN), f32),
        in_specs=[spec(VM)] * 2,
        out_specs=spec(VM),
        scratch_shapes=[pltpu.VMEM((2, WIN, LANES), f32)],
        cost_estimate=CHEAP,
        compiler_params=vmem(8),
    )(jnp.stack([jnp.cos(prop_phase), jnp.sin(prop_phase)]), shuffle)

    args = (field, intensity, probe_wave, kernel, (forms, shuffle))
    in_back, tiles_in = run_slots(flags, table_in, *args, inner)
    in_back = move(in_back, within)
    back_wide, back_narrow, tiles_out = run_slots(flags, table_out, *args, wide, narrow)
    tiles_in = pltpu.with_memory_space_constraint(tiles_in, HB)
    tiles_out = pltpu.with_memory_space_constraint(tiles_out, HB)
    back_wide = move(back_wide, wide_pairs)
    back_narrow = move(back_narrow, narrow_pairs)
    total = pl.pallas_call(
        sum_kernel,
        out_shape=jax.ShapeDtypeStruct(field.shape, f32),
        in_specs=[spec(SM)] * 3 + [spec(pl.ANY)] * 3 + [spec(HB)],
        out_specs=spec(VM),
        scratch_shapes=[
            pltpu.VMEM((CAP_WIDE, 4, SUB, WIN), f32),
            pltpu.VMEM((2 * CAP, 4, WIN, WIN), f32),
            pltpu.SemaphoreType.DMA,
            pltpu.SemaphoreType.DMA((2 * CAP,)),
            pltpu.SemaphoreType.DMA,
        ],
        cost_estimate=CHEAP,
        compiler_params=vmem(20),
    )(flags, table_in, table_out, in_back, tiles_in, tiles_out, grad)
    grad = pl.pallas_call(
        finish_kernel,
        out_shape=jax.ShapeDtypeStruct(field.shape, f32),
        in_specs=[spec(SM)] * 2 + [spec(VM)] + [spec(pl.ANY)] * 2,
        out_specs=spec(HB),
        scratch_shapes=[
            pltpu.VMEM(field.shape, f32),
            pltpu.VMEM((CAP_WIDE, 4, SUB, WIN), f32),
            pltpu.SemaphoreType.DMA,
            pltpu.SemaphoreType.DMA((4,)),
        ],
        cost_estimate=CHEAP,
        compiler_params=vmem(16),
    )(flags, table_out, total, back_wide, back_narrow)
    return grad, again[0]


def shards(obj_field, probe_wave, prop_phase, win_offsets, live_counts, intensity):
    field = pltpu.with_memory_space_constraint(obj_field.reshape((4,) + obj_field.shape[2:]), HB)
    maps = pltpu.with_memory_space_constraint(intensity.reshape(CAP, INT_GROUPS, 4, SUB, WIN), HB)
    intensity = pltpu.with_memory_space_constraint(intensity, HB)
    axes = ("groups", "row")
    count = lax.axis_size("groups") * lax.axis_size("row")
    own = jnp.concatenate([win_offsets.reshape(-1), live_counts, jnp.zeros((INFO - PLACE - 1,), jnp.int32)])
    info = lax.all_to_all(jnp.broadcast_to(own, (count, 1, INFO)), axes, 0, 0, tiled=True).reshape(count, INFO)

    def body(state):
        turn, _, grad = state
        grad, again = one_round(turn, grad, field, maps, intensity, probe_wave, prop_phase, info)
        return turn + 1, again, grad

    empty = pl.pallas_call(
        lambda out: None,
        out_shape=jax.ShapeDtypeStruct(field.shape, f32),
        out_specs=spec(HB),
    )()
    _, _, grad = lax.while_loop(lambda state: state[1] > 0, body, (jnp.int32(0), jnp.int32(1), empty))
    return grad.reshape(obj_field.shape)


def solution(mesh):
    in_specs = (
        P(None, None, ("groups", "row"), None),
        P("groups", None, None),
        P(),
        P(("groups", "row"), None),
        P(("groups", "row")),
        P(("groups", "row"), None, None),
    )
    out_specs = P(None, None, ("groups", "row"), None)
    return jax.shard_map(shards, mesh=mesh, in_specs=in_specs, out_specs=out_specs, check_vma=False)
```

```python
import functools

import jax
import jax.numpy as jnp
import numpy as np
from jax import lax
from jax.experimental import pallas as pl
from jax.experimental.pallas import tpu as pltpu
from jax.sharding import PartitionSpec as P

WIN = 256
HALF = WIN // 2
LANES = 128
SUB = 8
CAP = 4
GROUPS = WIN // SUB
INT_GROUPS = GROUPS // 4
CAP_WIDE = 48
CAP_NARROW = 28
NARROW_SLOTS = 2
CAP_INNER = 64
UNEVEN = 100
DEAD, AT_A, AT_B = 0, 1, 2
FIELDS = 8
f32 = jnp.float32
bf16 = jnp.bfloat16
VM = pltpu.MemorySpace.VMEM
SM = pltpu.MemorySpace.SMEM
HB = pltpu.MemorySpace.HBM
CHEAP = pl.CostEstimate(flops=1, transcendentals=0, bytes_accessed=1)


def real_tables():
    k = np.arange(HALF)[:, None]
    n = np.arange(HALF)[None, :]
    out = []
    for odd in (0, 1):
        angle = 2.0 * np.pi * (((2 * k + odd) * n) % WIN) / WIN
        c, s = np.cos(angle) / 16.0, np.sin(angle) / 16.0
        out.append(np.block([[c, s], [-s, c]]))
    return out


def high_low(table):
    high = table.astype(np.float32).astype(bf16)
    low = (table - high.astype(np.float64)).astype(np.float32).astype(bf16)
    return high, low


def make_tables():
    even, odd = real_tables()
    forms = np.stack([np.stack(high_low(m)) for m in (even, odd, even.T, odd.T)])
    order = np.concatenate([np.arange(0, WIN, 2), np.arange(1, WIN, 2)])
    shuffle = np.zeros((WIN, WIN), np.float32)
    shuffle[order, np.arange(WIN)] = 1.0
    return forms, shuffle.astype(bf16)


EVEN, ODD, EVEN_T, ODD_T = range(4)


def split(x):
    high = x.astype(bf16)
    return high, (x - high.astype(f32)).astype(bf16)


def left_mul(forms, which, x):
    high, low = split(x)
    t_high, t_low = forms[which, 0], forms[which, 1]
    wide = jnp.concatenate([t_high, t_low, t_high], axis=1)
    return jnp.dot(wide, jnp.concatenate([high, high, low], axis=0), preferred_element_type=f32)


def right_mul(x, forms, which):
    high, low = split(x)
    t_high, t_low = forms[which, 0], forms[which, 1]
    tall = jnp.concatenate([t_high, t_high, t_low], axis=0)
    return jnp.dot(jnp.concatenate([high, low, high], axis=1), tall, preferred_element_type=f32)


def rows_forward(re, im, forms):
    tr, br, ti, bi = re[:HALF], re[HALF:], im[:HALF], im[HALF:]
    e = left_mul(forms, EVEN, jnp.concatenate([tr + br, ti + bi], axis=0))
    o = left_mul(forms, ODD, jnp.concatenate([tr - br, ti - bi], axis=0))
    return e, o


def rows_inverse(re, im, forms):
    u = left_mul(forms, EVEN_T, jnp.concatenate([re[:HALF], im[:HALF]], axis=0))
    v = left_mul(forms, ODD_T, jnp.concatenate([re[HALF:], im[HALF:]], axis=0))
    return u, v


def lanes_forward(re, im, forms):
    lr, rr, li, ri = re[:, :HALF], re[:, HALF:], im[:, :HALF], im[:, HALF:]
    e = right_mul(jnp.concatenate([lr + rr, li + ri], axis=1), forms, EVEN_T)
    o = right_mul(jnp.concatenate([lr - rr, li - ri], axis=1), forms, ODD_T)
    return (
        jnp.concatenate([e[:, :HALF], o[:, :HALF]], axis=1),
        jnp.concatenate([e[:, HALF:], o[:, HALF:]], axis=1),
    )


def lanes_inverse(re, im, forms):
    u = right_mul(jnp.concatenate([re[:, :HALF], im[:, :HALF]], axis=1), forms, EVEN)
    v = right_mul(jnp.concatenate([re[:, HALF:], im[:, HALF:]], axis=1), forms, ODD)
    return (
        jnp.concatenate([u[:, :HALF] + v[:, :HALF], u[:, :HALF] - v[:, :HALF]], axis=1),
        jnp.concatenate([u[:, HALF:] + v[:, HALF:], u[:, HALF:] - v[:, HALF:]], axis=1),
    )


def cmul(ar, ai, br, bi):
    return ar * br - ai * bi, ar * bi + ai * br


def cmul_conj(ar, ai, br, bi):
    return ar * br + ai * bi, ar * bi - ai * br


INFO = LANES
PLACE = 2 * CAP


def decide(info, who, table, first_slot, last_slot, cap):
    count = jnp.where(who < 0, 0, info[jnp.maximum(who, 0), PLACE])
    who = jnp.maximum(who, 0)
    rows = [jnp.bitwise_and(info[who, 2 * j], WIN - 1) for j in range(CAP)]
    last_slot = jnp.minimum(last_slot, count)
    used = [jnp.logical_and(j >= first_slot, j < last_slot).astype(jnp.int32) for j in range(CAP)]
    on_a = [used[j] * ((rows[j] + SUB - 1) // SUB) for j in range(CAP)]
    on_b = [used[j] * (GROUPS - rows[j] // SUB + INT_GROUPS) for j in range(CAP)]
    best, chosen = jnp.int32(10000), jnp.int32(0)
    for mask in range(1 << CAP):
        total_a = jnp.int32(0)
        total_b = jnp.int32(0)
        slots_a = jnp.int32(0)
        slots_b = jnp.int32(0)
        for j in range(CAP):
            if mask >> j & 1:
                total_b = total_b + on_b[j]
                slots_b = slots_b + used[j]
            else:
                total_a = total_a + on_a[j]
                slots_a = slots_a + used[j]
        cost = jnp.maximum(total_a, total_b)
        cost = cost + jnp.where(cost > cap, 1000, 0)
        cost = cost + jnp.where(jnp.maximum(slots_a, slots_b) > 2, UNEVEN, 0)
        better = cost < best
        best = jnp.where(better, cost, best)
        chosen = jnp.where(better, mask, chosen)
    at_a = jnp.int32(0)
    at_b = jnp.int32(0)
    back = jnp.int32(0)
    for j in range(CAP):
        to_b = jnp.bitwise_and(chosen >> j, 1) * used[j]
        to_b = jnp.where(rows[j] == 0, 0, to_b)
        to_a = used[j] - to_b
        table[FIELDS * j] = to_a * AT_A + to_b * AT_B
        table[FIELDS * j + 1] = rows[j]
        table[FIELDS * j + 2] = info[who, 2 * j + 1]
        table[FIELDS * j + 3] = jnp.where(to_b == 1, at_b, at_a)
        table[FIELDS * j + 4] = jnp.where(to_b == 1, back, at_a)
        at_a = at_a + to_a * on_a[j]
        at_b = at_b + to_b * on_b[j]
        back = back + to_b * (on_b[j] - INT_GROUPS)


def slot_of(table, j):
    base = FIELDS * j
    return table[base], table[base + 1], table[base + 2], table[base + 3], table[base + 4]


def lane_blocks(col):
    first = col // LANES
    starts = [jnp.minimum(first + k, 7) * LANES for k in range(3)]
    return [pl.multiple_of(start, LANES) for start in starts], jnp.bitwise_and(col, LANES - 1)


WIDE = 3 * LANES


def near_columns(col):
    first = jnp.minimum(col // LANES, 5)
    skip = col // LANES - first
    starts = [pl.multiple_of(jnp.minimum(skip + k, 2) * LANES, LANES) for k in range(3)]
    return pl.ds(pl.multiple_of(first * LANES, LANES), WIDE), starts, jnp.bitwise_and(col, LANES - 1)


def lane_iota():
    return lax.broadcasted_iota(jnp.int32, (SUB, LANES), 1)


def load_group(field, plane, group, starts, shift):
    rows = pl.ds(pl.multiple_of(group * SUB, SUB), SUB)
    first = field[plane, rows, pl.ds(starts[0], LANES)]
    second = field[plane, rows, pl.ds(starts[1], LANES)]
    third = field[plane, rows, pl.ds(starts[2], LANES)]
    return jnp.where(lane_iota() >= shift, first, third), second


def add_group(total, plane, group, starts, shift, left, right):
    rows = pl.ds(pl.multiple_of(group * SUB, SUB), SUB)
    inside = lane_iota() >= shift
    total[plane, rows, pl.ds(starts[0], LANES)] += jnp.where(inside, left, 0.0)
    total[plane, rows, pl.ds(starts[1], LANES)] += right
    total[plane, rows, pl.ds(starts[2], LANES)] += jnp.where(inside, 0.0, left)


def fetch_columns(table, wanted, field, held, sem, base):
    for j in range(CAP):

        @pl.when(table[FIELDS * j] == wanted)
        def _():
            columns, _, _ = near_columns(table[FIELDS * j + 2])
            pltpu.make_async_copy(field.at[:, :, columns], held.at[base + j], sem.at[base + j]).start()


def copy_groups(held, out, at, offset, low, high, starts, shift):
    def body(group, carry):
        for plane in range(4):
            left, right = load_group(held.at[at], plane, group, starts, shift)
            out[offset + group, plane, :, :LANES] = left
            out[offset + group, plane, :, LANES:] = right
        return carry

    lax.fori_loop(low, high, body, 0)


def pack_to_b(table, field, intensity, out, held, sem, int_sem, base):
    def intensity_copy(j):
        _, row, _, start, _ = slot_of(table, j)
        after = start + GROUPS - row // SUB
        return pltpu.make_async_copy(intensity.at[j], out.at[pl.ds(after, INT_GROUPS)], int_sem.at[j])

    for j in range(CAP):

        @pl.when(table[FIELDS * j] == AT_B)
        def _():
            intensity_copy(j).start()

    for j in range(CAP):
        state, row, col, start, _ = slot_of(table, j)

        @pl.when(state == AT_B)
        def _():
            columns, starts, shift = near_columns(col)
            at = base + j
            pltpu.make_async_copy(field.at[:, :, columns], held.at[at], sem.at[at]).wait()
            copy_groups(held, out, at, start - row // SUB, row // SUB, GROUPS, starts, shift)
            intensity_copy(j).wait()


def pack_to_a(table, field, out, held, sem, base):
    for j in range(CAP):
        state, row, col, start, _ = slot_of(table, j)

        @pl.when(state == AT_A)
        def _():
            columns, starts, shift = near_columns(col)
            at = base + j
            pltpu.make_async_copy(field.at[:, :, columns], held.at[at], sem.at[at]).wait()
            copy_groups(held, out, at, start, 0, (row + SUB - 1) // SUB, starts, shift)


def pack_kernel(
    flags, info, field, intensity, inner, wide, narrow, table_in, table_out, again, held, sem, int_sem
):
    turn = flags[2]
    is_narrow = flags[1] == 1
    own, before = flags[3], flags[4]
    first_slot = jnp.where(is_narrow, NARROW_SLOTS * turn, CAP * turn)
    last_slot = jnp.where(is_narrow, NARROW_SLOTS * (turn + 1), CAP)
    cap = jnp.where(is_narrow, CAP_NARROW, CAP_WIDE)

    def outward(pack):
        @pl.when(is_narrow)
        def _():
            pack(narrow)

        @pl.when(jnp.logical_not(is_narrow))
        def _():
            pack(wide)

    @pl.when(flags[0] == 0)
    def _():
        decide(info, before, table_out, first_slot, last_slot, cap)
        fetch_columns(table_out, AT_A, field, held, sem, 0)
        decide(info, own, table_in, CAP * turn, CAP, CAP_INNER)
        fetch_columns(table_in, AT_B, field, held, sem, CAP)
        outward(lambda out: pack_to_a(table_out, field, out, held, sem, 0))
        pack_to_b(table_in, field, intensity, inner, held, sem, int_sem, CAP)

    @pl.when(flags[0] == 1)
    def _():
        decide(info, own, table_out, first_slot, last_slot, cap)
        fetch_columns(table_out, AT_B, field, held, sem, 0)
        decide(info, before, table_in, CAP * turn, CAP, CAP_INNER)
        fetch_columns(table_in, AT_A, field, held, sem, CAP)
        outward(lambda out: pack_to_b(table_out, field, intensity, out, held, sem, int_sem, 0))
        pack_to_a(table_in, field, inner, held, sem, CAP)

    def check(k, most):
        narrow_first = jnp.bitwise_and(k, 3) == 3
        return jnp.maximum(most, jnp.where(narrow_first, info[k, PLACE], 0))

    most = lax.fori_loop(0, info.shape[0], check, jnp.int32(0))
    again[0] = jnp.logical_and(turn == 0, most > NARROW_SLOTS).astype(jnp.int32)


def prepare_kernel(phases, shuffle, out, halves):
    for plane in range(2):
        halves[0] = phases[plane, :, :LANES]
        halves[1] = phases[plane, :, LANES:]
        for part in range(2):
            every = pl.ds(part, HALF, stride=2)
            x = jnp.concatenate([halves[0, every, :], halves[1, every, :]], axis=1)
            high = x.astype(bf16)
            rest = x - high.astype(f32)
            middle, low = split(rest)
            total = jnp.dot(high, shuffle[...], preferred_element_type=f32)
            total += jnp.dot(middle, shuffle[...], preferred_element_type=f32)
            total += jnp.dot(low, shuffle[...], preferred_element_type=f32)
            out[plane, part * HALF : (part + 1) * HALF, :] = total


def fetch_pieces(is_narrow, wide, narrow, got, sem):
    @pl.when(is_narrow)
    def _():
        pltpu.make_async_copy(narrow, got.at[pl.ds(0, CAP_NARROW)], sem).start()

    @pl.when(jnp.logical_not(is_narrow))
    def _():
        pltpu.make_async_copy(wide, got, sem).start()


def await_pieces(is_narrow, wide, narrow, got, sem):
    @pl.when(is_narrow)
    def _():
        pltpu.make_async_copy(narrow, got.at[pl.ds(0, CAP_NARROW)], sem).wait()

    @pl.when(jnp.logical_not(is_narrow))
    def _():
        pltpu.make_async_copy(wide, got, sem).wait()


def slots_kernel(between, flags, table, field, intensity, probe, kernel, forms, shuffle, wide, *rest):
    narrow = rest[0] if between else wide
    back_wide, back_narrow = (rest[1], rest[2]) if between else (rest[0], rest[0])
    tiles, held, got, tile, measured, twice, beam, work, entered, chosen = rest[3 if between else 1 : -4]
    held_sem, int_sem, got_sem, tile_sem = rest[-4:]
    is_a = flags[0] == (1 if between else 0)
    is_narrow = jnp.logical_and(between, flags[1] == 1)
    mine = jnp.where(is_a, AT_A, AT_B)
    if between:
        fetch_pieces(is_narrow, wide, narrow, got, got_sem)
    else:
        pltpu.make_async_copy(wide, got, got_sem).start()
    fetch_columns(table, mine, field, held, held_sem, 0)

    def intensity_copies(j):
        return [
            pltpu.make_async_copy(
                intensity.at[j, :, pl.ds(part * LANES, LANES)], measured.at[j, part], int_sem.at[j, part]
            )
            for part in range(2)
        ]

    for j in range(CAP):

        @pl.when(jnp.logical_and(is_a, table[FIELDS * j] == AT_A))
        def _():
            for copy in intensity_copies(j):
                copy.start()

    for plane in range(2):
        for part in range(2):
            cut = probe[plane, :, part * LANES : (part + 1) * LANES]
            twice[2 * plane + part, :WIN] = cut
            twice[2 * plane + part, WIN:] = cut
    found = jnp.int32(0)
    for j in range(CAP):
        chosen[j] = 0
    for j in range(CAP):
        state = table[FIELDS * j]

        @pl.when(state == mine)
        def _():
            chosen[found] = j

        found = found + (state == mine).astype(jnp.int32)
    if between:
        await_pieces(is_narrow, wide, narrow, got, got_sem)
    else:
        pltpu.make_async_copy(wide, got, got_sem).wait()
    sublane = lax.broadcasted_iota(jnp.int32, (SUB, LANES), 0)

    def load(m, j):
        _, row, col, start, _ = slot_of(table, j)
        columns, starts, shift = near_columns(col)
        low = row // SUB
        high = (row + SUB - 1) // SUB
        base = jnp.where(is_a, start, start - low)

        def own_groups(group, carry):
            rows = pl.ds(pl.multiple_of(group * SUB, SUB), SUB)
            for plane in range(4):
                lf, rt = load_group(held.at[j], plane, group, starts, shift)
                tile[m, plane, rows, :LANES] = lf
                tile[m, plane, rows, LANES:] = rt
            return carry

        def their_groups(group, carry):
            rows = pl.ds(pl.multiple_of(group * SUB, SUB), SUB)
            for plane in range(4):
                tile[m, plane, rows, :] = got[base + group, plane]
            return carry

        lax.fori_loop(jnp.where(is_a, 0, low), jnp.where(is_a, high, GROUPS), their_groups, 0)
        lax.fori_loop(jnp.where(is_a, high, 0), jnp.where(is_a, GROUPS, low), own_groups, 0)

        @pl.when(low < high)
        def _():
            own = (low * SUB + sublane < row).astype(jnp.int32) == jnp.where(is_a, 0, 1)
            rows = pl.ds(pl.multiple_of(low * SUB, SUB), SUB)
            for plane in range(4):
                lf, rt = load_group(held.at[j], plane, low, starts, shift)
                tile[m, plane, rows, :LANES] = jnp.where(own, lf, tile[m, plane, rows, :LANES])
                tile[m, plane, rows, LANES:] = jnp.where(own, rt, tile[m, plane, rows, LANES:])

        @pl.when(jnp.logical_not(is_a))
        def _():
            after = start + GROUPS - low

            def unpack(group, carry):
                for plane in range(4):
                    rows = pl.ds(pl.multiple_of((group * 4 + plane) * SUB, SUB), SUB)
                    measured[j, 0, rows, :] = got[after + group, plane, :, :LANES]
                    measured[j, 1, rows, :] = got[after + group, plane, :, LANES:]
                return carry

            lax.fori_loop(0, INT_GROUPS, unpack, 0)

        for plane in range(2):
            parts = [twice[2 * plane + part, pl.ds(WIN - row, WIN), :] for part in range(2)]
            beam[m, plane] = pltpu.roll(jnp.concatenate(parts, axis=1), shift, 1)

    def arrive(j):
        columns, _, _ = near_columns(table[FIELDS * j + 2])
        pltpu.make_async_copy(field.at[:, :, columns], held.at[j], held_sem.at[j]).wait()

        @pl.when(is_a)
        def _():
            for copy in intensity_copies(j):
                copy.wait()

    def store_rows(m, e, o):
        work[m, 0, :HALF], work[m, 1, :HALF] = e[:HALF], e[HALF:]
        work[m, 0, HALF:], work[m, 1, HALF:] = o[:HALF], o[HALF:]

    def middle(pointwise, members, slots=None):
        for half in range(2):
            rows = pl.ds(half * HALF, HALF)
            for m in range(members):
                re, im = lanes_forward(work[m, 0, rows, :], work[m, 1, rows, :], forms)
                re, im = pointwise(m, half, rows, re, im, slots)
                re, im = lanes_inverse(re, im, forms)
                work[m, 0, rows, :], work[m, 1, rows, :] = re, im

    def rows_back(m):
        u, v = rows_inverse(work[m, 0], work[m, 1], forms)
        return (
            jnp.concatenate([u[:HALF] + v[:HALF], u[:HALF] - v[:HALF]], axis=0),
            jnp.concatenate([u[HALF:] + v[HALF:], u[HALF:] - v[HALF:]], axis=0),
        )

    def propagate(m, half, rows, re, im, slots):
        return cmul(kernel[0, rows, :], kernel[1, rows, :], re, im)

    def propagate_back(m, half, rows, re, im, slots):
        return cmul_conj(kernel[0, rows, :], kernel[1, rows, :], re, im)

    def residual(m, half, rows, re, im, slots):
        every = pl.ds(half, HALF, stride=2)
        at = slots[m]
        rows_of = jnp.concatenate([measured[at, 0, every, :], measured[at, 1, every, :]], axis=1)
        high, low = split(rows_of)
        wanted = jnp.dot(high, shuffle[...], preferred_element_type=f32)
        wanted += jnp.dot(low, shuffle[...], preferred_element_type=f32)
        scale = re * re + im * im - wanted
        return scale * re, scale * im

    def tile_copy(m, j):
        return pltpu.make_async_copy(tile.at[m], tiles.at[j], tile_sem.at[m])

    def write(m, j):
        _, row, _, _, back = slot_of(table, j)
        low = row // SUB

        def send(out, offset):
            def body(group, carry):
                rows = pl.ds(pl.multiple_of(group * SUB, SUB), SUB)
                for plane in range(4):
                    out[offset + group, plane] = tile[m, plane, rows, :]
                return carry

            return body

        tile_copy(m, j).start()

        offset = jnp.where(is_a, back, back - low)
        lower = jnp.where(is_a, 0, low)
        upper = jnp.where(is_a, (row + SUB - 1) // SUB, GROUPS)
        if between:

            @pl.when(is_narrow)
            def _():
                lax.fori_loop(lower, upper, send(back_narrow, offset), 0)

            @pl.when(jnp.logical_not(is_narrow))
            def _():
                lax.fori_loop(lower, upper, send(back_wide, offset), 0)

        else:
            lax.fori_loop(lower, upper, send(back_wide, offset), 0)

    def run(p, members):
        full = 2 * p + members <= found
        last = jnp.where(full, 2 * p + members - 1, 2 * p)
        slots = [chosen[2 * p], chosen[last]][:members]

        @pl.when(p > 0)
        def _():
            tile_copy(0, 0).wait()
            tile_copy(1, 0).wait()

        arrive(slots[0])
        if members == 2:

            @pl.when(full)
            def _():
                arrive(slots[1])

        for m in range(members):
            load(m, slots[m])
        for m in range(members):
            re, im = cmul(beam[m, 0], beam[m, 1], tile[m, 0], tile[m, 1])
            store_rows(m, *rows_forward(re, im, forms))
        middle(propagate, members)
        for m in range(members):
            re, im = rows_back(m)
            entered[m, 0], entered[m, 1] = re, im
            re, im = cmul(re, im, tile[m, 2], tile[m, 3])
            store_rows(m, *rows_forward(re, im, forms))
        middle(residual, members, slots)
        for m in range(members):
            br, bi = rows_back(m)
            re, im = cmul_conj(tile[m, 2], tile[m, 3], br, bi)
            tile[m, 2], tile[m, 3] = cmul_conj(entered[m, 0], entered[m, 1], br, bi)
            store_rows(m, *rows_forward(re, im, forms))
        middle(propagate_back, members)
        for m in range(members):
            br, bi = rows_back(m)
            tile[m, 0], tile[m, 1] = cmul_conj(beam[m, 0], beam[m, 1], br, bi)
        write(0, slots[0])
        if members == 2:

            @pl.when(full)
            def _():
                write(1, slots[1])

    def pair(p, carry):
        run(p, 2)
        return carry

    alone = jnp.bitwise_and(found, 1) == 1
    if between:
        lax.fori_loop(0, found // 2, pair, 0)

        @pl.when(alone)
        def _():
            run(found // 2, 1)

    else:
        lax.fori_loop(0, (found + 1) // 2, pair, 0)

    @pl.when(found > 0)
    def _():
        tile_copy(0, 0).wait()

    @pl.when(jnp.logical_and(found > 0, jnp.logical_not(alone)))
    def _():
        tile_copy(1, 0).wait()


def add_back(is_a, table, got, total, planes):
    theirs = jnp.where(is_a, AT_B, AT_A)
    for j in range(CAP):
        state, row, col, _, back = slot_of(table, j)

        @pl.when(state == theirs)
        def _():
            starts, shift = lane_blocks(col)
            low = row // SUB
            base = jnp.where(is_a, back - low, back)
            sublane = lax.broadcasted_iota(jnp.int32, (SUB, LANES), 0)

            def body(group, carry):
                below = (group * SUB + sublane < row).astype(jnp.int32)
                own = below == jnp.where(is_a, 0, 1)
                for plane in planes:
                    lf = jnp.where(own, got[base + group, plane, :, :LANES], 0.0)
                    rt = jnp.where(own, got[base + group, plane, :, LANES:], 0.0)
                    add_group(total, plane, group, starts, shift, lf, rt)
                return carry

            lax.fori_loop(jnp.where(is_a, low, 0), jnp.where(is_a, GROUPS, (row + SUB - 1) // SUB), body, 0)


def sum_kernel(
    flags, table_in, table_out, in_back, tiles_in, tiles_out, grad, total, got, tile, got_sem, tile_sem, total_sem
):
    pltpu.make_async_copy(in_back, got, got_sem).start()
    sublane = lax.broadcasted_iota(jnp.int32, (SUB, LANES), 0)
    kinds = ((flags[0] == 0, table_in, tiles_in), (flags[0] == 1, table_out, tiles_out))
    for k, (is_a, table, tiles) in enumerate(kinds):
        mine = jnp.where(is_a, AT_A, AT_B)
        for j in range(CAP):

            @pl.when(table[FIELDS * j] == mine)
            def _():
                pltpu.make_async_copy(tiles.at[j], tile.at[k * CAP + j], tile_sem.at[k * CAP + j]).start()

    @pl.when(flags[2] == 0)
    def _():
        total[...] = jnp.zeros_like(total)

    @pl.when(flags[2] > 0)
    def _():
        copy = pltpu.make_async_copy(grad, total, total_sem)
        copy.start()
        copy.wait()

    pltpu.make_async_copy(in_back, got, got_sem).wait()
    add_back(flags[0] == 0, table_in, got, total, range(4))
    for k, (is_a, table, tiles) in enumerate(kinds):
        mine = jnp.where(is_a, AT_A, AT_B)
        for j in range(CAP):
            state, row, col, _, _ = slot_of(table, j)

            @pl.when(state == mine)
            def _():
                at = k * CAP + j
                pltpu.make_async_copy(tiles.at[j], tile.at[at], tile_sem.at[at]).wait()
                starts, shift = lane_blocks(col)
                low = row // SUB

                def body(group, carry):
                    below = (group * SUB + sublane < row).astype(jnp.int32)
                    own = below == jnp.where(is_a, 0, 1)
                    rows = pl.ds(pl.multiple_of(group * SUB, SUB), SUB)
                    for plane in range(4):
                        lf = jnp.where(own, tile[at, plane, rows, :LANES], 0.0)
                        rt = jnp.where(own, tile[at, plane, rows, LANES:], 0.0)
                        add_group(total, plane, group, starts, shift, lf, rt)
                    return carry

                lax.fori_loop(
                    jnp.where(is_a, low, 0), jnp.where(is_a, GROUPS, (row + SUB - 1) // SUB), body, 0
                )


def finish_kernel(flags, table, total_in, wide, narrow, grad, total, got, got_sem, out_sem):
    is_narrow = flags[1] == 1
    fetch_pieces(is_narrow, wide, narrow, got, got_sem)
    await_pieces(is_narrow, wide, narrow, got, got_sem)
    for plane in range(4):
        total[plane] = total_in[plane]
        add_back(flags[0] == 1, table, got, total, (plane,))
        pltpu.make_async_copy(total.at[plane], grad.at[plane], out_sem.at[plane]).start()
    for plane in range(4):
        pltpu.make_async_copy(total.at[plane], grad.at[plane], out_sem.at[plane]).wait()


def spec(space):
    return pl.BlockSpec(memory_space=space)


def vmem(mib):
    return pltpu.CompilerParams(vmem_limit_bytes=mib << 20)


def packed(groups):
    return jax.ShapeDtypeStruct((groups, 4, SUB, WIN), f32)


def run_slots(flags, table, field, intensity, probe, kernel, tables, *pieces):
    between = len(pieces) == 2
    backs = (CAP_WIDE, CAP_NARROW) if between else (CAP_INNER,)
    return pl.pallas_call(
        functools.partial(slots_kernel, between),
        out_shape=tuple(packed(n) for n in backs) + (HB((CAP, 4, WIN, WIN), f32),),
        in_specs=[spec(SM)] * 2 + [spec(HB)] * 2 + [spec(VM)] * 4 + [spec(pl.ANY)] * len(pieces),
        out_specs=(spec(VM),) * len(backs) + (spec(HB),),
        scratch_shapes=[
            pltpu.VMEM((CAP, 4, WIN, WIDE), f32),
            pltpu.VMEM((backs[0], 4, SUB, WIN), f32),
            pltpu.VMEM((2, 4, WIN, WIN), f32),
            pltpu.VMEM((CAP, 2, WIN, LANES), f32),
            pltpu.VMEM((4, 2 * WIN, LANES), f32),
            pltpu.VMEM((2, 2, WIN, WIN), f32),
            pltpu.VMEM((2, 2, WIN, WIN), f32),
            pltpu.VMEM((2, 2, WIN, WIN), f32),
            pltpu.SMEM((CAP,), jnp.int32),
            pltpu.SemaphoreType.DMA((CAP,)),
            pltpu.SemaphoreType.DMA((CAP, 2)),
            pltpu.SemaphoreType.DMA,
            pltpu.SemaphoreType.DMA((2,)),
        ],
        cost_estimate=CHEAP,
        compiler_params=vmem(24),
    )(flags, table, field, intensity, probe, kernel, *tables, *pieces)


def both_ways(pairs):
    return pairs + [(b, a) for a, b in pairs]


def one_round(turn, grad, field, maps, intensity, probe_wave, prop_phase, info):
    count = lax.axis_size("row")
    within = both_ways([(i, i + 1) for i in range(0, count - 1, 2)])
    wide_pairs = both_ways([(i, i + 1) for i in range(1, count - 1, 4)])
    narrow_pairs = both_ways([(i, i + 1) for i in range(3, count - 1, 4)])
    move = lambda x, pairs: lax.ppermute(x, "row", pairs)
    place = lax.axis_index("row")
    odd = jnp.bitwise_and(place, 1)
    is_narrow = (jnp.bitwise_and(place + 1, 2) == 0).astype(jnp.int32)
    own = lax.axis_index("groups") * count + place
    flags = jnp.stack([odd, is_narrow, turn, own, jnp.where(place == 0, -1, own - 1)])
    prop_phase, _ = lax.optimization_barrier((prop_phase, turn))

    table = jax.ShapeDtypeStruct((CAP * FIELDS,), jnp.int32)
    inner, wide, narrow, table_in, table_out, again = pl.pallas_call(
        pack_kernel,
        out_shape=(
            packed(CAP_INNER),
            packed(CAP_WIDE),
            packed(CAP_NARROW),
            table,
            table,
            jax.ShapeDtypeStruct((1,), jnp.int32),
        ),
        in_specs=[spec(SM)] * 2 + [spec(HB)] * 2,
        out_specs=(spec(VM),) * 3 + (spec(SM),) * 3,
        scratch_shapes=[
            pltpu.VMEM((2 * CAP, 4, WIN, WIDE), f32),
            pltpu.SemaphoreType.DMA((2 * CAP,)),
            pltpu.SemaphoreType.DMA((CAP,)),
        ],
        cost_estimate=CHEAP,
        compiler_params=vmem(24),
    )(flags, info, field, maps)
    wide = move(wide, wide_pairs)
    narrow = move(narrow, narrow_pairs)
    inner = move(inner, within)

    forms, shuffle = (jnp.asarray(t) for t in make_tables())
    kernel = pl.pallas_call(
        prepare_kernel,
        out_shape=jax.ShapeDtypeStruct((2, WIN, WIN), f32),
        in_specs=[spec(VM)] * 2,
        out_specs=spec(VM),
        scratch_shapes=[pltpu.VMEM((2, WIN, LANES), f32)],
        cost_estimate=CHEAP,
        compiler_params=vmem(8),
    )(jnp.stack([jnp.cos(prop_phase), jnp.sin(prop_phase)]), shuffle)

    args = (field, intensity, probe_wave, kernel, (forms, shuffle))
    in_back, tiles_in = run_slots(flags, table_in, *args, inner)
    in_back = move(in_back, within)
    back_wide, back_narrow, tiles_out = run_slots(flags, table_out, *args, wide, narrow)
    tiles_in = pltpu.with_memory_space_constraint(tiles_in, HB)
    tiles_out = pltpu.with_memory_space_constraint(tiles_out, HB)
    back_wide = move(back_wide, wide_pairs)
    back_narrow = move(back_narrow, narrow_pairs)
    total = pl.pallas_call(
        sum_kernel,
        out_shape=jax.ShapeDtypeStruct(field.shape, f32),
        in_specs=[spec(SM)] * 3 + [spec(pl.ANY)] * 3 + [spec(HB)],
        out_specs=spec(VM),
        scratch_shapes=[
            pltpu.VMEM((CAP_INNER, 4, SUB, WIN), f32),
            pltpu.VMEM((2 * CAP, 4, WIN, WIN), f32),
            pltpu.SemaphoreType.DMA,
            pltpu.SemaphoreType.DMA((2 * CAP,)),
            pltpu.SemaphoreType.DMA,
        ],
        cost_estimate=CHEAP,
        compiler_params=vmem(20),
    )(flags, table_in, table_out, in_back, tiles_in, tiles_out, grad)
    grad = pl.pallas_call(
        finish_kernel,
        out_shape=jax.ShapeDtypeStruct(field.shape, f32),
        in_specs=[spec(SM)] * 2 + [spec(VM)] + [spec(pl.ANY)] * 2,
        out_specs=spec(HB),
        scratch_shapes=[
            pltpu.VMEM(field.shape, f32),
            pltpu.VMEM((CAP_WIDE, 4, SUB, WIN), f32),
            pltpu.SemaphoreType.DMA,
            pltpu.SemaphoreType.DMA((4,)),
        ],
        cost_estimate=CHEAP,
        compiler_params=vmem(16),
    )(flags, table_out, total, back_wide, back_narrow)
    return grad, again[0]


def shards(obj_field, probe_wave, prop_phase, win_offsets, live_counts, intensity):
    field = pltpu.with_memory_space_constraint(obj_field.reshape((4,) + obj_field.shape[2:]), HB)
    maps = pltpu.with_memory_space_constraint(intensity.reshape(CAP, INT_GROUPS, 4, SUB, WIN), HB)
    intensity = pltpu.with_memory_space_constraint(intensity, HB)
    axes = ("groups", "row")
    count = lax.axis_size("groups") * lax.axis_size("row")
    own = jnp.concatenate([win_offsets.reshape(-1), live_counts, jnp.zeros((INFO - PLACE - 1,), jnp.int32)])
    info = lax.all_to_all(jnp.broadcast_to(own, (count, 1, INFO)), axes, 0, 0, tiled=True).reshape(count, INFO)

    def body(state):
        turn, _, grad = state
        grad, again = one_round(turn, grad, field, maps, intensity, probe_wave, prop_phase, info)
        return turn + 1, again, grad

    empty = pl.pallas_call(
        lambda out: None,
        out_shape=jax.ShapeDtypeStruct(field.shape, f32),
        out_specs=spec(HB),
    )()
    _, _, grad = lax.while_loop(lambda state: state[1] > 0, body, (jnp.int32(0), jnp.int32(1), empty))
    return grad.reshape(obj_field.shape)


def solution(mesh):
    in_specs = (
        P(None, None, ("groups", "row"), None),
        P("groups", None, None),
        P(),
        P(("groups", "row"), None),
        P(("groups", "row")),
        P(("groups", "row"), None, None),
    )
    out_specs = P(None, None, ("groups", "row"), None)
    return jax.shard_map(shards, mesh=mesh, in_specs=in_specs, out_specs=out_specs, check_vma=False)
```
